32 devices in a mesh: sky: 4 (over y, x), visit: 4 (over z), patch: 2 (over core).
Axes of the slice: x: 2, y: 2, z: 4, core: 2. Of those that a mesh axis runs over, the one named last changes fastest.
Arguments:
- template_store: float32 [4, 128, 2048], P('visit', 'patch', 'sky'), may hold values from -6 to 6
- science: float32 [4, 128, 2048], P('visit', 'patch', 'sky'), may hold values from -40 to 40
- owner_visit: int32 [4, 2], P('sky', 'patch'), may hold values from 0 to 3, as said below
- stamp_offset: int32 [2, 4, 2, 32], P(None, 'visit', 'patch', 'sky'), may hold values from 0 to 32
Outputs:
- difference: float32 [4, 128, 2048], P('visit', 'patch', 'sky')
The draws below stay inside these ranges and needn't reach their ends.
Inputs may be any that keep to these rules, and one draw needn't show every extreme that they name: owner_visit[s, p] = (owner_visit[s, 0] + p) mod 4; only that visit's slot of template_store holds the current coadd of sky tile s, patch p.
All inputs are finite; a program needn't handle non-finite values.
Results may differ from the reference program's by a relative error of at most 0.0003.
Values sent between devices are 32-bit elements; how exact they have to be, the bound alone decides.
A program may use at most 128 MiB of HBM per device.

```python
import math
import jax
import jax.numpy as jnp
from jax import lax

PR = 64
PC = 512
HALF = 15
NBASIS = 25
CELL = 64
STAMP = 32
TILES = 4
VISITS = 4
PATCHES = 2
NR = 128
NC = 2048
RC = 1
CC = 8


blur_spread = 2.0


blur_reach = 6


def owner_table(key):
    base_visit = jax.random.randint(jax.random.fold_in(key, 11), (TILES, 1), 0, VISITS)
    return (base_visit + jnp.arange(PATCHES)[None, :]) % VISITS


def gauss_profile(spread_px, tap_reach):
    offsets = jnp.arange(2 * tap_reach + 1).astype(jnp.float32) - tap_reach
    ratio = offsets / spread_px
    profile = jnp.exp(-0.5 * ratio * ratio)
    return profile / jnp.sum(profile, axis=-1, keepdims=True)


def blur_rows(values, profile, tap_reach):
    length = values.shape[1] - 2 * tap_reach
    summed = profile[:, 0, None, None] * values[:, 0:length, :]
    for tap_at in range(1, 2 * tap_reach + 1):
        summed = summed + profile[:, tap_at, None, None] * values[:, tap_at:tap_at + length, :]
    return summed


def blur_cols(values, profile, tap_reach):
    length = values.shape[2] - 2 * tap_reach
    summed = profile[:, 0, None, None] * values[:, :, 0:length]
    for tap_at in range(1, 2 * tap_reach + 1):
        summed = summed + profile[:, tap_at, None, None] * values[:, :, tap_at:tap_at + length]
    return summed


def coadd_slots(key):
    draw_key = jax.random.fold_in(key, 23)
    grid_shape = (VISITS, NR + 2 * blur_reach, NC + 2 * blur_reach)
    speckle = jax.random.normal(draw_key, grid_shape, jnp.float32)
    profile = gauss_profile(blur_spread, blur_reach)[None]
    blurred = blur_cols(blur_rows(speckle, profile, blur_reach), profile, blur_reach)
    blurred = blurred / jnp.sum(profile * profile)
    return jnp.clip(blurred, -6.0, 6.0)


def draw_template_store(key, part):
    return coadd_slots(key)


def draw_owner_visit(key, part):
    return owner_table(key).astype(jnp.int32)


def draw_science(key, part):
    slot_values = coadd_slots(key)
    owners = owner_table(key).astype(jnp.int32)
    pixel_owner = jnp.repeat(jnp.repeat(owners.T, PR, axis=0), PC, axis=1)
    current = jnp.take_along_axis(slot_values, pixel_owner[None], axis=0)[0]
    padded = jnp.pad(current, HALF)[None]
    visit_spread = (4.0 + 0.3 * jnp.arange(VISITS).astype(jnp.float32))[:, None]
    profile = gauss_profile(visit_spread, HALF)
    matched_sky = blur_cols(blur_rows(padded, profile, HALF), profile, HALF)
    column_ramp = 1.0 + 2.0 * jnp.arange(NC).astype(jnp.float32) / max(NC - 1, 1)
    visit_gain = 1.5 + 0.75 * jnp.arange(VISITS).astype(jnp.float32)
    noise_field = 0.5 * jax.random.normal(jax.random.fold_in(key, 37), (VISITS, NR, NC), jnp.float32)
    values = visit_gain[:, None, None] * column_ramp[None, None, :] * matched_sky + noise_field
    return jnp.clip(values, -40.0, 40.0)


def set_ends(values, key, smallest, top_value):
    longest = values.shape.index(max(values.shape))
    spots = []
    for shift in (0, 1):
        where = [jax.random.randint(jax.random.fold_in(key, axis), (), 0, length) for axis, length in enumerate(values.shape)]
        where[longest] = (where[longest] + shift) % values.shape[longest]
        spots.append(tuple(where))
    return values.at[spots[0]].set(smallest).at[spots[1]].set(top_value)


def setup_inputs(seed: int = 0) -> dict:
    arg_keys = jax.random.split(jax.random.key(seed), 5)
    template_store = draw_template_store(jax.random.fold_in(arg_keys[4], 71), 0)
    science = draw_science(jax.random.fold_in(arg_keys[4], 71), 0)
    owner_visit = draw_owner_visit(jax.random.fold_in(arg_keys[4], 71), 0)
    stamp_offset = set_ends(jax.random.randint(arg_keys[3], (2, VISITS, RC * PATCHES, CC * TILES), 0, CELL - STAMP + 1), jax.random.fold_in(arg_keys[3], 1), 0, CELL - STAMP).astype(jnp.int32)
    return {"template_store": template_store, "science": science, "owner_visit": owner_visit, "stamp_offset": stamp_offset}


kernel_sigma = 5.0
highest = lax.Precision.HIGHEST

def filter_bank():
    tap_offset = jnp.arange(2 * HALF + 1).astype(jnp.float32) - HALF
    scaled = tap_offset / kernel_sigma
    envelope = jnp.exp(-0.5 * scaled * scaled)
    square = scaled * scaled
    polynoms = [jnp.ones_like(scaled), 2.0 * scaled, 4.0 * square - 2.0, 8.0 * square * scaled - 12.0 * scaled, 16.0 * square * square - 48.0 * square + 12.0]
    shaped = jnp.stack(polynoms) * envelope[None, :]
    filters = shaped / jnp.sqrt(lax.optimization_barrier(jnp.sum(shaped * shaped, axis=1, keepdims=True)))
    return (filters, lax.optimization_barrier(jnp.sum(filters, axis=1)))

def solve_small(matrix, targets):
    count = matrix.shape[0]
    order = jnp.arange(count)
    remain = matrix
    factor_cols = []
    for column_at in range(count):
        pivot = jnp.sqrt(remain[column_at, column_at])
        column = jnp.where((order >= column_at)[:, None], remain[:, column_at] / pivot[None, :], 0.0)
        factor_cols.append(column)
        remain = remain - column[:, None, :] * column[None, :, :]
    factor = jnp.stack(factor_cols, axis=1)
    answer = targets
    for column_at in range(count):
        solved = answer[column_at] / factor[column_at, column_at][None, :]
        update = factor[:, column_at][:, None, :] * solved[None]
        answer = jnp.where((order > column_at)[:, None, None], answer - update, answer)
        answer = jnp.where((order == column_at)[:, None, None], solved[None], answer)
    for column_at in reversed(range(count)):
        solved = answer[column_at] / factor[column_at, column_at][None, :]
        update = factor[column_at, :][:, None, :] * solved[None]
        answer = jnp.where((order < column_at)[:, None, None], answer - update, answer)
        answer = jnp.where((order == column_at)[:, None, None], solved[None], answer)
    return answer

def reference(template_store, science, owner_visit, stamp_offset):
    filters, tap_sums = filter_bank()
    flux_vector = (tap_sums[:, None] * tap_sums[None, :]).reshape(-1)
    pixel_owner = jnp.repeat(jnp.repeat(owner_visit.T, PR, axis=0), PC, axis=1)
    coadd_image = jnp.zeros((NR, NC), dtype=template_store.dtype)
    for visit_at in range(VISITS):
        coadd_image = coadd_image + jnp.where(pixel_owner == visit_at, template_store[visit_at], 0.0)
    padded = jnp.pad(coadd_image, HALF)
    local = jnp.arange(CELL).astype(jnp.int32)

    def one_patch(patch_id):
        visit_at = patch_id // (PATCHES * TILES)
        patch_at = patch_id // TILES % PATCHES
        tile_at = patch_id % TILES
        row_first = (patch_at * PR).astype(jnp.int32)
        col_first = (tile_at * PC).astype(jnp.int32)
        zero_at = jnp.zeros((), jnp.int32)
        extended = lax.dynamic_slice(padded, (row_first, col_first), (PR + 2 * HALF, PC + 2 * HALF))
        image = lax.dynamic_slice(science, (visit_at.astype(jnp.int32), row_first, col_first), (1, PR, PC))[0]
        offsets = lax.dynamic_slice(stamp_offset, (zero_at, visit_at.astype(jnp.int32), (patch_at * RC).astype(jnp.int32), (tile_at * CC).astype(jnp.int32)), (2, 1, RC, CC))[:, 0]
        columns_done = filters[:, 0, None, None] * extended[None, :, 0:PC]
        for tap_at in range(1, 2 * HALF + 1):
            columns_done = columns_done + filters[:, tap_at, None, None] * extended[None, :, tap_at:tap_at + PC]
        basis_full = filters[None, :, 0, None, None] * columns_done[:, None, 0:PR, :]
        for tap_at in range(1, 2 * HALF + 1):
            basis_full = basis_full + filters[None, :, tap_at, None, None] * columns_done[:, None, tap_at:tap_at + PR, :]
        basis_cells = basis_full.reshape(NBASIS, RC, CELL, CC, CELL)
        row_off = offsets[0]
        col_off = offsets[1]
        in_y = (local[None, :, None] >= row_off[:, None, :]) & (local[None, :, None] < row_off[:, None, :] + STAMP)
        in_x = (local[None, :, None] >= col_off[:, None, :]) & (local[None, :, None] < col_off[:, None, :] + STAMP)
        in_stamp = (in_y[:, :, :, None] & jnp.transpose(in_x, (0, 2, 1))[:, None, :, :]).astype(image.dtype)
        masked = basis_cells * in_stamp[None]
        gram_matrix = jnp.einsum('krycx,lrycx->klrc', masked, basis_cells, precision=highest).reshape(NBASIS, NBASIS, RC * CC)
        right_side = jnp.einsum('krycx,rycx->krc', masked, image.reshape(RC, CELL, CC, CELL), precision=highest).reshape(NBASIS, RC * CC)
        targets = jnp.stack([right_side, jnp.broadcast_to(flux_vector[:, None], right_side.shape)], axis=1)
        answer = solve_small(gram_matrix, targets)
        weights = answer[:, 0]
        unit_sol = answer[:, 1]
        fitted = jnp.einsum('krycx,krc->rycx', basis_cells, weights.reshape(NBASIS, RC, CC), precision=highest)
        unit_match = jnp.einsum('krycx,krc->rycx', basis_cells, unit_sol.reshape(NBASIS, RC, CC), precision=highest)
        flux_sums = jnp.einsum('k,kc->c', flux_vector, weights, precision=highest)
        curvature = jnp.einsum('k,kc->c', flux_vector, unit_sol, precision=highest)
        return (fitted, unit_match, flux_sums, curvature)
    total_patches = VISITS * PATCHES * TILES
    group_size = math.gcd(8, total_patches)
    patch_ids = jnp.arange(total_patches).astype(jnp.int32).reshape(-1, group_size)
    fitted, unit_match, flux_sums, curvature = lax.map(jax.vmap(one_patch), patch_ids)
    fitted = fitted.reshape(total_patches, RC, CELL, CC, CELL)
    unit_match = unit_match.reshape(total_patches, RC, CELL, CC, CELL)
    flux_sums = flux_sums.reshape(total_patches, RC * CC)
    curvature = curvature.reshape(total_patches, RC * CC)
    mean_flux = lax.optimization_barrier(jnp.mean(flux_sums.reshape(VISITS, -1), axis=1))
    mean_each = jnp.repeat(mean_flux, PATCHES * TILES)[:, None]
    correction = ((mean_each - flux_sums) / curvature).reshape(total_patches, RC, 1, CC, 1)
    matched = fitted + correction * unit_match
    matched = matched.reshape(VISITS, PATCHES, TILES, PR, PC)
    matched = jnp.transpose(matched, (0, 1, 3, 2, 4)).reshape(VISITS, NR, NC)
    return science - matched
```

```python
import numpy as np
import jax
import jax.numpy as jnp
from jax import lax
from jax.experimental import pallas as pl
from jax.experimental.pallas import tpu as pltpu
from jax.sharding import PartitionSpec as P

HALF = 15
TAPS = 2 * HALF + 1
ORDERS = 5
NBASIS = 25
CELL = 64
STAMP = 32
ROWS = 64
PAD = 16
LANES = 128
PIECES = 2
SIGMA = 5.0
MESH = pl.DeviceIdType.MESH
F32 = jnp.float32
BF16 = jnp.bfloat16


def filter_bank():
    x = (np.arange(TAPS) - HALF) / SIGMA
    env = np.exp(-0.5 * x * x)
    poly = [
        np.ones_like(x),
        2.0 * x,
        4.0 * x**2 - 2.0,
        8.0 * x**3 - 12.0 * x,
        16.0 * x**4 - 48.0 * x**2 + 12.0,
    ]
    shaped = np.stack(poly) * env[None]
    return shaped / np.sqrt(np.sum(shaped * shaped, axis=1, keepdims=True))


def taps_at(filters, index):
    inside = (index >= 0) & (index < TAPS)
    return np.where(inside[None], filters[:, np.clip(index, 0, TAPS - 1)], 0.0)


def halves(values):
    values = np.asarray(values, np.float32)
    high = values.astype(BF16)
    low = (values - high.astype(np.float32)).astype(BF16)
    return [jnp.asarray(np.stack([high, low]))]


def constants(filters, cells):
    width = cells * CELL
    stamp_rows = taps_at(filters, np.arange(CELL)[None, :] - np.arange(STAMP)[:, None])
    stamp_rows = stamp_rows.reshape(ORDERS * STAMP, CELL)
    one = taps_at(filters, np.arange(CELL)[:, None] - np.arange(STAMP)[None, :])
    stamp_cols = np.zeros((4, CELL, ORDERS, 4, STAMP))
    for g in range(4):
        stamp_cols[g, :, :, g, :] = np.transpose(one, (1, 0, 2))
    stamp_cols = stamp_cols.reshape(4 * CELL, ORDERS * LANES)
    full_cols = taps_at(filters, np.arange(2 * LANES)[:, None] - np.arange(LANES)[None, :] - 1)
    full_cols = np.transpose(full_cols, (1, 0, 2)).reshape(2 * LANES, ORDERS * LANES)
    full_rows = taps_at(filters, np.arange(ROWS + 2 * PAD)[None, :] - np.arange(ROWS)[:, None] - 1)
    full_rows = np.transpose(full_rows, (1, 0, 2)).reshape(ROWS, ORDERS * (ROWS + 2 * PAD))
    lane_cell = np.arange(cells * STAMP)[:, None] // STAMP == np.arange(LANES)[None, :]
    cell_lane = np.arange(LANES)[:, None] == np.arange(width)[None, :] // CELL
    return (
        halves(stamp_rows)
        + halves(stamp_cols)
        + halves(full_cols)
        + halves(full_rows)
        + [jnp.asarray(lane_cell, BF16), jnp.asarray(cell_lane, BF16)]
    )


def dot(a, b):
    return jnp.dot(a, b, preferred_element_type=F32)


def split2(x):
    high = x.astype(BF16)
    return high, (x - high.astype(F32)).astype(BF16)


def split3(x):
    high = x.astype(BF16)
    rest = x - high.astype(F32)
    mid = rest.astype(BF16)
    return high, mid, (rest - mid.astype(F32)).astype(BF16)


def dot3(a, b):
    return dot(a[0], b[0]) + (dot(a[0], b[1]) + dot(a[1], b[0]))


def pick_sum(x, selector):
    high, mid, low = split3(x)
    return dot(high, selector) + (dot(mid, selector) + dot(low, selector))


def eliminate(rows, flux):
    count = len(rows)
    starts = [8 * (k // 8) for k in range(count)]
    for j in range(count):
        first = 8 * (j // 8)
        for i in range(j):
            if starts[i] < first:
                rows[i] = rows[i][first - starts[i] :]
                starts[i] = first
        pivot_row = rows[j]
        scaled = pivot_row * (1.0 / pivot_row[j - first : j - first + 1])
        for i in range(count):
            if i < j:
                rows[i] = rows[i] - rows[i][j - first : j - first + 1] * scaled
            elif i > j:
                factor = pivot_row[i - first : i - first + 1]
                rows[i] = rows[i] - factor * scaled[starts[i] - first :]
        rows[j] = scaled
    weights = jnp.concatenate([row[1:2] for row in rows] + [jnp.zeros((7, LANES), F32)], axis=0)
    unit = jnp.concatenate([row[2:3] for row in rows] + [jnp.zeros((7, LANES), F32)], axis=0)
    return weights, unit


def fused_kernel(
    counts, flux, owner_hbm, offset_hbm, slot_hbm, image_hbm,
    srow_hbm, scol_hbm, fcol_hbm, frow_hbm, pick_hbm, put_hbm,
    out_ref,
    owner_ref, offset_ref, slot_ref, image_ref, srow, scol, fcol, frow, lane_cell, cell_lane,
    ext, landed, edge, edge_landed, shifted, stamps, pairs, combined_h, combined_l, sum_ref, sum_landed,
    local_sem, rs_send, rs_recv, ag_send, ag_recv, ha_send, ha_recv, ed_send, ed_recv, fx_send, fx_recv,
):
    sky_count, visits, patches = counts
    members = sky_count * patches
    sky = lax.axis_index("sky")
    visit = lax.axis_index("visit")
    patch = lax.axis_index("patch")
    me = sky * patches + patch
    width = image_ref.shape[1]
    cells = width // CELL
    full = width + 2 * LANES
    ext_rows = ROWS + 2 * PAD
    first_reducer = visits // 2 - 1
    half = width // 2
    piece = half // PIECES
    side = visit - first_reducer
    reduces = (side == 0) | (side == 1)
    steps = [(ds, dp) for dp in (-1, 0, 1) for ds in (-1, 0, 1)]
    ends = [(ds, dp) for ds, dp in steps if ds != 0]

    def exists(ds, dp):
        return (sky + ds >= 0) & (sky + ds < sky_count) & (patch + dp >= 0) & (patch + dp < patches)

    def there(ds, dp, v):
        return {
            "sky": jnp.clip(sky + ds, 0, sky_count - 1),
            "visit": v,
            "patch": jnp.clip(patch + dp, 0, patches - 1),
        }

    def member(d):
        other = lax.rem(me + d, members)
        return {"sky": other // patches, "patch": lax.rem(other, patches)}

    def columns_of(i, j):
        at = i * half + (j + i * (PIECES - 1 - 2 * j)) * piece
        return at if isinstance(at, int) else pl.multiple_of(at, LANES)

    moves = [
        (owner_hbm, owner_ref),
        (offset_hbm, offset_ref),
        (image_hbm.at[0], image_ref),
        (slot_hbm.at[0], slot_ref),
        (srow_hbm, srow),
        (scol_hbm, scol),
        (fcol_hbm, fcol),
        (frow_hbm, frow),
        (pick_hbm, lane_cell),
        (put_hbm, cell_lane),
    ]
    loads = [pltpu.make_async_copy(src, dst, local_sem.at[i]) for i, (src, dst) in enumerate(moves)]

    ext[0:PAD, :] = jnp.zeros((PAD, full), F32)
    ext[PAD + ROWS :, :] = jnp.zeros((PAD, full), F32)
    ext[PAD : PAD + ROWS, 0:LANES] = jnp.zeros((ROWS, LANES), F32)
    ext[PAD : PAD + ROWS, full - LANES :] = jnp.zeros((ROWS, LANES), F32)

    barrier = pltpu.get_barrier_semaphore()
    for d in range(1, members):
        pl.semaphore_signal(barrier, inc=1, device_id=member(d), device_id_type=MESH)
    for ds, dp in steps:

        @pl.when(exists(ds, dp))
        def _():
            for d in range(1, visits):
                to = lax.rem(visit + d, visits)
                other = to - first_reducer

                @pl.when(reduces | (other == 0) | (other == 1))
                def _():
                    pl.semaphore_signal(barrier, inc=1, device_id=there(ds, dp, to), device_id_type=MESH)

    for load in loads:
        load.start()
    around = sum(exists(ds, dp).astype(jnp.int32) for ds, dp in steps)
    pl.semaphore_wait(barrier, members - 1 + around * jnp.where(reduces, visits - 1, 2))

    def scatter(i, j):
        start = columns_of(i, j)
        return pltpu.make_async_remote_copy(
            src_ref=slot_hbm.at[0, :, pl.ds(start, piece)],
            dst_ref=landed.at[visit, :, pl.ds(start - i * half, piece)],
            send_sem=rs_send.at[i, j],
            recv_sem=rs_recv.at[visit, j],
            device_id={"visit": first_reducer + i},
            device_id_type=MESH,
        )

    for j in range(PIECES):
        for i in range(2):

            @pl.when(side != i)
            def _():
                scatter(i, j).start()

    for load in loads[:4]:
        load.wait()
    groups = cells // 4
    lane = lax.broadcasted_iota(jnp.int32, (STAMP, LANES), 1)
    for q in range(groups):
        merged = jnp.zeros((STAMP, LANES), F32)
        for inner in range(4):
            g = 4 * q + inner
            first = LANES * (g // 2)
            block = image_ref[:, first : first + LANES]
            block = pltpu.roll(block, lax.rem(ROWS - offset_ref[0, 0, 0, g], ROWS), 0)[0:STAMP]
            move = lax.rem(2 * LANES + STAMP * inner - CELL * (g % 2) - offset_ref[1, 0, 0, g], LANES)
            merged = jnp.where(lane // STAMP == inner, pltpu.roll(block, move, 1), merged)
        stamps[NBASIS, :, LANES * q : LANES * (q + 1)] = merged
    for spare in range(NBASIS + 1, 32):
        stamps[spare] = jnp.zeros((STAMP, cells * STAMP), F32)

    owner = owner_ref[0, 0]
    lane8 = lax.broadcasted_iota(jnp.int32, (8, LANES), 1) // PAD
    row_span = {-1: (PAD, PAD + ROWS), 1: (ROWS, 0)}

    def own_copy(j, i, to):
        spot = ext.at[pl.ds(PAD, ROWS), pl.ds(LANES + columns_of(i, j), piece)]
        return pltpu.make_async_remote_copy(
            src_ref=spot,
            dst_ref=spot,
            send_sem=ag_send.at[j, to],
            recv_sem=ag_recv.at[i, j],
            device_id={"visit": to},
            device_id_type=MESH,
        )

    def row_copy(j, i, dp, to, d):
        first, last = row_span[dp]
        at = LANES + columns_of(i, j)
        return pltpu.make_async_remote_copy(
            src_ref=ext.at[pl.ds(first, PAD), pl.ds(at, piece)],
            dst_ref=ext.at[pl.ds(last, PAD), pl.ds(at, piece)],
            send_sem=ha_send.at[j, (dp + 1) // 2, to],
            recv_sem=ha_recv.at[i, j, (dp + 1) // 2],
            device_id=there(0, d, to),
            device_id_type=MESH,
        )

    def edge_copy(way, to, d):
        ds, dp = ends[way]
        return pltpu.make_async_remote_copy(
            src_ref=edge,
            dst_ref=edge_landed.at[way],
            send_sem=ed_send.at[way, to],
            recv_sem=ed_recv.at[way],
            device_id=there(ds * d, dp * d, to),
            device_id_type=MESH,
        )

    @pl.when(reduces)
    def _():
        for j in range(PIECES):
            start = columns_of(side, j)
            spot = pl.ds(pl.multiple_of(start - side * half, LANES), piece)
            current = jnp.where(owner == visit, slot_ref[:, pl.ds(start, piece)], 0.0)
            for d in range(1, visits):
                source = lax.rem(visit + visits - d, visits)
                pltpu.make_async_remote_copy(
                    src_ref=landed.at[source, :, spot],
                    dst_ref=landed.at[source, :, spot],
                    send_sem=rs_send.at[0, j],
                    recv_sem=rs_recv.at[source, j],
                    device_id={"visit": source},
                    device_id_type=MESH,
                ).wait_recv()
                current = jnp.where(owner == source, landed[source, :, spot], current)
            ext[PAD : PAD + ROWS, pl.ds(LANES + start, piece)] = current
            if j == 0:
                merged = jnp.zeros((8, LANES), F32)
                for r in range(ROWS // 8):
                    left = pltpu.roll(current[8 * r : 8 * r + 8, 0:LANES], (PAD * r) % LANES, 1)
                    right = pltpu.roll(current[8 * r : 8 * r + 8, piece - LANES :], (PAD * (r + 1)) % LANES, 1)
                    merged = jnp.where(lane8 == r, jnp.where(side == 0, left, right), merged)
                edge[...] = merged
            for to in range(visits):

                @pl.when(visit != to)
                def _():
                    own_copy(j, side, to).start()

                if j == 0:
                    for way, (ds, dp) in enumerate(ends):

                        @pl.when(exists(ds, dp) & (side == (ds + 1) // 2))
                        def _():
                            edge_copy(way, to, 1).start()

                for dp in (-1, 1):

                    @pl.when(exists(0, dp))
                    def _():
                        row_copy(j, side, dp, to, dp).start()

    for j in range(PIECES):
        for i in range(2):

            @pl.when(side != i)
            def _():
                own_copy(j, i, first_reducer + i).wait_recv()

            for dp in (-1, 1):

                @pl.when(exists(0, -dp))
                def _():
                    row_copy(j, i, dp, first_reducer + i, -dp).wait_recv()

    for way, (ds, dp) in enumerate(ends):

        @pl.when(exists(-ds, -dp))
        def _():
            edge_copy(way, first_reducer + (ds + 1) // 2, -1).wait_recv()
            first, base = (full - LANES, 0) if ds < 0 else (0, LANES - PAD)
            spans = {0: (0, ROWS // 8, PAD), -1: (0, 2, PAD + ROWS), 1: (ROWS // 8 - 2, 2, 0)}
            group, number, row = spans[dp]
            packed = edge_landed[way]
            for r in range(number):
                moved = pltpu.roll(packed, (base - PAD * (group + r)) % LANES, 1)
                ext[row + 8 * r : row + 8 * r + 8, first : first + LANES] = moved

    for load in loads[4:]:
        load.wait()

    shifted[0:ext_rows, :] = pltpu.roll(ext[...], full - (LANES - PAD), 1)
    shifted[ext_rows:, :] = jnp.zeros((8, full), F32)

    lane = lax.broadcasted_iota(jnp.int32, (CELL, LANES), 1)
    windows = []
    for h in range(cells // 2):
        parts = []
        for odd in range(2):
            g = 2 * h + odd
            block = shifted[:, LANES * h : LANES * h + 2 * LANES]
            block = pltpu.roll(block, ext_rows + 7 - offset_ref[0, 0, 0, g], 0)[0:CELL]
            move = 2 * LANES - offset_ref[1, 0, 0, g] - 1
            parts.append(pltpu.roll(block, move, 1)[:, 0:LANES])
        windows.append(jnp.where(lane < CELL, parts[0], parts[1]))
    window = jnp.concatenate(windows, axis=1)
    rows_done = dot3((srow[0], srow[1]), split2(window))
    stacked = jnp.concatenate([rows_done[:, 4 * CELL * q : 4 * CELL * (q + 1)] for q in range(groups)], axis=0)
    basis = dot3(split2(stacked), (scol[0], scol[1]))
    for q in range(groups):
        for b in range(ORDERS):
            first = (q * ORDERS + b) * STAMP
            for a in range(ORDERS):
                stamps[ORDERS * a + b, :, LANES * q : LANES * (q + 1)] = basis[first : first + STAMP, LANES * a : LANES * (a + 1)]
    spots = []
    at = 0
    for k in range(NBASIS):
        low = 8 * (k // 8)
        mine = stamps[k]
        for tile in range(low, 32, 8):
            pairs[at + tile - low : at + tile - low + 8, :] = jnp.sum(stamps[tile : tile + 8] * mine[None], axis=1)
        spots.append((at, 32 - low))
        at += 32 - low
    sums = pick_sum(pairs[...], lane_cell[...])
    rows = []
    for k, (at, length) in enumerate(spots):
        row = sums[at : at + length]
        place = lax.broadcasted_iota(jnp.int32, row.shape, 0) + (32 - length)
        row = jnp.where(place == NBASIS + 1, float(flux[k]), row)
        rows.append(row)
    padding = lax.broadcasted_iota(jnp.int32, (1, LANES), 1) >= cells
    diag = []
    for k, (at, length) in enumerate(spots):
        place = lax.broadcasted_iota(jnp.int32, rows[k].shape, 0) + (32 - length)
        diag.append(jnp.where(padding & (place == k), 1.0, rows[k]))
    weights, unit = eliminate(diag, flux)

    flux_col = jnp.concatenate([jnp.full((1, LANES), float(f), F32) for f in flux] + [jnp.zeros((7, LANES), F32)], axis=0)
    flux_cells = jnp.sum(weights * flux_col, axis=0, keepdims=True)
    curve_cells = jnp.sum(unit * flux_col, axis=0, keepdims=True)
    local = jnp.sum(jnp.where(padding, 0.0, flux_cells), axis=1, keepdims=True)
    sum_ref[...] = jnp.broadcast_to(local, (8, LANES))
    copies = []
    for d in range(1, members):
        copy = pltpu.make_async_remote_copy(
            src_ref=sum_ref,
            dst_ref=sum_landed.at[d - 1],
            send_sem=fx_send.at[d - 1],
            recv_sem=fx_recv.at[d - 1],
            device_id=member(d),
            device_id_type=MESH,
        )
        copy.start()
        copies.append(copy)

    both = jnp.concatenate([flux_cells, curve_cells, jnp.zeros((6, LANES), F32)], axis=0)
    spread = pick_sum(jnp.concatenate([weights, unit, both], axis=0), cell_lane[...])
    blocks = width // LANES
    windows = jnp.concatenate(
        [shifted[0:ext_rows, LANES * h : LANES * h + 2 * LANES] for h in range(blocks)], axis=0
    )
    columns = dot3(split2(windows), (fcol[0], fcol[1]))
    for which in range(2):
        for h in range(blocks):
            for b in range(ORDERS):
                acc = None
                for a in range(ORDERS):
                    k = 32 * which + ORDERS * a + b
                    term = spread[k : k + 1, LANES * h : LANES * (h + 1)] * columns[
                        ext_rows * h : ext_rows * (h + 1), LANES * a : LANES * (a + 1)
                    ]
                    acc = term if acc is None else acc + term
                high, low = split2(acc)
                spot = (slice(ext_rows * b, ext_rows * (b + 1)), slice(width * which + LANES * h, width * which + LANES * (h + 1)))
                combined_h[spot] = high
                combined_l[spot] = low
    matched = dot3((frow[0], frow[1]), (combined_h[...], combined_l[...]))
    total = sum_ref[...]
    for d in range(1, members):
        copies[d - 1].wait_recv()
        total = total + sum_landed[d - 1]
    mean_flux = total[0:1, 0:1] * (1.0 / (cells * members))
    correction = (mean_flux - spread[64:65]) / spread[65:66]
    out_ref[...] = image_ref[...] - matched[:, 0:width] - correction * matched[:, width:]
    for copy in copies:
        copy.wait_send()
    for j in range(PIECES):
        for i in range(2):

            @pl.when(side != i)
            def _():
                scatter(i, j).wait_send()

    @pl.when(reduces)
    def _():
        for j in range(PIECES):
            for to in range(visits):

                @pl.when(visit != to)
                def _():
                    own_copy(j, side, to).wait_send()

                if j == 0:
                    for way, (ds, dp) in enumerate(ends):

                        @pl.when(exists(ds, dp) & (side == (ds + 1) // 2))
                        def _():
                            edge_copy(way, to, 1).wait_send()

                for dp in (-1, 1):

                    @pl.when(exists(0, dp))
                    def _():
                        row_copy(j, side, dp, to, dp).wait_send()


def fused(owner, offsets, slot, image, filters, counts):
    width = image.shape[2]
    cells = width // CELL
    visits = counts[1]
    members = counts[0] * counts[2]
    sums = filters.sum(axis=1)
    flux = (sums[:, None] * sums[None, :]).reshape(-1)
    consts = constants(filters, cells)
    pair_rows = sum(32 - 8 * (k // 8) for k in range(NBASIS))
    deep = ORDERS * (ROWS + 2 * PAD)
    full = width + 2 * LANES
    dma = pltpu.SemaphoreType.DMA
    hbm = pl.BlockSpec(memory_space=pltpu.HBM)
    return pl.pallas_call(
        lambda *refs: fused_kernel(counts, flux, *refs),
        name="difference_patch",
        out_shape=jax.ShapeDtypeStruct((ROWS, width), F32),
        in_specs=[hbm] * (4 + len(consts)),
        out_specs=pl.BlockSpec(memory_space=pltpu.VMEM),
        scratch_shapes=[
            pltpu.SMEM(owner.shape, jnp.int32),
            pltpu.SMEM(offsets.shape, jnp.int32),
            pltpu.VMEM((ROWS, width), F32),
            pltpu.VMEM((ROWS, width), F32),
        ]
        + [pltpu.VMEM(const.shape, const.dtype) for const in consts]
        + [
            pltpu.VMEM((ROWS + 2 * PAD, full), F32),
            pltpu.VMEM((visits, ROWS, width // 2), F32),
            pltpu.VMEM((8, LANES), F32),
            pltpu.VMEM((6, 8, LANES), F32),
            pltpu.VMEM((ROWS + 2 * PAD + 8, full), F32),
            pltpu.VMEM((32, STAMP, cells * STAMP), F32),
            pltpu.VMEM((pair_rows, cells * STAMP), F32),
            pltpu.VMEM((deep, 2 * width), BF16),
            pltpu.VMEM((deep, 2 * width), BF16),
            pltpu.VMEM((8, LANES), F32),
            pltpu.VMEM((members - 1, 8, LANES), F32),
            dma((10,)),
            dma((2, PIECES)),
            dma((visits, PIECES)),
            dma((PIECES, visits)),
            dma((2, PIECES)),
            dma((PIECES, 2, visits)),
            dma((2, PIECES, 2)),
            dma((6, visits)),
            dma((6,)),
            dma((members - 1,)),
            dma((members - 1,)),
        ],
        compiler_params=pltpu.CompilerParams(
            collective_id=0, has_side_effects=True, vmem_limit_bytes=40 << 20
        ),
    )(owner, *[pltpu.with_memory_space_constraint(v, pltpu.HBM) for v in (offsets, slot, image, *consts)])


def solution(mesh):
    counts = (mesh.shape["sky"], mesh.shape["visit"], mesh.shape["patch"])
    filters = filter_bank()

    def body(template_store, science, owner_visit, stamp_offset):
        return fused(owner_visit, stamp_offset, template_store, science, filters, counts)[None]

    spec = P("visit", "patch", "sky")
    in_specs = (spec, spec, P("sky", "patch"), P(None, "visit", "patch", "sky"))
    return jax.shard_map(body, mesh=mesh, in_specs=in_specs, out_specs=spec, check_vma=False)
```

```python
import numpy as np
import jax
import jax.numpy as jnp
from jax import lax
from jax.experimental import pallas as pl
from jax.experimental.pallas import tpu as pltpu
from jax.sharding import PartitionSpec as P

HALF = 15
TAPS = 2 * HALF + 1
ORDERS = 5
NBASIS = 25
CELL = 64
STAMP = 32
ROWS = 64
PAD = 16
LANES = 128
PIECES = 2
SIGMA = 5.0
MESH = pl.DeviceIdType.MESH
F32 = jnp.float32
BF16 = jnp.bfloat16


def filter_bank():
    x = (np.arange(TAPS) - HALF) / SIGMA
    env = np.exp(-0.5 * x * x)
    poly = [
        np.ones_like(x),
        2.0 * x,
        4.0 * x**2 - 2.0,
        8.0 * x**3 - 12.0 * x,
        16.0 * x**4 - 48.0 * x**2 + 12.0,
    ]
    shaped = np.stack(poly) * env[None]
    return shaped / np.sqrt(np.sum(shaped * shaped, axis=1, keepdims=True))


def taps_at(filters, index):
    inside = (index >= 0) & (index < TAPS)
    return np.where(inside[None], filters[:, np.clip(index, 0, TAPS - 1)], 0.0)


def halves(values):
    values = np.asarray(values, np.float32)
    high = values.astype(BF16)
    low = (values - high.astype(np.float32)).astype(BF16)
    return [jnp.asarray(np.stack([high, low]))]


def constants(filters, cells):
    width = cells * CELL
    stamp_rows = taps_at(filters, np.arange(CELL)[None, :] - np.arange(STAMP)[:, None])
    stamp_rows = stamp_rows.reshape(ORDERS * STAMP, CELL)
    one = taps_at(filters, np.arange(CELL)[:, None] - np.arange(STAMP)[None, :])
    stamp_cols = np.zeros((4, CELL, ORDERS, 4, STAMP))
    for g in range(4):
        stamp_cols[g, :, :, g, :] = np.transpose(one, (1, 0, 2))
    stamp_cols = stamp_cols.reshape(4 * CELL, ORDERS * LANES)
    full_cols = taps_at(filters, np.arange(2 * LANES)[:, None] - np.arange(LANES)[None, :] - 1)
    full_cols = np.transpose(full_cols, (1, 0, 2)).reshape(2 * LANES, ORDERS * LANES)
    full_rows = taps_at(filters, np.arange(ROWS + 2 * PAD)[None, :] - np.arange(ROWS)[:, None] - 1)
    full_rows = np.transpose(full_rows, (1, 0, 2)).reshape(ROWS, ORDERS * (ROWS + 2 * PAD))
    lane_cell = np.arange(cells * STAMP)[:, None] // STAMP == np.arange(LANES)[None, :]
    cell_lane = np.arange(LANES)[:, None] == np.arange(width)[None, :] // CELL
    return (
        halves(stamp_rows)
        + halves(stamp_cols)
        + halves(full_cols)
        + halves(full_rows)
        + [jnp.asarray(lane_cell, BF16), jnp.asarray(cell_lane, BF16)]
    )


def dot(a, b):
    return jnp.dot(a, b, preferred_element_type=F32)


def split2(x):
    high = x.astype(BF16)
    return high, (x - high.astype(F32)).astype(BF16)


def split3(x):
    high = x.astype(BF16)
    rest = x - high.astype(F32)
    mid = rest.astype(BF16)
    return high, mid, (rest - mid.astype(F32)).astype(BF16)


def dot3(a, b):
    return dot(a[0], b[0]) + (dot(a[0], b[1]) + dot(a[1], b[0]))


def pick_sum(x, selector):
    high, mid, low = split3(x)
    return dot(high, selector) + (dot(mid, selector) + dot(low, selector))


def eliminate(rows, flux):
    count = len(rows)
    starts = [8 * (k // 8) for k in range(count)]
    for j in range(count):
        first = 8 * (j // 8)
        for i in range(j):
            if starts[i] < first:
                rows[i] = rows[i][first - starts[i] :]
                starts[i] = first
        pivot_row = rows[j]
        scaled = pivot_row * (1.0 / pivot_row[j - first : j - first + 1])
        for i in range(count):
            if i < j:
                rows[i] = rows[i] - rows[i][j - first : j - first + 1] * scaled
            elif i > j:
                factor = pivot_row[i - first : i - first + 1]
                rows[i] = rows[i] - factor * scaled[starts[i] - first :]
        rows[j] = scaled
    weights = jnp.concatenate([row[1:2] for row in rows] + [jnp.zeros((7, LANES), F32)], axis=0)
    unit = jnp.concatenate([row[2:3] for row in rows] + [jnp.zeros((7, LANES), F32)], axis=0)
    return weights, unit


def fused_kernel(
    counts, flux, owner_hbm, offset_hbm, slot_hbm, image_hbm,
    srow_hbm, scol_hbm, fcol_hbm, frow_hbm, pick_hbm, put_hbm,
    out_ref,
    owner_ref, offset_ref, slot_ref, image_ref, srow, scol, fcol, frow, lane_cell, cell_lane,
    ext, landed, edge, edge_landed, shifted, stamps, pairs, combined_h, combined_l, sum_ref, sum_landed,
    local_sem, ready, go, rs_send, rs_recv, ag_send, ag_recv, row_recv, edge_send, edge_recv, flux_sem,
):
    sky_count, visits, patches = counts
    members = sky_count * patches
    sky = lax.axis_index("sky")
    visit = lax.axis_index("visit")
    patch = lax.axis_index("patch")
    me = sky * patches + patch
    width = image_ref.shape[1]
    cells = width // CELL
    full = width + 2 * LANES
    ext_rows = ROWS + 2 * PAD
    first_reducer = visits // 2 - 1
    half = width // 2
    piece = half // PIECES
    side = visit - first_reducer
    reduces = (side == 0) | (side == 1)
    outward = 2 * side - 1
    hub = (sky == sky_count - 1) & (patch == 0)

    def inside(ds):
        return (sky + ds >= 0) & (sky + ds < sky_count)

    def there(ds, other, v):
        return {
            "sky": jnp.clip(sky + ds, 0, sky_count - 1),
            "visit": v,
            "patch": 1 - patch if other else patch,
        }

    def member(d):
        other = lax.rem(me + d, members)
        return {"sky": other // patches, "patch": lax.rem(other, patches)}

    def columns_of(i, j):
        at = i * half + (j + i * (PIECES - 1 - 2 * j)) * piece
        return at if isinstance(at, int) else pl.multiple_of(at, LANES)

    def signal(semaphore, where):
        pl.semaphore_signal(semaphore, inc=1, device_id=where, device_id_type=MESH)

    moves = [
        (owner_hbm, owner_ref),
        (offset_hbm, offset_ref),
        (image_hbm.at[0], image_ref),
        (slot_hbm.at[0], slot_ref),
        (srow_hbm, srow),
        (scol_hbm, scol),
        (fcol_hbm, fcol),
        (frow_hbm, frow),
        (pick_hbm, lane_cell),
        (put_hbm, cell_lane),
    ]
    loads = [pltpu.make_async_copy(src, dst, local_sem.at[i]) for i, (src, dst) in enumerate(moves)]

    ext[0:PAD, :] = jnp.zeros((PAD, full), F32)
    ext[PAD + ROWS :, :] = jnp.zeros((PAD, full), F32)
    ext[PAD : PAD + ROWS, 0:LANES] = jnp.zeros((ROWS, LANES), F32)
    ext[PAD : PAD + ROWS, full - LANES :] = jnp.zeros((ROWS, LANES), F32)

    barrier = pltpu.get_barrier_semaphore()

    @pl.when(reduces)
    def _():
        for ds in (0, -1, 1):

            @pl.when(inside(ds))
            def _():
                for other in (0, 1):
                    for to in range(visits):
                        if ds == 0 and not other:

                            @pl.when(visit != to)
                            def _():
                                signal(barrier, there(ds, other, to))

                        else:
                            signal(barrier, there(ds, other, to))

    @pl.when(jnp.logical_not(hub))
    def _():
        signal(barrier, {"sky": sky_count - 1, "patch": 0})

    around = patches * (1 + inside(-1).astype(jnp.int32) + inside(1).astype(jnp.int32))
    alone = reduces.astype(jnp.int32)
    pl.semaphore_wait(barrier, 2 * around - alone + jnp.where(hub, members - 1, 0))

    def scatter(i, j):
        start = columns_of(i, j)
        return pltpu.make_async_remote_copy(
            src_ref=slot_hbm.at[0, :, pl.ds(start, piece)],
            dst_ref=landed.at[visit, :, pl.ds(start - i * half, piece)],
            send_sem=rs_send,
            recv_sem=rs_recv.at[j],
            device_id={"visit": first_reducer + i},
            device_id_type=MESH,
        )

    for j in range(PIECES):
        for i in range(2):

            @pl.when(side != i)
            def _():
                scatter(i, j).start()

    for load in loads:
        load.start()

    for ds in (0, -1, 1):

        @pl.when(inside(ds))
        def _():
            for other in (0, 1):
                for i in range(2):
                    if ds == 0 and not other:

                        @pl.when(side != i)
                        def _():
                            signal(ready, there(ds, other, first_reducer + i))

                    else:
                        signal(ready, there(ds, other, first_reducer + i))

    @pl.when(hub)
    def _():
        for d in range(1, members):
            signal(go, member(d))

    for load in loads[:4]:
        load.wait()
    groups = cells // 4
    lane = lax.broadcasted_iota(jnp.int32, (STAMP, LANES), 1)
    for q in range(groups):
        merged = jnp.zeros((STAMP, LANES), F32)
        for inner in range(4):
            g = 4 * q + inner
            first = LANES * (g // 2)
            block = image_ref[:, first : first + LANES]
            block = pltpu.roll(block, lax.rem(ROWS - offset_ref[0, 0, 0, g], ROWS), 0)[0:STAMP]
            move = lax.rem(2 * LANES + STAMP * inner - CELL * (g % 2) - offset_ref[1, 0, 0, g], LANES)
            merged = jnp.where(lane // STAMP == inner, pltpu.roll(block, move, 1), merged)
        stamps[NBASIS, :, LANES * q : LANES * (q + 1)] = merged
    for spare in range(NBASIS + 1, 32):
        stamps[spare] = jnp.zeros((STAMP, cells * STAMP), F32)

    owner = owner_ref[0, 0]
    lane8 = lax.broadcasted_iota(jnp.int32, (8, LANES), 1) // PAD

    def await_bytes(ref, semaphore):
        pltpu.make_async_copy(ref, ref, semaphore).wait()

    def own_copy(j, to):
        spot = ext.at[pl.ds(PAD, ROWS), pl.ds(LANES + columns_of(side, j), piece)]
        return pltpu.make_async_remote_copy(
            src_ref=spot,
            dst_ref=spot,
            send_sem=ag_send,
            recv_sem=ag_recv.at[side, j],
            device_id={"visit": to},
            device_id_type=MESH,
        )

    def row_copy(j, to):
        at = pl.ds(LANES + columns_of(side, j), piece)
        return pltpu.make_async_remote_copy(
            src_ref=ext.at[pl.ds(pl.multiple_of(ROWS - (ROWS - PAD) * patch, 8), PAD), at],
            dst_ref=ext.at[pl.ds(pl.multiple_of((PAD + ROWS) * patch, 8), PAD), at],
            send_sem=ag_send,
            recv_sem=row_recv,
            device_id=there(0, 1, to),
            device_id_type=MESH,
        )

    def edge_copy(to, other):
        return pltpu.make_async_remote_copy(
            src_ref=edge,
            dst_ref=edge_landed.at[side, other],
            send_sem=edge_send,
            recv_sem=edge_recv.at[side],
            device_id=there(outward, other, to),
            device_id_type=MESH,
        )

    def spread_piece(j, to):
        @pl.when(visit != to)
        def _():
            own_copy(j, to).start()

        row_copy(j, to).start()
        if j == 0:

            @pl.when(inside(outward))
            def _():
                for other in (0, 1):
                    edge_copy(to, other).start()

    @pl.when(reduces)
    def _():
        pl.semaphore_wait(ready, around * visits - 1)
        for j in range(PIECES):
            start = columns_of(side, j)
            spot = pl.ds(pl.multiple_of(start - side * half, LANES), piece)
            await_bytes(landed.at[pl.ds(0, visits - 1), :, spot], rs_recv.at[j])
            current = slot_ref[:, pl.ds(start, piece)]
            for d in range(1, visits):
                source = lax.rem(visit + visits - d, visits)
                current = jnp.where(owner == source, landed[source, :, spot], current)
            ext[PAD : PAD + ROWS, pl.ds(LANES + start, piece)] = current
            if j == 0:
                merged = jnp.zeros((8, LANES), F32)
                for r in range(ROWS // 8):
                    left = pltpu.roll(current[8 * r : 8 * r + 8, 0:LANES], (PAD * r) % LANES, 1)
                    right = pltpu.roll(current[8 * r : 8 * r + 8, piece - LANES :], (PAD * (r + 1)) % LANES, 1)
                    merged = jnp.where(lane8 == r, jnp.where(side == 0, left, right), merged)
                edge[...] = merged
            spread_piece(j, 0)
        for to in range(1, visits):
            for j in range(PIECES):
                spread_piece(j, to)

    for load in loads[4:]:
        load.wait()
    for i in range(2):

        @pl.when(side != i)
        def _():
            for j in range(PIECES):
                await_bytes(ext.at[pl.ds(PAD, ROWS), pl.ds(LANES, piece)], ag_recv.at[i, j])

    await_bytes(ext.at[pl.ds(0, PAD), pl.ds(LANES, width)], row_recv)
    for i in range(2):

        @pl.when(inside(1 - 2 * i))
        def _():
            await_bytes(edge_landed.at[i], edge_recv.at[i])
            first, base = (full - LANES, 0) if i == 0 else (0, LANES - PAD)
            packed = edge_landed[i, 0]
            for r in range(ROWS // 8):
                moved = pltpu.roll(packed, (base - PAD * r) % LANES, 1)
                ext[PAD + 8 * r : PAD + 8 * r + 8, first : first + LANES] = moved
            packed = pltpu.roll(edge_landed[i, 1], lax.rem(base + LANES - (LANES - 2 * PAD) * patch, LANES), 1)
            row = pl.multiple_of((PAD + ROWS) * (1 - patch), 8)
            ext[pl.ds(row, 8), first : first + LANES] = packed
            ext[pl.ds(row + 8, 8), first : first + LANES] = pltpu.roll(packed, LANES - PAD, 1)

    shifted[0:ext_rows, :] = pltpu.roll(ext[...], full - (LANES - PAD), 1)
    shifted[ext_rows:, :] = jnp.zeros((8, full), F32)

    lane = lax.broadcasted_iota(jnp.int32, (CELL, LANES), 1)
    windows = []
    for h in range(cells // 2):
        parts = []
        for odd in range(2):
            g = 2 * h + odd
            block = shifted[:, LANES * h : LANES * h + 2 * LANES]
            block = pltpu.roll(block, ext_rows + 7 - offset_ref[0, 0, 0, g], 0)[0:CELL]
            move = 2 * LANES - offset_ref[1, 0, 0, g] - 1
            parts.append(pltpu.roll(block, move, 1)[:, 0:LANES])
        windows.append(jnp.where(lane < CELL, parts[0], parts[1]))
    window = jnp.concatenate(windows, axis=1)
    rows_done = dot3((srow[0], srow[1]), split2(window))
    stacked = jnp.concatenate([rows_done[:, 4 * CELL * q : 4 * CELL * (q + 1)] for q in range(groups)], axis=0)
    basis = dot3(split2(stacked), (scol[0], scol[1]))
    for q in range(groups):
        for b in range(ORDERS):
            first = (q * ORDERS + b) * STAMP
            for a in range(ORDERS):
                stamps[ORDERS * a + b, :, LANES * q : LANES * (q + 1)] = basis[first : first + STAMP, LANES * a : LANES * (a + 1)]
    spots = []
    at = 0
    for k in range(NBASIS):
        low = 8 * (k // 8)
        mine = stamps[k]
        for tile in range(low, 32, 8):
            pairs[at + tile - low : at + tile - low + 8, :] = jnp.sum(stamps[tile : tile + 8] * mine[None], axis=1)
        spots.append((at, 32 - low))
        at += 32 - low
    sums = pick_sum(pairs[...], lane_cell[...])
    rows = []
    for k, (at, length) in enumerate(spots):
        row = sums[at : at + length]
        place = lax.broadcasted_iota(jnp.int32, row.shape, 0) + (32 - length)
        row = jnp.where(place == NBASIS + 1, float(flux[k]), row)
        rows.append(row)
    padding = lax.broadcasted_iota(jnp.int32, (1, LANES), 1) >= cells
    diag = []
    for k, (at, length) in enumerate(spots):
        place = lax.broadcasted_iota(jnp.int32, rows[k].shape, 0) + (32 - length)
        diag.append(jnp.where(padding & (place == k), 1.0, rows[k]))
    weights, unit = eliminate(diag, flux)

    flux_col = jnp.concatenate([jnp.full((1, LANES), float(f), F32) for f in flux] + [jnp.zeros((7, LANES), F32)], axis=0)
    flux_cells = jnp.sum(weights * flux_col, axis=0, keepdims=True)
    curve_cells = jnp.sum(unit * flux_col, axis=0, keepdims=True)
    local = jnp.sum(jnp.where(padding, 0.0, flux_cells), axis=1, keepdims=True)
    sum_ref[...] = jnp.broadcast_to(local, (8, LANES))
    @pl.when(jnp.logical_not(hub))
    def _():
        pl.semaphore_wait(go, 1)

    for d in range(1, members):
        pltpu.make_async_remote_copy(
            src_ref=sum_ref,
            dst_ref=sum_landed.at[d - 1],
            send_sem=flux_sem.at[0],
            recv_sem=flux_sem.at[1],
            device_id=member(d),
            device_id_type=MESH,
        ).start()

    both = jnp.concatenate([flux_cells, curve_cells, jnp.zeros((6, LANES), F32)], axis=0)
    spread = pick_sum(jnp.concatenate([weights, unit, both], axis=0), cell_lane[...])
    blocks = width // LANES
    windows = jnp.concatenate(
        [shifted[0:ext_rows, LANES * h : LANES * h + 2 * LANES] for h in range(blocks)], axis=0
    )
    columns = dot3(split2(windows), (fcol[0], fcol[1]))
    for which in range(2):
        for h in range(blocks):
            for b in range(ORDERS):
                acc = None
                for a in range(ORDERS):
                    k = 32 * which + ORDERS * a + b
                    term = spread[k : k + 1, LANES * h : LANES * (h + 1)] * columns[
                        ext_rows * h : ext_rows * (h + 1), LANES * a : LANES * (a + 1)
                    ]
                    acc = term if acc is None else acc + term
                high, low = split2(acc)
                spot = (slice(ext_rows * b, ext_rows * (b + 1)), slice(width * which + LANES * h, width * which + LANES * (h + 1)))
                combined_h[spot] = high
                combined_l[spot] = low
    matched = dot3((frow[0], frow[1]), (combined_h[...], combined_l[...]))
    total = sum_ref[...]
    await_bytes(sum_landed, flux_sem.at[1])
    for d in range(1, members):
        total = total + sum_landed[d - 1]
    mean_flux = total[0:1, 0:1] * (1.0 / (cells * members))
    correction = (mean_flux - spread[64:65]) / spread[65:66]
    out_ref[...] = image_ref[...] - matched[:, 0:width] - correction * matched[:, width:]
    await_bytes(sum_landed, flux_sem.at[0])

    @pl.when(reduces)
    def _():
        await_bytes(landed.at[0], rs_send)
        await_bytes(landed, ag_send)

        @pl.when(inside(outward))
        def _():
            await_bytes(landed.at[0, pl.ds(0, 2 * 8 * visits * LANES // half)], edge_send)

    @pl.when(jnp.logical_not(reduces))
    def _():
        await_bytes(slot_ref, rs_send)


def fused(owner, offsets, slot, image, filters, counts):
    width = image.shape[2]
    cells = width // CELL
    visits = counts[1]
    members = counts[0] * counts[2]
    sums = filters.sum(axis=1)
    flux = (sums[:, None] * sums[None, :]).reshape(-1)
    consts = constants(filters, cells)
    pair_rows = sum(32 - 8 * (k // 8) for k in range(NBASIS))
    deep = ORDERS * (ROWS + 2 * PAD)
    full = width + 2 * LANES
    dma = pltpu.SemaphoreType.DMA
    hbm = pl.BlockSpec(memory_space=pltpu.HBM)
    return pl.pallas_call(
        lambda *refs: fused_kernel(counts, flux, *refs),
        name="difference_patch",
        out_shape=jax.ShapeDtypeStruct((ROWS, width), F32),
        in_specs=[hbm] * (4 + len(consts)),
        out_specs=pl.BlockSpec(memory_space=pltpu.VMEM),
        scratch_shapes=[
            pltpu.SMEM(owner.shape, jnp.int32),
            pltpu.SMEM(offsets.shape, jnp.int32),
            pltpu.VMEM((ROWS, width), F32),
            pltpu.VMEM((ROWS, width), F32),
        ]
        + [pltpu.VMEM(const.shape, const.dtype) for const in consts]
        + [
            pltpu.VMEM((ROWS + 2 * PAD, full), F32),
            pltpu.VMEM((visits, ROWS, width // 2), F32),
            pltpu.VMEM((8, LANES), F32),
            pltpu.VMEM((2, 2, 8, LANES), F32),
            pltpu.VMEM((ROWS + 2 * PAD + 8, full), F32),
            pltpu.VMEM((32, STAMP, cells * STAMP), F32),
            pltpu.VMEM((pair_rows, cells * STAMP), F32),
            pltpu.VMEM((deep, 2 * width), BF16),
            pltpu.VMEM((deep, 2 * width), BF16),
            pltpu.VMEM((8, LANES), F32),
            pltpu.VMEM((members - 1, 8, LANES), F32),
            dma((10,)),
            pltpu.SemaphoreType.REGULAR,
            pltpu.SemaphoreType.REGULAR,
            dma,
            dma((PIECES,)),
            dma,
            dma((2, PIECES)),
            dma,
            dma,
            dma((2,)),
            dma((2,)),
        ],
        compiler_params=pltpu.CompilerParams(
            collective_id=0, has_side_effects=True, vmem_limit_bytes=40 << 20
        ),
    )(owner, *[pltpu.with_memory_space_constraint(v, pltpu.HBM) for v in (offsets, slot, image, *consts)])


def solution(mesh):
    counts = (mesh.shape["sky"], mesh.shape["visit"], mesh.shape["patch"])
    filters = filter_bank()

    def body(template_store, science, owner_visit, stamp_offset):
        return fused(owner_visit, stamp_offset, template_store, science, filters, counts)[None]

    spec = P("visit", "patch", "sky")
    in_specs = (spec, spec, P("sky", "patch"), P(None, "visit", "patch", "sky"))
    return jax.shard_map(body, mesh=mesh, in_specs=in_specs, out_specs=spec, check_vma=False)
```

```python
import numpy as np
import jax
import jax.numpy as jnp
from jax import lax
from jax.experimental import pallas as pl
from jax.experimental.pallas import tpu as pltpu
from jax.sharding import PartitionSpec as P

HALF = 15
TAPS = 2 * HALF + 1
ORDERS = 5
NBASIS = 25
CELL = 64
STAMP = 32
ROWS = 64
PAD = 16
LANES = 128
PIECES = 2
APART = ORDERS * STAMP + 1
SIGMA = 5.0
MESH = pl.DeviceIdType.MESH
F32 = jnp.float32
BF16 = jnp.bfloat16


def filter_bank():
    x = (np.arange(TAPS) - HALF) / SIGMA
    env = np.exp(-0.5 * x * x)
    poly = [
        np.ones_like(x),
        2.0 * x,
        4.0 * x**2 - 2.0,
        8.0 * x**3 - 12.0 * x,
        16.0 * x**4 - 48.0 * x**2 + 12.0,
    ]
    shaped = np.stack(poly) * env[None]
    return shaped / np.sqrt(np.sum(shaped * shaped, axis=1, keepdims=True))


def taps_at(filters, index):
    inside = (index >= 0) & (index < TAPS)
    return np.where(inside[None], filters[:, np.clip(index, 0, TAPS - 1)], 0.0)


def two_parts(values):
    values = np.asarray(values, np.float32)
    high = values.astype(BF16)
    return high, (values - high.astype(np.float32)).astype(BF16)


def halves(values):
    return [jnp.asarray(np.stack(two_parts(values)))]


def stacked_halves(values, axis):
    high, low = two_parts(values)
    return [jnp.asarray(np.concatenate([high, high, low, low], axis=axis))]


def constants(filters, cells):
    width = cells * CELL
    stamp_rows = taps_at(filters, np.arange(CELL)[None, :] - np.arange(STAMP)[:, None])
    stamp_rows = stamp_rows.reshape(ORDERS * STAMP, CELL)
    stamp_cols = taps_at(filters, np.arange(CELL)[:, None] - np.arange(STAMP)[None, :])
    high, low = [np.asarray(part, np.float32) for part in two_parts(stamp_cols)]
    placed = np.zeros((4 * 3 * CELL, ORDERS, 4, STAMP), np.float32)
    for m in range(4):
        for part in range(2):
            at = 2 * CELL * m + CELL * part
            placed[at : at + CELL, :, m, :] = np.transpose(high, (1, 0, 2))
        at = 8 * CELL + CELL * m
        placed[at : at + CELL, :, m, :] = np.transpose(low, (1, 0, 2))
    placed = placed.reshape(-1, ORDERS * LANES)
    full_cols = taps_at(filters, np.arange(2 * LANES)[:, None] - np.arange(LANES)[None, :] - 1)
    full_cols = np.transpose(full_cols, (1, 0, 2)).reshape(2 * LANES, ORDERS * LANES)
    full_rows = taps_at(filters, np.arange(ROWS + 2 * PAD)[None, :] - np.arange(ROWS)[:, None] - 1)
    full_rows = np.transpose(full_rows, (1, 0, 2)).reshape(ROWS, ORDERS * (ROWS + 2 * PAD))
    cell_lane = np.arange(LANES)[:, None] == np.arange(width)[None, :] // CELL
    return (
        stacked_halves(stamp_rows, 1)
        + [jnp.asarray(placed, BF16)]
        + halves(full_cols)
        + halves(full_rows)
        + [jnp.asarray(cell_lane, BF16)]
    )


def dot(a, b):
    return jnp.dot(a, b, preferred_element_type=F32)


def split2(x):
    high = x.astype(BF16)
    return high, (x - high.astype(F32)).astype(BF16)


def split3(x):
    high = x.astype(BF16)
    rest = x - high.astype(F32)
    mid = rest.astype(BF16)
    return high, mid, (rest - mid.astype(F32)).astype(BF16)


def dot3(a, b):
    return dot(a[0], b[0]) + (dot(a[0], b[1]) + dot(a[1], b[0]))


def pick_sum(x, selector):
    high, mid, low = split3(x)
    return dot(high, selector) + (dot(mid, selector) + dot(low, selector))


def eliminate(rows, flux):
    count = len(rows)
    starts = [8 * (k // 8) for k in range(count)]
    for j in range(count):
        first = 8 * (j // 8)
        for i in range(j):
            if starts[i] < first:
                rows[i] = rows[i][first - starts[i] :]
                starts[i] = first
        pivot_row = rows[j]
        scaled = pivot_row * (1.0 / pivot_row[j - first : j - first + 1])
        for i in range(count):
            if i < j:
                rows[i] = rows[i] - rows[i][j - first : j - first + 1] * scaled
            elif i > j:
                factor = pivot_row[i - first : i - first + 1]
                rows[i] = rows[i] - factor * scaled[starts[i] - first :]
        rows[j] = scaled
    weights = jnp.concatenate([row[1:2] for row in rows] + [jnp.zeros((7, LANES), F32)], axis=0)
    unit = jnp.concatenate([row[2:3] for row in rows] + [jnp.zeros((7, LANES), F32)], axis=0)
    return weights, unit


def fused_kernel(
    counts, flux, owner_hbm, offset_hbm, slot_hbm, image_hbm,
    srow_hbm, scol_hbm, fcol_hbm, frow_hbm, put_hbm,
    out_ref,
    owner_ref, offset_ref, slot_ref, image_ref, srow, scol, fcol, frow, cell_lane,
    ext, landed, edge, edge_landed, shifted, image_rows, image_stamps, filtered, combined_h, combined_l, sum_ref, sum_landed,
    local_sem, ready, go, rs_send, rs_recv, ag_send, ag_recv, row_recv, edge_send, edge_recv, flux_sem,
):
    sky_count, visits, patches = counts
    members = sky_count * patches
    sky = lax.axis_index("sky")
    visit = lax.axis_index("visit")
    patch = lax.axis_index("patch")
    me = sky * patches + patch
    width = image_ref.shape[1]
    cells = width // CELL
    full = width + 2 * LANES
    ext_rows = ROWS + 2 * PAD
    first_reducer = visits // 2 - 1
    half = width // 2
    piece = half // PIECES
    side = visit - first_reducer
    reduces = (side == 0) | (side == 1)
    outward = 2 * side - 1
    hub = (sky == sky_count - 1) & (patch == 0)

    def inside(ds):
        return (sky + ds >= 0) & (sky + ds < sky_count)

    def there(ds, other, v):
        return {
            "sky": jnp.clip(sky + ds, 0, sky_count - 1),
            "visit": v,
            "patch": 1 - patch if other else patch,
        }

    def member(d):
        other = lax.rem(me + d, members)
        return {"sky": other // patches, "patch": lax.rem(other, patches)}

    def columns_of(i, j):
        at = i * half + (j + i * (PIECES - 1 - 2 * j)) * piece
        return at if isinstance(at, int) else pl.multiple_of(at, LANES)

    def signal(semaphore, where):
        pl.semaphore_signal(semaphore, inc=1, device_id=where, device_id_type=MESH)

    moves = [
        (owner_hbm, owner_ref),
        (offset_hbm, offset_ref),
        (image_hbm.at[0], image_ref),
        (slot_hbm.at[0], slot_ref),
        (srow_hbm, srow),
        (scol_hbm, scol),
        (fcol_hbm, fcol),
        (frow_hbm, frow),
        (put_hbm, cell_lane),
    ]
    loads = [pltpu.make_async_copy(src, dst, local_sem.at[i]) for i, (src, dst) in enumerate(moves)]

    ext[0:PAD, :] = jnp.zeros((PAD, full), F32)
    ext[PAD + ROWS :, :] = jnp.zeros((PAD + 8, full), F32)
    ext[PAD : PAD + ROWS, 0:LANES] = jnp.zeros((ROWS, LANES), F32)
    ext[PAD : PAD + ROWS, full - LANES :] = jnp.zeros((ROWS, LANES), F32)

    barrier = pltpu.get_barrier_semaphore()

    @pl.when(reduces)
    def _():
        for ds in (0, -1, 1):

            @pl.when(inside(ds))
            def _():
                for other in (0, 1):
                    for to in range(visits):
                        if ds == 0 and not other:

                            @pl.when(visit != to)
                            def _():
                                signal(barrier, there(ds, other, to))

                        else:
                            signal(barrier, there(ds, other, to))

    @pl.when(jnp.logical_not(hub))
    def _():
        signal(barrier, {"sky": sky_count - 1, "patch": 0})

    around = patches * (1 + inside(-1).astype(jnp.int32) + inside(1).astype(jnp.int32))
    alone = reduces.astype(jnp.int32)
    pl.semaphore_wait(barrier, 2 * around - alone + jnp.where(hub, members - 1, 0))

    def scatter(i, j):
        start = columns_of(i, j)
        return pltpu.make_async_remote_copy(
            src_ref=slot_hbm.at[0, :, pl.ds(start, piece)],
            dst_ref=landed.at[visit, :, pl.ds(start - i * half, piece)],
            send_sem=rs_send,
            recv_sem=rs_recv.at[j],
            device_id={"visit": first_reducer + i},
            device_id_type=MESH,
        )

    for j in range(PIECES):
        for i in range(2):

            @pl.when(side != i)
            def _():
                scatter(i, j).start()

    for load in loads:
        load.start()

    for ds in (0, -1, 1):

        @pl.when(inside(ds))
        def _():
            for other in (0, 1):
                for i in range(2):
                    if ds == 0 and not other:

                        @pl.when(side != i)
                        def _():
                            signal(ready, there(ds, other, first_reducer + i))

                    else:
                        signal(ready, there(ds, other, first_reducer + i))

    @pl.when(hub)
    def _():
        for d in range(1, members):
            signal(go, member(d))

    for load in loads[:4]:
        load.wait()
    lane = lax.broadcasted_iota(jnp.int32, (STAMP, LANES), 1)
    for g in range(cells):
        first = LANES * (g // 2)
        block = image_ref[:, first : first + LANES]
        block = pltpu.roll(block, lax.rem(ROWS - offset_ref[0, 0, 0, g], ROWS), 0)[0:STAMP]
        block = pltpu.roll(block, lax.rem(2 * LANES - CELL * (g % 2) - offset_ref[1, 0, 0, g], LANES), 1)
        block = jnp.where(lane < STAMP, block, pltpu.roll(block, STAMP, 1))
        block = jnp.where(lane < 2 * STAMP, block, pltpu.roll(block, 2 * STAMP, 1))
        image_rows[STAMP * g : STAMP * (g + 1), :] = block
    group8 = lax.broadcasted_iota(jnp.int32, (cells, LANES), 1) // STAMP
    for j in range(STAMP // 4):
        merged = image_rows[pl.ds(4 * j, cells, stride=STAMP), :]
        for m in range(1, 4):
            merged = jnp.where(group8 == m, image_rows[pl.ds(4 * j + m, cells, stride=STAMP), :], merged)
        image_stamps[:, LANES * j : LANES * (j + 1)] = merged

    owner = owner_ref[0, 0]
    lane8 = lax.broadcasted_iota(jnp.int32, (8, LANES), 1) // PAD

    def await_bytes(ref, semaphore):
        pltpu.make_async_copy(ref, ref, semaphore).wait()

    def own_copy(j, to):
        spot = ext.at[pl.ds(PAD, ROWS), pl.ds(LANES + columns_of(side, j), piece)]
        return pltpu.make_async_remote_copy(
            src_ref=spot,
            dst_ref=spot,
            send_sem=ag_send,
            recv_sem=ag_recv.at[side, j],
            device_id={"visit": to},
            device_id_type=MESH,
        )

    def row_copy(j, to):
        at = pl.ds(LANES + columns_of(side, j), piece)
        return pltpu.make_async_remote_copy(
            src_ref=ext.at[pl.ds(pl.multiple_of(ROWS - (ROWS - PAD) * patch, 8), PAD), at],
            dst_ref=ext.at[pl.ds(pl.multiple_of((PAD + ROWS) * patch, 8), PAD), at],
            send_sem=ag_send,
            recv_sem=row_recv,
            device_id=there(0, 1, to),
            device_id_type=MESH,
        )

    def edge_copy(to, other):
        return pltpu.make_async_remote_copy(
            src_ref=edge,
            dst_ref=edge_landed.at[side, other],
            send_sem=edge_send,
            recv_sem=edge_recv.at[side],
            device_id=there(outward, other, to),
            device_id_type=MESH,
        )

    def spread_piece(j, to):
        @pl.when(visit != to)
        def _():
            own_copy(j, to).start()

        row_copy(j, to).start()
        if j == 0:

            @pl.when(inside(outward))
            def _():
                for other in (0, 1):
                    edge_copy(to, other).start()

    @pl.when(reduces)
    def _():
        pl.semaphore_wait(ready, around * visits - 1)
        for j in range(PIECES):
            start = columns_of(side, j)
            spot = pl.ds(pl.multiple_of(start - side * half, LANES), piece)
            await_bytes(landed.at[pl.ds(0, visits - 1), :, spot], rs_recv.at[j])
            current = slot_ref[:, pl.ds(start, piece)]
            for d in range(1, visits):
                source = lax.rem(visit + visits - d, visits)
                current = jnp.where(owner == source, landed[source, :, spot], current)
            ext[PAD : PAD + ROWS, pl.ds(LANES + start, piece)] = current
            if j == 0:
                merged = jnp.zeros((8, LANES), F32)
                for r in range(ROWS // 8):
                    left = pltpu.roll(current[8 * r : 8 * r + 8, 0:LANES], (PAD * r) % LANES, 1)
                    right = pltpu.roll(current[8 * r : 8 * r + 8, piece - LANES :], (PAD * (r + 1)) % LANES, 1)
                    merged = jnp.where(lane8 == r, jnp.where(side == 0, left, right), merged)
                edge[...] = merged
            spread_piece(j, 0)
        for to in range(1, visits):
            for j in range(PIECES):
                spread_piece(j, to)

    for load in loads[4:]:
        load.wait()
    for i in range(2):

        @pl.when(side != i)
        def _():
            for j in range(PIECES):
                await_bytes(ext.at[pl.ds(PAD, ROWS), pl.ds(LANES, piece)], ag_recv.at[i, j])

    await_bytes(ext.at[pl.ds(0, PAD), pl.ds(LANES, width)], row_recv)
    for i in range(2):

        @pl.when(inside(1 - 2 * i))
        def _():
            await_bytes(edge_landed.at[i], edge_recv.at[i])
            first, base = (full - LANES, 0) if i == 0 else (0, LANES - PAD)
            packed = edge_landed[i, 0]
            for r in range(ROWS // 8):
                moved = pltpu.roll(packed, (base - PAD * r) % LANES, 1)
                ext[PAD + 8 * r : PAD + 8 * r + 8, first : first + LANES] = moved
            packed = pltpu.roll(edge_landed[i, 1], lax.rem(base + LANES - (LANES - 2 * PAD) * patch, LANES), 1)
            row = pl.multiple_of((PAD + ROWS) * (1 - patch), 8)
            ext[pl.ds(row, 8), first : first + LANES] = packed
            ext[pl.ds(row + 8, 8), first : first + LANES] = pltpu.roll(packed, LANES - PAD, 1)

    shifted[...] = pltpu.roll(ext[...], full - (LANES - PAD), 1)
    tall = ext_rows + 8
    lane = lax.broadcasted_iota(jnp.int32, (CELL, LANES), 1)
    windows = []
    for g in range(cells):
        first = LANES * (g // 2)
        block = pltpu.roll(shifted[:, first : first + 2 * LANES], 2 * LANES - 1 - offset_ref[1, 0, 0, g], 1)[:, 0:LANES]
        block = pltpu.roll(block, tall - 1 - offset_ref[0, 0, 0, g], 0)[0:CELL]
        own = lane < CELL if g % 2 == 0 else lane >= CELL
        windows.append(jnp.where(own, block, pltpu.roll(block, CELL, 1)))
    high, low = split2(jnp.concatenate(windows, axis=1))
    rows_done = dot(srow[...], jnp.concatenate([high, low, high, low], axis=0))
    count = ORDERS * STAMP
    for g in range(cells):
        filtered[APART * g : APART * g + count, :] = rows_done[:, LANES * g : LANES * (g + 1)]
    lane = lax.broadcasted_iota(jnp.int32, (cells * count // 4, LANES), 1)
    parts, tops = [], []
    for m in range(4):
        by_cell = jnp.concatenate([filtered[pl.ds(r, cells, stride=APART), :] for r in range(m, count, 4)], axis=0)
        top = by_cell.astype(BF16).astype(F32)
        parts.append(jnp.where(lane < CELL, top, by_cell - top).astype(BF16))
        tops.append(top)
    for m in (0, 2):
        parts.append(jnp.where(lane < CELL, tops[m], tops[m + 1]).astype(BF16))
    basis = dot(jnp.concatenate(parts, axis=1), scol[...])
    filled = [basis[:, LANES * a : LANES * (a + 1)].reshape(count // 4, cells, LANES) for a in range(ORDERS)]
    eighth = STAMP // 4
    flat = [
        jnp.concatenate([filled[a][eighth * b + j] for j in range(eighth)], axis=1)
        for a in range(ORDERS)
        for b in range(ORDERS)
    ]
    high, low = split2(jnp.concatenate(flat + [image_stamps[...]], axis=0))
    used = cells * (NBASIS + 1)
    spare = jnp.zeros((2 * LANES - used, STAMP * STAMP), BF16)
    across = (((1,), (1,)), ((), ()))
    high_all, low_all = jnp.concatenate([high, spare], axis=0), jnp.concatenate([low, spare], axis=0)
    gram = lax.dot_general(jnp.concatenate([high, low], axis=0), high_all, across, preferred_element_type=F32)
    gram = gram[:used] + gram[used:] + lax.dot_general(high, low_all, across, preferred_element_type=F32)
    gram = gram.reshape(NBASIS + 1, cells, 2 * LANES)
    same = lax.rem(lax.broadcasted_iota(jnp.int32, gram.shape, 2), cells) == lax.broadcasted_iota(jnp.int32, gram.shape, 1)
    sums = jnp.sum(jnp.where(same, gram, 0.0), axis=1)
    sums = jnp.concatenate([sums, jnp.zeros((32 - NBASIS - 1, 2 * LANES), F32)], axis=0)
    padding = lax.broadcasted_iota(jnp.int32, (1, LANES), 1) >= cells
    diag = []
    for k in range(NBASIS):
        low = 8 * (k // 8)
        tile, at = divmod(cells * k, LANES)
        row = sums[low:, LANES * tile : LANES * (tile + 1)]
        row = pltpu.roll(row, LANES - at, 1) if at else row
        place = lax.broadcasted_iota(jnp.int32, row.shape, 0) + low
        diag.append(jnp.where(place == NBASIS + 1, float(flux[k]), row))
    weights, unit = eliminate(diag, flux)
    weights = jnp.where(padding, 0.0, weights)
    unit = jnp.where(padding, 0.0, unit)

    flux_col = jnp.concatenate([jnp.full((1, LANES), float(f), F32) for f in flux] + [jnp.zeros((7, LANES), F32)], axis=0)
    flux_cells = jnp.sum(weights * flux_col, axis=0, keepdims=True)
    curve_cells = jnp.sum(unit * flux_col, axis=0, keepdims=True)
    local = jnp.sum(flux_cells, axis=1, keepdims=True)
    sum_ref[...] = jnp.broadcast_to(local, (8, LANES))
    @pl.when(jnp.logical_not(hub))
    def _():
        pl.semaphore_wait(go, 1)

    for d in range(1, members):
        pltpu.make_async_remote_copy(
            src_ref=sum_ref,
            dst_ref=sum_landed.at[d - 1],
            send_sem=flux_sem.at[0],
            recv_sem=flux_sem.at[1],
            device_id=member(d),
            device_id_type=MESH,
        ).start()

    both = jnp.concatenate([flux_cells, curve_cells, jnp.zeros((6, LANES), F32)], axis=0)
    spread = pick_sum(jnp.concatenate([weights, unit, both], axis=0), cell_lane[...])
    blocks = width // LANES
    windows = jnp.concatenate(
        [shifted[0:ext_rows, LANES * h : LANES * h + 2 * LANES] for h in range(blocks)], axis=0
    )
    columns = dot3(split2(windows), (fcol[0], fcol[1]))
    for which in range(2):
        for h in range(blocks):
            for b in range(ORDERS):
                acc = None
                for a in range(ORDERS):
                    k = 32 * which + ORDERS * a + b
                    term = spread[k : k + 1, LANES * h : LANES * (h + 1)] * columns[
                        ext_rows * h : ext_rows * (h + 1), LANES * a : LANES * (a + 1)
                    ]
                    acc = term if acc is None else acc + term
                high, low = split2(acc)
                spot = (slice(ext_rows * b, ext_rows * (b + 1)), slice(width * which + LANES * h, width * which + LANES * (h + 1)))
                combined_h[spot] = high
                combined_l[spot] = low
    matched = dot3((frow[0], frow[1]), (combined_h[...], combined_l[...]))
    total = sum_ref[...]
    await_bytes(sum_landed, flux_sem.at[1])
    for d in range(1, members):
        total = total + sum_landed[d - 1]
    mean_flux = total[0:1, 0:1] * (1.0 / (cells * members))
    correction = (mean_flux - spread[64:65]) / spread[65:66]
    out_ref[...] = image_ref[...] - matched[:, 0:width] - correction * matched[:, width:]
    await_bytes(sum_landed, flux_sem.at[0])

    @pl.when(reduces)
    def _():
        await_bytes(landed.at[0], rs_send)
        await_bytes(landed, ag_send)

        @pl.when(inside(outward))
        def _():
            await_bytes(landed.at[0, pl.ds(0, 2 * 8 * visits * LANES // half)], edge_send)

    @pl.when(jnp.logical_not(reduces))
    def _():
        await_bytes(slot_ref, rs_send)


def fused(owner, offsets, slot, image, filters, counts):
    width = image.shape[2]
    cells = width // CELL
    visits = counts[1]
    members = counts[0] * counts[2]
    sums = filters.sum(axis=1)
    flux = (sums[:, None] * sums[None, :]).reshape(-1)
    consts = constants(filters, cells)
    deep = ORDERS * (ROWS + 2 * PAD)
    full = width + 2 * LANES
    dma = pltpu.SemaphoreType.DMA
    hbm = pl.BlockSpec(memory_space=pltpu.HBM)
    return pl.pallas_call(
        lambda *refs: fused_kernel(counts, flux, *refs),
        name="difference_patch",
        out_shape=jax.ShapeDtypeStruct((ROWS, width), F32),
        in_specs=[hbm] * (4 + len(consts)),
        out_specs=pl.BlockSpec(memory_space=pltpu.VMEM),
        scratch_shapes=[
            pltpu.SMEM(owner.shape, jnp.int32),
            pltpu.SMEM(offsets.shape, jnp.int32),
            pltpu.VMEM((ROWS, width), F32),
            pltpu.VMEM((ROWS, width), F32),
        ]
        + [pltpu.VMEM(const.shape, const.dtype) for const in consts]
        + [
            pltpu.VMEM((ROWS + 2 * PAD + 8, full), F32),
            pltpu.VMEM((visits, ROWS, width // 2), F32),
            pltpu.VMEM((8, LANES), F32),
            pltpu.VMEM((2, 2, 8, LANES), F32),
            pltpu.VMEM((ROWS + 2 * PAD + 8, full), F32),
            pltpu.VMEM((cells * STAMP, LANES), F32),
            pltpu.VMEM((cells, STAMP * STAMP), F32),
            pltpu.VMEM((cells * (APART + 1), LANES), F32),
            pltpu.VMEM((deep, 2 * width), BF16),
            pltpu.VMEM((deep, 2 * width), BF16),
            pltpu.VMEM((8, LANES), F32),
            pltpu.VMEM((members - 1, 8, LANES), F32),
            dma((9,)),
            pltpu.SemaphoreType.REGULAR,
            pltpu.SemaphoreType.REGULAR,
            dma,
            dma((PIECES,)),
            dma,
            dma((2, PIECES)),
            dma,
            dma,
            dma((2,)),
            dma((2,)),
        ],
        compiler_params=pltpu.CompilerParams(
            collective_id=0, has_side_effects=True, vmem_limit_bytes=40 << 20
        ),
    )(owner, *[pltpu.with_memory_space_constraint(v, pltpu.HBM) for v in (offsets, slot, image, *consts)])


def solution(mesh):
    counts = (mesh.shape["sky"], mesh.shape["visit"], mesh.shape["patch"])
    filters = filter_bank()

    def body(template_store, science, owner_visit, stamp_offset):
        return fused(owner_visit, stamp_offset, template_store, science, filters, counts)[None]

    spec = P("visit", "patch", "sky")
    in_specs = (spec, spec, P("sky", "patch"), P(None, "visit", "patch", "sky"))
    return jax.shard_map(body, mesh=mesh, in_specs=in_specs, out_specs=spec, check_vma=False)
```

```python
import numpy as np
import jax
import jax.numpy as jnp
from jax import lax
from jax.experimental import pallas as pl
from jax.experimental.pallas import tpu as pltpu
from jax.sharding import PartitionSpec as P

HALF = 15
TAPS = 2 * HALF + 1
ORDERS = 5
NBASIS = 25
CELL = 64
STAMP = 32
ROWS = 64
PAD = 16
LANES = 128
PIECES = 2
APART = ORDERS * STAMP + 1
SIGMA = 5.0
MESH = pl.DeviceIdType.MESH
F32 = jnp.float32
BF16 = jnp.bfloat16


def filter_bank():
    x = (np.arange(TAPS) - HALF) / SIGMA
    env = np.exp(-0.5 * x * x)
    poly = [
        np.ones_like(x),
        2.0 * x,
        4.0 * x**2 - 2.0,
        8.0 * x**3 - 12.0 * x,
        16.0 * x**4 - 48.0 * x**2 + 12.0,
    ]
    shaped = np.stack(poly) * env[None]
    return shaped / np.sqrt(np.sum(shaped * shaped, axis=1, keepdims=True))


def taps_at(filters, index):
    inside = (index >= 0) & (index < TAPS)
    return np.where(inside[None], filters[:, np.clip(index, 0, TAPS - 1)], 0.0)


def two_parts(values):
    values = np.asarray(values, np.float32)
    high = values.astype(BF16)
    return high, (values - high.astype(np.float32)).astype(BF16)


def halves(values):
    return [jnp.asarray(np.stack(two_parts(values)))]


def stacked_halves(values, axis):
    high, low = two_parts(values)
    return [jnp.asarray(np.concatenate([high, high, low, low], axis=axis))]


def constants(filters, cells):
    width = cells * CELL
    stamp_rows = taps_at(filters, np.arange(CELL)[None, :] - np.arange(STAMP)[:, None])
    stamp_rows = stamp_rows.reshape(ORDERS * STAMP, CELL)
    stamp_cols = taps_at(filters, np.arange(CELL)[:, None] - np.arange(STAMP)[None, :])
    high, low = [np.asarray(part, np.float32) for part in two_parts(stamp_cols)]
    placed = np.zeros((4 * 3 * CELL, ORDERS, 4, STAMP), np.float32)
    for m in range(4):
        for part in range(2):
            at = 2 * CELL * m + CELL * part
            placed[at : at + CELL, :, m, :] = np.transpose(high, (1, 0, 2))
        at = 8 * CELL + CELL * m
        placed[at : at + CELL, :, m, :] = np.transpose(low, (1, 0, 2))
    placed = placed.reshape(-1, ORDERS * LANES)
    full_cols = taps_at(filters, np.arange(2 * LANES)[:, None] - np.arange(LANES)[None, :] - 1)
    full_cols = np.transpose(full_cols, (1, 0, 2)).reshape(2 * LANES, ORDERS * LANES)
    high, low = two_parts(full_cols)
    full_rows = taps_at(filters, np.arange(ROWS + 2 * PAD)[None, :] - np.arange(ROWS)[:, None] - 1)
    full_rows = np.transpose(full_rows, (1, 0, 2)).reshape(ROWS, ORDERS * (ROWS + 2 * PAD))
    lane = np.arange(LANES)[:, None]
    cell_lane = (lane % cells == np.arange(width)[None, :] // CELL) & (lane < 3 * cells)
    return (
        stacked_halves(stamp_rows, 1)
        + [jnp.asarray(placed, BF16)]
        + [jnp.asarray(np.concatenate([high, high, low], axis=0))]
        + halves(full_rows)
        + [jnp.asarray(cell_lane, BF16)]
    )


def dot(a, b):
    return jnp.dot(a, b, preferred_element_type=F32)


def split2(x):
    high = x.astype(BF16)
    return high, (x - high.astype(F32)).astype(BF16)


def split3(x):
    high = x.astype(BF16)
    rest = x - high.astype(F32)
    mid = rest.astype(BF16)
    return high, mid, (rest - mid.astype(F32)).astype(BF16)


def eliminate(rows, flux):
    count = len(rows)
    starts = [8 * (k // 8) for k in range(count)]
    for j in range(count):
        first = 8 * (j // 8)
        for i in range(j):
            if starts[i] < first:
                rows[i] = rows[i][first - starts[i] :]
                starts[i] = first
        pivot_row = rows[j]
        scaled = pivot_row * (1.0 / pivot_row[j - first : j - first + 1])
        for i in range(count):
            if i < j:
                rows[i] = rows[i] - rows[i][j - first : j - first + 1] * scaled
            elif i > j:
                factor = pivot_row[i - first : i - first + 1]
                rows[i] = rows[i] - factor * scaled[starts[i] - first :]
        rows[j] = scaled
    weights = jnp.concatenate([row[1:2] for row in rows] + [jnp.zeros((7, LANES), F32)], axis=0)
    unit = jnp.concatenate([row[2:3] for row in rows] + [jnp.zeros((7, LANES), F32)], axis=0)
    return weights, unit


def fused_kernel(
    counts, flux, owner_hbm, offset_hbm, slot_hbm, image_hbm,
    srow_hbm, scol_hbm, fcol_hbm, frow_hbm, put_hbm,
    out_ref,
    owner_ref, offset_ref, slot_ref, image_ref, srow, scol, fcol, frow, cell_lane,
    ext, landed, edge, edge_landed, shifted, image_rows, image_stamps, filtered, combined_h, combined_l, sum_ref, sum_landed,
    local_sem, ready, go, rs_send, rs_recv, ag_send, ag_recv, row_recv, edge_send, edge_recv, flux_sem,
):
    sky_count, visits, patches = counts
    members = sky_count * patches
    sky = lax.axis_index("sky")
    visit = lax.axis_index("visit")
    patch = lax.axis_index("patch")
    me = sky * patches + patch
    width = image_ref.shape[1]
    cells = width // CELL
    full = width + 2 * LANES
    ext_rows = ROWS + 2 * PAD
    first_reducer = visits // 2 - 1
    half = width // 2
    piece = half // PIECES
    side = visit - first_reducer
    reduces = (side == 0) | (side == 1)
    outward = 2 * side - 1
    hub = (sky == sky_count - 1) & (patch == 0)

    def inside(ds):
        return (sky + ds >= 0) & (sky + ds < sky_count)

    def there(ds, other, v):
        return {
            "sky": jnp.clip(sky + ds, 0, sky_count - 1),
            "visit": v,
            "patch": 1 - patch if other else patch,
        }

    def member(d):
        other = lax.rem(me + d, members)
        return {"sky": other // patches, "patch": lax.rem(other, patches)}

    def rows_of(t):
        return pl.multiple_of(lax.rem(t + 1 - patch, 2) * (ROWS // 2), 8)

    def columns_of(i, j):
        at = i * half + (j + i * (PIECES - 1 - 2 * j)) * piece
        return at if isinstance(at, int) else pl.multiple_of(at, LANES)

    def signal(semaphore, where):
        pl.semaphore_signal(semaphore, inc=1, device_id=where, device_id_type=MESH)

    moves = [
        (owner_hbm, owner_ref),
        (offset_hbm, offset_ref),
        (image_hbm.at[0], image_ref),
        (slot_hbm.at[0], slot_ref),
        (srow_hbm, srow),
        (scol_hbm, scol),
        (fcol_hbm, fcol),
        (frow_hbm, frow),
        (put_hbm, cell_lane),
    ]
    loads = [pltpu.make_async_copy(src, dst, local_sem.at[i]) for i, (src, dst) in enumerate(moves)]

    ext[0:PAD, :] = jnp.zeros((PAD, full), F32)
    ext[PAD + ROWS :, :] = jnp.zeros((PAD + 8, full), F32)
    ext[PAD : PAD + ROWS, 0:LANES] = jnp.zeros((ROWS, LANES), F32)
    ext[PAD : PAD + ROWS, full - LANES :] = jnp.zeros((ROWS, LANES), F32)

    barrier = pltpu.get_barrier_semaphore()

    @pl.when(reduces)
    def _():
        for ds in (0, -1, 1):

            @pl.when(inside(ds))
            def _():
                for other in (0, 1):
                    for to in range(visits):
                        if ds == 0 and not other:

                            @pl.when(visit != to)
                            def _():
                                signal(barrier, there(ds, other, to))

                        else:
                            signal(barrier, there(ds, other, to))

    @pl.when(jnp.logical_not(hub))
    def _():
        signal(barrier, {"sky": sky_count - 1, "patch": 0})

    around = patches * (1 + inside(-1).astype(jnp.int32) + inside(1).astype(jnp.int32))
    alone = reduces.astype(jnp.int32)
    pl.semaphore_wait(barrier, 2 * around - alone + jnp.where(hub, members - 1, 0))

    def scatter(i, n):
        start = columns_of(i, n // 2)
        rows = pl.ds(rows_of(n % 2), ROWS // 2)
        return pltpu.make_async_remote_copy(
            src_ref=slot_hbm.at[0, rows, pl.ds(start, piece)],
            dst_ref=landed.at[visit, rows, pl.ds(start - i * half, piece)],
            send_sem=rs_send,
            recv_sem=rs_recv.at[n],
            device_id={"visit": first_reducer + i},
            device_id_type=MESH,
        )

    for n in range(2 * PIECES):
        for i in range(2):

            @pl.when(side != i)
            def _():
                scatter(i, n).start()

    for load in loads:
        load.start()

    for ds in (0, -1, 1):

        @pl.when(inside(ds))
        def _():
            for other in (0, 1):
                for i in range(2):
                    if ds == 0 and not other:

                        @pl.when(side != i)
                        def _():
                            signal(ready, there(ds, other, first_reducer + i))

                    else:
                        signal(ready, there(ds, other, first_reducer + i))

    @pl.when(hub)
    def _():
        for d in range(1, members):
            signal(go, member(d))

    for load in loads[:4]:
        load.wait()
    lane = lax.broadcasted_iota(jnp.int32, (STAMP, LANES), 1)
    for g in range(cells):
        first = LANES * (g // 2)
        block = image_ref[:, first : first + LANES]
        block = pltpu.roll(block, lax.rem(ROWS - offset_ref[0, 0, 0, g], ROWS), 0)[0:STAMP]
        block = pltpu.roll(block, lax.rem(2 * LANES - CELL * (g % 2) - offset_ref[1, 0, 0, g], LANES), 1)
        block = jnp.where(lane < STAMP, block, pltpu.roll(block, STAMP, 1))
        block = jnp.where(lane < 2 * STAMP, block, pltpu.roll(block, 2 * STAMP, 1))
        image_rows[STAMP * g : STAMP * (g + 1), :] = block
    group8 = lax.broadcasted_iota(jnp.int32, (cells, LANES), 1) // STAMP
    for j in range(STAMP // 4):
        merged = image_rows[pl.ds(4 * j, cells, stride=STAMP), :]
        for m in range(1, 4):
            merged = jnp.where(group8 == m, image_rows[pl.ds(4 * j + m, cells, stride=STAMP), :], merged)
        image_stamps[:, LANES * j : LANES * (j + 1)] = merged

    owner = owner_ref[0, 0]
    lane8 = lax.broadcasted_iota(jnp.int32, (8, LANES), 1) // PAD

    def await_bytes(ref, semaphore):
        pltpu.make_async_copy(ref, ref, semaphore).wait()

    def own_copy(n, to):
        at = pl.ds(LANES + columns_of(side, n // 2), piece)
        spot = ext.at[pl.ds(pl.multiple_of(PAD + rows_of(n % 2), 8), ROWS // 2), at]
        return pltpu.make_async_remote_copy(
            src_ref=spot,
            dst_ref=spot,
            send_sem=ag_send,
            recv_sem=ag_recv.at[side],
            device_id={"visit": to},
            device_id_type=MESH,
        )

    def row_copy(j, to):
        at = pl.ds(LANES + columns_of(side, j), piece)
        return pltpu.make_async_remote_copy(
            src_ref=ext.at[pl.ds(pl.multiple_of(ROWS - (ROWS - PAD) * patch, 8), PAD), at],
            dst_ref=ext.at[pl.ds(pl.multiple_of((PAD + ROWS) * patch, 8), PAD), at],
            send_sem=ag_send,
            recv_sem=row_recv,
            device_id=there(0, 1, to),
            device_id_type=MESH,
        )

    def edge_copy(to, other):
        return pltpu.make_async_remote_copy(
            src_ref=edge,
            dst_ref=edge_landed.at[side, other],
            send_sem=edge_send,
            recv_sem=edge_recv.at[side],
            device_id=there(outward, other, to),
            device_id_type=MESH,
        )

    def spread_piece(n, to):
        @pl.when(visit != to)
        def _():
            own_copy(n, to).start()

        if n % 2 == 0:
            row_copy(n // 2, to).start()
        if n == 1:

            @pl.when(inside(outward))
            def _():
                for other in (0, 1):
                    edge_copy(to, other).start()

    @pl.when(reduces)
    def _():
        pl.semaphore_wait(ready, around * visits - 1)
        for n in range(2 * PIECES):
            start = columns_of(side, n // 2)
            rows = pl.ds(rows_of(n % 2), ROWS // 2)
            spot = pl.ds(pl.multiple_of(start - side * half, LANES), piece)
            await_bytes(landed.at[pl.ds(0, visits - 1), rows, spot], rs_recv.at[n])
            current = slot_ref[rows, pl.ds(start, piece)]
            for d in range(1, visits):
                source = lax.rem(visit + visits - d, visits)
                current = jnp.where(owner == source, landed[source, rows, spot], current)
            at = pl.ds(LANES + start, piece)
            ext[pl.ds(pl.multiple_of(PAD + rows_of(n % 2), 8), ROWS // 2), at] = current
            if n == 1:
                merged = jnp.zeros((8, LANES), F32)
                for r in range(ROWS // 8):
                    block = ext[PAD + 8 * r : PAD + 8 * r + 8, at]
                    left = pltpu.roll(block[:, 0:LANES], (PAD * r) % LANES, 1)
                    right = pltpu.roll(block[:, piece - LANES :], (PAD * (r + 1)) % LANES, 1)
                    merged = jnp.where(lane8 == r, jnp.where(side == 0, left, right), merged)
                edge[...] = merged
            spread_piece(n, 0)
        for to in range(1, visits):
            for n in range(2 * PIECES):
                spread_piece(n, to)

    for load in loads[4:]:
        load.wait()
    for i in range(2):

        @pl.when(side != i)
        def _():
            await_bytes(ext.at[pl.ds(PAD, ROWS), pl.ds(LANES, half)], ag_recv.at[i])

    await_bytes(ext.at[pl.ds(0, PAD), pl.ds(LANES, width)], row_recv)
    for i in range(2):

        @pl.when(inside(1 - 2 * i))
        def _():
            await_bytes(edge_landed.at[i], edge_recv.at[i])
            first, base = (full - LANES, 0) if i == 0 else (0, LANES - PAD)
            packed = edge_landed[i, 0]
            for r in range(ROWS // 8):
                moved = pltpu.roll(packed, (base - PAD * r) % LANES, 1)
                ext[PAD + 8 * r : PAD + 8 * r + 8, first : first + LANES] = moved
            packed = pltpu.roll(edge_landed[i, 1], lax.rem(base + LANES - (LANES - 2 * PAD) * patch, LANES), 1)
            row = pl.multiple_of((PAD + ROWS) * (1 - patch), 8)
            ext[pl.ds(row, 8), first : first + LANES] = packed
            ext[pl.ds(row + 8, 8), first : first + LANES] = pltpu.roll(packed, LANES - PAD, 1)

    shifted[...] = pltpu.roll(ext[...], full - (LANES - PAD), 1)
    tall = ext_rows + 8
    tall_lane = lax.broadcasted_iota(jnp.int32, (tall, LANES), 1)
    lane = lax.broadcasted_iota(jnp.int32, (CELL, LANES), 1)
    windows = []
    for g in range(cells):
        first = LANES * (g // 2)
        block = shifted[:, first : first + LANES]
        if g % 2:
            block = jnp.where(tall_lane < CELL, shifted[:, first + LANES : first + 2 * LANES], block)
        block = pltpu.roll(block, tall - 1 - offset_ref[0, 0, 0, g], 0)[0:CELL]
        move = 2 * LANES - 1 - CELL * (g % 2) - offset_ref[1, 0, 0, g]
        block = pltpu.roll(block, lax.rem(move, LANES), 1)
        windows.append(jnp.where(lane < CELL, block, pltpu.roll(block, CELL, 1)))
    high, low = split2(jnp.concatenate(windows, axis=1))
    rows_done = dot(srow[...], jnp.concatenate([high, low, high, low], axis=0))
    count = ORDERS * STAMP
    for g in range(cells):
        filtered[APART * g : APART * g + count, :] = rows_done[:, LANES * g : LANES * (g + 1)]
    lane = lax.broadcasted_iota(jnp.int32, (cells * count // 4, LANES), 1)
    parts, tops = [], []
    for m in range(4):
        by_cell = jnp.concatenate([filtered[pl.ds(r, cells, stride=APART), :] for r in range(m, count, 4)], axis=0)
        top = by_cell.astype(BF16).astype(F32)
        parts.append(jnp.where(lane < CELL, top, by_cell - top).astype(BF16))
        tops.append(top)
    for m in (0, 2):
        parts.append(jnp.where(lane < CELL, tops[m], tops[m + 1]).astype(BF16))
    basis = dot(jnp.concatenate(parts, axis=1), scol[...])
    filled = [basis[:, LANES * a : LANES * (a + 1)].reshape(count // 4, cells, LANES) for a in range(ORDERS)]
    eighth = STAMP // 4
    flat = [
        jnp.concatenate([filled[a][eighth * b + j] for j in range(eighth)], axis=1)
        for a in range(ORDERS)
        for b in range(ORDERS)
    ]
    high, low = split2(jnp.concatenate(flat + [image_stamps[...]], axis=0))
    used = cells * (NBASIS + 1)
    spare = jnp.zeros((2 * LANES - used, STAMP * STAMP), BF16)
    across = (((1,), (1,)), ((), ()))
    high_all, low_all = jnp.concatenate([high, spare], axis=0), jnp.concatenate([low, spare], axis=0)
    gram = lax.dot_general(jnp.concatenate([high, low], axis=0), high_all, across, preferred_element_type=F32)
    gram = gram[:used] + gram[used:] + lax.dot_general(high, low_all, across, preferred_element_type=F32)
    gram = gram.reshape(NBASIS + 1, cells, 2 * LANES)
    same = lax.rem(lax.broadcasted_iota(jnp.int32, gram.shape, 2), cells) == lax.broadcasted_iota(jnp.int32, gram.shape, 1)
    sums = jnp.sum(jnp.where(same, gram, 0.0), axis=1)
    sums = jnp.concatenate([sums, jnp.zeros((32 - NBASIS - 1, 2 * LANES), F32)], axis=0)
    padding = lax.broadcasted_iota(jnp.int32, (1, LANES), 1) >= cells
    diag = []
    for k in range(NBASIS):
        low = 8 * (k // 8)
        tile, at = divmod(cells * k, LANES)
        row = sums[low:, LANES * tile : LANES * (tile + 1)]
        row = pltpu.roll(row, LANES - at, 1) if at else row
        place = lax.broadcasted_iota(jnp.int32, row.shape, 0) + low
        diag.append(jnp.where(place == NBASIS + 1, float(flux[k]), row))
    weights, unit = eliminate(diag, flux)
    weights = jnp.where(padding, 0.0, weights)
    unit = jnp.where(padding, 0.0, unit)

    flux_col = jnp.concatenate([jnp.full((1, LANES), float(f), F32) for f in flux] + [jnp.zeros((7, LANES), F32)], axis=0)
    flux_cells = jnp.sum(weights * flux_col, axis=0, keepdims=True)
    curve_cells = jnp.sum(unit * flux_col, axis=0, keepdims=True)
    local = jnp.sum(flux_cells, axis=1, keepdims=True)
    sum_ref[...] = jnp.broadcast_to(local, (8, LANES))
    @pl.when(jnp.logical_not(hub))
    def _():
        pl.semaphore_wait(go, 1)

    for d in range(1, members):
        pltpu.make_async_remote_copy(
            src_ref=sum_ref,
            dst_ref=sum_landed.at[d - 1],
            send_sem=flux_sem.at[0],
            recv_sem=flux_sem.at[1],
            device_id=member(d),
            device_id_type=MESH,
        ).start()

    both = jnp.concatenate([flux_cells, curve_cells, jnp.zeros((6, LANES), F32)], axis=0)
    high, mid, low = [part.astype(F32) for part in split3(jnp.concatenate([weights, unit, both], axis=0))]
    lane = lax.broadcasted_iota(jnp.int32, high.shape, 1)
    low = jnp.where(lane < 2 * cells, pltpu.roll(mid, cells, 1), pltpu.roll(low, 2 * cells, 1))
    spread = dot(jnp.where(lane < cells, high, low).astype(BF16), cell_lane[...])
    blocks = width // LANES
    high, low = split2(shifted[0:ext_rows, :])
    windows = [
        jnp.concatenate([part[:, LANES * h : LANES * h + 2 * LANES] for h in range(blocks)], axis=0) for part in (high, low)
    ]
    columns = dot(jnp.concatenate(windows + windows[:1], axis=1), fcol[...])
    for which in range(2):
        for h in range(blocks):
            for b in range(ORDERS):
                acc = None
                for a in range(ORDERS):
                    k = 32 * which + ORDERS * a + b
                    term = spread[k : k + 1, LANES * h : LANES * (h + 1)] * columns[
                        ext_rows * h : ext_rows * (h + 1), LANES * a : LANES * (a + 1)
                    ]
                    acc = term if acc is None else acc + term
                high, low = split2(acc)
                spot = (slice(ext_rows * b, ext_rows * (b + 1)), slice(width * which + LANES * h, width * which + LANES * (h + 1)))
                combined_h[spot] = high
                combined_l[spot] = low
    matched = dot(frow[...].reshape(2 * ROWS, -1), combined_h[...])
    matched = matched[:ROWS] + (matched[ROWS:] + dot(frow[0], combined_l[...]))
    total = sum_ref[...]
    await_bytes(sum_landed, flux_sem.at[1])
    for d in range(1, members):
        total = total + sum_landed[d - 1]
    mean_flux = total[0:1, 0:1] * (1.0 / (cells * members))
    correction = (mean_flux - spread[64:65]) / spread[65:66]
    out_ref[...] = image_ref[...] - matched[:, 0:width] - correction * matched[:, width:]
    await_bytes(sum_landed, flux_sem.at[0])

    @pl.when(reduces)
    def _():
        await_bytes(landed.at[0], rs_send)
        await_bytes(landed, ag_send)

        @pl.when(inside(outward))
        def _():
            await_bytes(landed.at[0, pl.ds(0, 2 * 8 * visits * LANES // half)], edge_send)

    @pl.when(jnp.logical_not(reduces))
    def _():
        await_bytes(slot_ref, rs_send)


def fused(owner, offsets, slot, image, filters, counts):
    width = image.shape[2]
    cells = width // CELL
    visits = counts[1]
    members = counts[0] * counts[2]
    sums = filters.sum(axis=1)
    flux = (sums[:, None] * sums[None, :]).reshape(-1)
    consts = constants(filters, cells)
    deep = ORDERS * (ROWS + 2 * PAD)
    full = width + 2 * LANES
    dma = pltpu.SemaphoreType.DMA
    hbm = pl.BlockSpec(memory_space=pltpu.HBM)
    return pl.pallas_call(
        lambda *refs: fused_kernel(counts, flux, *refs),
        name="difference_patch",
        out_shape=jax.ShapeDtypeStruct((ROWS, width), F32),
        in_specs=[hbm] * (4 + len(consts)),
        out_specs=pl.BlockSpec(memory_space=pltpu.VMEM),
        scratch_shapes=[
            pltpu.SMEM(owner.shape, jnp.int32),
            pltpu.SMEM(offsets.shape, jnp.int32),
            pltpu.VMEM((ROWS, width), F32),
            pltpu.VMEM((ROWS, width), F32),
        ]
        + [pltpu.VMEM(const.shape, const.dtype) for const in consts]
        + [
            pltpu.VMEM((ROWS + 2 * PAD + 8, full), F32),
            pltpu.VMEM((visits, ROWS, width // 2), F32),
            pltpu.VMEM((8, LANES), F32),
            pltpu.VMEM((2, 2, 8, LANES), F32),
            pltpu.VMEM((ROWS + 2 * PAD + 8, full), F32),
            pltpu.VMEM((cells * STAMP, LANES), F32),
            pltpu.VMEM((cells, STAMP * STAMP), F32),
            pltpu.VMEM((cells * (APART + 1), LANES), F32),
            pltpu.VMEM((deep, 2 * width), BF16),
            pltpu.VMEM((deep, 2 * width), BF16),
            pltpu.VMEM((8, LANES), F32),
            pltpu.VMEM((members - 1, 8, LANES), F32),
            dma((9,)),
            pltpu.SemaphoreType.REGULAR,
            pltpu.SemaphoreType.REGULAR,
            dma,
            dma((2 * PIECES,)),
            dma,
            dma((2,)),
            dma,
            dma,
            dma((2,)),
            dma((2,)),
        ],
        compiler_params=pltpu.CompilerParams(
            collective_id=0, has_side_effects=True, vmem_limit_bytes=40 << 20
        ),
    )(owner, *[pltpu.with_memory_space_constraint(v, pltpu.HBM) for v in (offsets, slot, image, *consts)])


def solution(mesh):
    counts = (mesh.shape["sky"], mesh.shape["visit"], mesh.shape["patch"])
    filters = filter_bank()

    def body(template_store, science, owner_visit, stamp_offset):
        return fused(owner_visit, stamp_offset, template_store, science, filters, counts)[None]

    spec = P("visit", "patch", "sky")
    in_specs = (spec, spec, P("sky", "patch"), P(None, "visit", "patch", "sky"))
    return jax.shard_map(body, mesh=mesh, in_specs=in_specs, out_specs=spec, check_vma=False)
```

```python
import numpy as np
import jax
import jax.numpy as jnp
from jax import lax
from jax.experimental import pallas as pl
from jax.experimental.pallas import tpu as pltpu
from jax.sharding import PartitionSpec as P

HALF = 15
TAPS = 2 * HALF + 1
ORDERS = 5
NBASIS = 25
CELL = 64
STAMP = 32
ROWS = 64
PAD = 16
LANES = 128
PIECES = 2
INNER = 2
APART = ORDERS * STAMP + 1
SIGMA = 5.0
MESH = pl.DeviceIdType.MESH
F32 = jnp.float32
BF16 = jnp.bfloat16


def filter_bank():
    x = (np.arange(TAPS) - HALF) / SIGMA
    env = np.exp(-0.5 * x * x)
    poly = [
        np.ones_like(x),
        2.0 * x,
        4.0 * x**2 - 2.0,
        8.0 * x**3 - 12.0 * x,
        16.0 * x**4 - 48.0 * x**2 + 12.0,
    ]
    shaped = np.stack(poly) * env[None]
    return shaped / np.sqrt(np.sum(shaped * shaped, axis=1, keepdims=True))


def taps_at(filters, index):
    inside = (index >= 0) & (index < TAPS)
    return np.where(inside[None], filters[:, np.clip(index, 0, TAPS - 1)], 0.0)


def two_parts(values):
    values = np.asarray(values, np.float32)
    high = values.astype(BF16)
    return high, (values - high.astype(np.float32)).astype(BF16)


def halves(values):
    return [jnp.asarray(np.stack(two_parts(values)))]


def stacked_halves(values, axis):
    high, low = two_parts(values)
    return [jnp.asarray(np.concatenate([high, high, low, low], axis=axis))]


def constants(filters, cells):
    width = cells * CELL
    stamp_rows = taps_at(filters, np.arange(CELL)[None, :] - np.arange(STAMP)[:, None])
    stamp_rows = stamp_rows.reshape(ORDERS * STAMP, CELL)
    stamp_cols = taps_at(filters, np.arange(CELL)[:, None] - np.arange(STAMP)[None, :])
    high, low = [np.asarray(part, np.float32) for part in two_parts(stamp_cols)]
    placed = np.zeros((4 * 3 * CELL, ORDERS, 4, STAMP), np.float32)
    for m in range(4):
        for part in range(2):
            at = 2 * CELL * m + CELL * part
            placed[at : at + CELL, :, m, :] = np.transpose(high, (1, 0, 2))
        at = 8 * CELL + CELL * m
        placed[at : at + CELL, :, m, :] = np.transpose(low, (1, 0, 2))
    placed = placed.reshape(-1, ORDERS * LANES)
    full_cols = taps_at(filters, np.arange(2 * LANES)[:, None] - np.arange(LANES)[None, :] - 1)
    full_cols = np.transpose(full_cols, (1, 0, 2)).reshape(2 * LANES, ORDERS * LANES)
    high, low = two_parts(full_cols)
    full_rows = taps_at(filters, np.arange(ROWS + 2 * PAD)[None, :] - np.arange(ROWS)[:, None] - 1)
    full_rows = np.transpose(full_rows, (1, 0, 2)).reshape(ROWS, ORDERS * (ROWS + 2 * PAD))
    lane = np.arange(LANES)[:, None]
    cell_lane = (lane % cells == np.arange(width)[None, :] // CELL) & (lane < 3 * cells)
    return (
        stacked_halves(stamp_rows, 1)
        + [jnp.asarray(placed, BF16)]
        + [jnp.asarray(np.concatenate([high, high, low], axis=0))]
        + halves(full_rows)
        + [jnp.asarray(cell_lane, BF16)]
    )


def dot(a, b):
    return jnp.dot(a, b, preferred_element_type=F32)


def split2(x):
    high = x.astype(BF16)
    return high, (x - high.astype(F32)).astype(BF16)


def split3(x):
    high = x.astype(BF16)
    rest = x - high.astype(F32)
    mid = rest.astype(BF16)
    return high, mid, (rest - mid.astype(F32)).astype(BF16)


def eliminate(rows, flux):
    count = len(rows)
    starts = [8 * (k // 8) for k in range(count)]
    for j in range(count):
        first = 8 * (j // 8)
        for i in range(j):
            if starts[i] < first:
                rows[i] = rows[i][first - starts[i] :]
                starts[i] = first
        pivot_row = rows[j]
        scaled = pivot_row * (1.0 / pivot_row[j - first : j - first + 1])
        for i in range(count):
            if i < j:
                rows[i] = rows[i] - rows[i][j - first : j - first + 1] * scaled
            elif i > j:
                factor = pivot_row[i - first : i - first + 1]
                rows[i] = rows[i] - factor * scaled[starts[i] - first :]
        rows[j] = scaled
    weights = jnp.concatenate([row[1:2] for row in rows] + [jnp.zeros((7, LANES), F32)], axis=0)
    unit = jnp.concatenate([row[2:3] for row in rows] + [jnp.zeros((7, LANES), F32)], axis=0)
    return weights, unit


def fused_kernel(
    counts, flux, owner_hbm, offset_hbm, slot_hbm, image_hbm,
    srow_hbm, scol_hbm, fcol_hbm, frow_hbm, put_hbm,
    out_ref,
    owner_ref, offset_ref, slot_ref, image_ref, srow, scol, fcol, frow, cell_lane,
    ext, landed, edge, edge_landed, shifted, image_rows, image_stamps, filtered, combined_h, combined_l, sum_ref, sum_landed,
    local_sem, ready, go, rs_send, rs_recv, ag_send, ag_recv, row_send, row_recv, edge_send, edge_recv, flux_sem,
):
    sky_count, visits, patches = counts
    members = sky_count * patches
    sky = lax.axis_index("sky")
    visit = lax.axis_index("visit")
    patch = lax.axis_index("patch")
    me = sky * patches + patch
    width = image_ref.shape[1]
    cells = width // CELL
    full = width + 2 * LANES
    ext_rows = ROWS + 2 * PAD
    first_reducer = visits // 2 - 1
    half = width // 2
    piece = half // PIECES
    side = visit - first_reducer
    middle = (side == 0) | (side == 1)
    origin = visit == 0
    reduces = middle | origin
    reducers = (0, first_reducer, first_reducer + 1)
    outward = 2 * side - 1
    hub = (sky == sky_count - 1) & (patch == 0)

    def inside(ds):
        return (sky + ds >= 0) & (sky + ds < sky_count)

    def there(ds, other, v):
        return {
            "sky": jnp.clip(sky + ds, 0, sky_count - 1),
            "visit": v,
            "patch": 1 - patch if other else patch,
        }

    def member(d):
        other = lax.rem(me + d, members)
        return {"sky": other // patches, "patch": lax.rem(other, patches)}

    def rows_of(t):
        return pl.multiple_of(lax.rem(t + 1 - patch, 2) * (ROWS // 2), 8)

    def columns_of(i, j):
        at = i * half + (j + i * (PIECES - 1 - 2 * j)) * piece
        return at if isinstance(at, int) else pl.multiple_of(at, LANES)

    def signal(semaphore, where):
        pl.semaphore_signal(semaphore, inc=1, device_id=where, device_id_type=MESH)

    moves = [
        (owner_hbm, owner_ref),
        (offset_hbm, offset_ref),
        (image_hbm.at[0], image_ref),
        (slot_hbm.at[0], slot_ref),
        (srow_hbm, srow),
        (scol_hbm, scol),
        (fcol_hbm, fcol),
        (frow_hbm, frow),
        (put_hbm, cell_lane),
    ]
    loads = [pltpu.make_async_copy(src, dst, local_sem.at[i]) for i, (src, dst) in enumerate(moves)]

    ext[0:PAD, :] = jnp.zeros((PAD, full), F32)
    ext[PAD + ROWS :, :] = jnp.zeros((PAD + 8, full), F32)
    ext[PAD : PAD + ROWS, 0:LANES] = jnp.zeros((ROWS, LANES), F32)
    ext[PAD : PAD + ROWS, full - LANES :] = jnp.zeros((ROWS, LANES), F32)

    barrier = pltpu.get_barrier_semaphore()

    @pl.when(reduces)
    def _():
        for ds in (0, -1, 1):

            @pl.when(inside(ds))
            def _():
                for other in (0, 1):
                    for to in range(visits):
                        if ds == 0 and not other:

                            @pl.when(visit != to)
                            def _():
                                signal(barrier, there(ds, other, to))

                        else:
                            signal(barrier, there(ds, other, to))

    @pl.when(jnp.logical_not(hub))
    def _():
        signal(barrier, {"sky": sky_count - 1, "patch": 0})

    around = patches * (1 + inside(-1).astype(jnp.int32) + inside(1).astype(jnp.int32))
    alone = reduces.astype(jnp.int32)
    pl.semaphore_wait(barrier, len(reducers) * around - alone + jnp.where(hub, members - 1, 0))

    def scatter(i, n):
        start = columns_of(i, n // 2)
        rows = pl.ds(rows_of(n % 2), ROWS // 2)
        inner = n == INNER
        return pltpu.make_async_remote_copy(
            src_ref=slot_hbm.at[0, rows, pl.ds(start, piece)],
            dst_ref=landed.at[visit, rows, pl.ds(i * piece if inner else start - i * half, piece)],
            send_sem=rs_send,
            recv_sem=rs_recv.at[n],
            device_id={"visit": 0 if inner else first_reducer + i},
            device_id_type=MESH,
        )

    for n in (0, 1, 3, INNER):
        for i in range(2):

            @pl.when(jnp.logical_not(origin) if n == INNER else side != i)
            def _():
                scatter(i, n).start()

    for load in loads:
        load.start()

    for ds in (0, -1, 1):

        @pl.when(inside(ds))
        def _():
            for other in (0, 1):
                for to in reducers:
                    if ds == 0 and not other:

                        @pl.when(visit != to)
                        def _():
                            signal(ready, there(ds, other, to))

                    else:
                        signal(ready, there(ds, other, to))

    @pl.when(hub)
    def _():
        for d in range(1, members):
            signal(go, member(d))

    for load in loads[:4]:
        load.wait()
    lane = lax.broadcasted_iota(jnp.int32, (STAMP, LANES), 1)
    for g in range(cells):
        first = LANES * (g // 2)
        block = image_ref[:, first : first + LANES]
        block = pltpu.roll(block, lax.rem(ROWS - offset_ref[0, 0, 0, g], ROWS), 0)[0:STAMP]
        block = pltpu.roll(block, lax.rem(2 * LANES - CELL * (g % 2) - offset_ref[1, 0, 0, g], LANES), 1)
        block = jnp.where(lane < STAMP, block, pltpu.roll(block, STAMP, 1))
        block = jnp.where(lane < 2 * STAMP, block, pltpu.roll(block, 2 * STAMP, 1))
        image_rows[STAMP * g : STAMP * (g + 1), :] = block
    group8 = lax.broadcasted_iota(jnp.int32, (cells, LANES), 1) // STAMP
    for j in range(STAMP // 4):
        merged = image_rows[pl.ds(4 * j, cells, stride=STAMP), :]
        for m in range(1, 4):
            merged = jnp.where(group8 == m, image_rows[pl.ds(4 * j + m, cells, stride=STAMP), :], merged)
        image_stamps[:, LANES * j : LANES * (j + 1)] = merged

    owner = owner_ref[0, 0]
    lane8 = lax.broadcasted_iota(jnp.int32, (8, LANES), 1) // PAD

    def await_bytes(ref, semaphore):
        pltpu.make_async_copy(ref, ref, semaphore).wait()

    def own_copy(n, to):
        at = pl.ds(LANES + half - piece, 2 * piece) if n == INNER else pl.ds(LANES + columns_of(side, n // 2), piece)
        spot = ext.at[pl.ds(pl.multiple_of(PAD + rows_of(n % 2), 8), ROWS // 2), at]
        return pltpu.make_async_remote_copy(
            src_ref=spot,
            dst_ref=spot,
            send_sem=ag_send,
            recv_sem=ag_recv.at[2 if n == INNER else side],
            device_id={"visit": to},
            device_id_type=MESH,
        )

    def row_copy(n, to):
        at = pl.ds(LANES + half - piece, 2 * piece) if n == INNER else pl.ds(LANES + columns_of(side, 0), piece)
        return pltpu.make_async_remote_copy(
            src_ref=ext.at[pl.ds(pl.multiple_of(ROWS - (ROWS - PAD) * patch, 8), PAD), at],
            dst_ref=ext.at[pl.ds(pl.multiple_of((PAD + ROWS) * patch, 8), PAD), at],
            send_sem=row_send,
            recv_sem=row_recv,
            device_id=there(0, 1, to),
            device_id_type=MESH,
        )

    def edge_copy(to, other):
        return pltpu.make_async_remote_copy(
            src_ref=edge,
            dst_ref=edge_landed.at[side, other],
            send_sem=edge_send,
            recv_sem=edge_recv.at[side],
            device_id=there(outward, other, to),
            device_id_type=MESH,
        )

    def spread_piece(n, to):
        if n == 1:

            @pl.when(inside(outward))
            def _():
                for other in (1, 0):
                    edge_copy(to, other).start()

        if n % 2 == 0:
            row_copy(n, to).start()

        @pl.when(visit != to)
        def _():
            own_copy(n, to).start()

    def chosen(rows, at, spot):
        current = slot_ref[rows, at]
        for d in range(1, visits):
            source = lax.rem(visit + visits - d, visits)
            current = jnp.where(owner == source, landed[source, rows, spot], current)
        return current

    @pl.when(reduces)
    def _():
        pl.semaphore_wait(ready, around * visits - 1)

    @pl.when(origin)
    def _():
        rows = pl.ds(rows_of(0), ROWS // 2)
        await_bytes(landed.at[pl.ds(1, visits - 1), rows], rs_recv.at[INNER])
        at = slice(half - piece, half + piece)
        ext[pl.ds(pl.multiple_of(PAD + rows_of(0), 8), ROWS // 2), LANES + half - piece : LANES + half + piece] = chosen(
            rows, at, slice(0, 2 * piece)
        )
        for to in range(visits):
            spread_piece(INNER, to)

    @pl.when(middle)
    def _():
        for n in (0, 1, 3):
            start = columns_of(side, n // 2)
            rows = pl.ds(rows_of(n % 2), ROWS // 2)
            spot = pl.ds(pl.multiple_of(start - side * half, LANES), piece)
            await_bytes(landed.at[pl.ds(0, visits - 1), rows, spot], rs_recv.at[n])
            current = chosen(rows, pl.ds(start, piece), spot)
            at = pl.ds(LANES + start, piece)
            ext[pl.ds(pl.multiple_of(PAD + rows_of(n % 2), 8), ROWS // 2), at] = current
            if n == 1:
                merged = jnp.zeros((8, LANES), F32)
                for r in range(ROWS // 8):
                    block = ext[PAD + 8 * r : PAD + 8 * r + 8, at]
                    left = pltpu.roll(block[:, 0:LANES], (PAD * r) % LANES, 1)
                    right = pltpu.roll(block[:, piece - LANES :], (PAD * (r + 1)) % LANES, 1)
                    merged = jnp.where(lane8 == r, jnp.where(side == 0, left, right), merged)
                edge[...] = merged
            spread_piece(n, 0)
        for to in range(1, visits):
            for n in (0, 1, 3):
                spread_piece(n, to)

    for load in loads[4:]:
        load.wait()
    for i in range(2):

        @pl.when(side != i)
        def _():
            await_bytes(landed.at[pl.ds(0, 3), pl.ds(0, ROWS // 2), pl.ds(0, piece)], ag_recv.at[i])

    @pl.when(jnp.logical_not(origin))
    def _():
        await_bytes(landed.at[0, pl.ds(0, ROWS // 2), pl.ds(0, 2 * piece)], ag_recv.at[2])

    await_bytes(ext.at[pl.ds(0, PAD), pl.ds(LANES, width)], row_recv)
    for i in range(2):

        @pl.when(inside(1 - 2 * i))
        def _():
            await_bytes(edge_landed.at[i], edge_recv.at[i])
            first, base = (full - LANES, 0) if i == 0 else (0, LANES - PAD)
            packed = edge_landed[i, 0]
            for r in range(ROWS // 8):
                moved = pltpu.roll(packed, (base - PAD * r) % LANES, 1)
                ext[PAD + 8 * r : PAD + 8 * r + 8, first : first + LANES] = moved
            packed = pltpu.roll(edge_landed[i, 1], lax.rem(base + LANES - (LANES - 2 * PAD) * patch, LANES), 1)
            row = pl.multiple_of((PAD + ROWS) * (1 - patch), 8)
            ext[pl.ds(row, 8), first : first + LANES] = packed
            ext[pl.ds(row + 8, 8), first : first + LANES] = pltpu.roll(packed, LANES - PAD, 1)

    shifted[...] = pltpu.roll(ext[...], full - (LANES - PAD), 1)
    tall = ext_rows + 8
    tall_lane = lax.broadcasted_iota(jnp.int32, (tall, LANES), 1)
    lane = lax.broadcasted_iota(jnp.int32, (CELL, LANES), 1)
    windows = []
    for g in range(cells):
        first = LANES * (g // 2)
        block = shifted[:, first : first + LANES]
        if g % 2:
            block = jnp.where(tall_lane < CELL, shifted[:, first + LANES : first + 2 * LANES], block)
        block = pltpu.roll(block, tall - 1 - offset_ref[0, 0, 0, g], 0)[0:CELL]
        move = 2 * LANES - 1 - CELL * (g % 2) - offset_ref[1, 0, 0, g]
        block = pltpu.roll(block, lax.rem(move, LANES), 1)
        windows.append(jnp.where(lane < CELL, block, pltpu.roll(block, CELL, 1)))
    high, low = split2(jnp.concatenate(windows, axis=1))
    rows_done = dot(srow[...], jnp.concatenate([high, low, high, low], axis=0))
    count = ORDERS * STAMP
    for g in range(cells):
        filtered[APART * g : APART * g + count, :] = rows_done[:, LANES * g : LANES * (g + 1)]
    lane = lax.broadcasted_iota(jnp.int32, (cells * count // 4, LANES), 1)
    parts, tops = [], []
    for m in range(4):
        by_cell = jnp.concatenate([filtered[pl.ds(r, cells, stride=APART), :] for r in range(m, count, 4)], axis=0)
        top = by_cell.astype(BF16).astype(F32)
        parts.append(jnp.where(lane < CELL, top, by_cell - top).astype(BF16))
        tops.append(top)
    for m in (0, 2):
        parts.append(jnp.where(lane < CELL, tops[m], tops[m + 1]).astype(BF16))
    basis = dot(jnp.concatenate(parts, axis=1), scol[...])
    filled = [basis[:, LANES * a : LANES * (a + 1)].reshape(count // 4, cells, LANES) for a in range(ORDERS)]
    eighth = STAMP // 4
    flat = [
        jnp.concatenate([filled[a][eighth * b + j] for j in range(eighth)], axis=1)
        for a in range(ORDERS)
        for b in range(ORDERS)
    ]
    high, low = split2(jnp.concatenate(flat + [image_stamps[...]], axis=0))
    used = cells * (NBASIS + 1)
    spare = jnp.zeros((2 * LANES - used, STAMP * STAMP), BF16)
    across = (((1,), (1,)), ((), ()))
    high_all, low_all = jnp.concatenate([high, spare], axis=0), jnp.concatenate([low, spare], axis=0)
    gram = lax.dot_general(jnp.concatenate([high, low], axis=0), high_all, across, preferred_element_type=F32)
    gram = gram[:used] + gram[used:] + lax.dot_general(high, low_all, across, preferred_element_type=F32)
    gram = gram.reshape(NBASIS + 1, cells, 2 * LANES)
    same = lax.rem(lax.broadcasted_iota(jnp.int32, gram.shape, 2), cells) == lax.broadcasted_iota(jnp.int32, gram.shape, 1)
    sums = jnp.sum(jnp.where(same, gram, 0.0), axis=1)
    sums = jnp.concatenate([sums, jnp.zeros((32 - NBASIS - 1, 2 * LANES), F32)], axis=0)
    padding = lax.broadcasted_iota(jnp.int32, (1, LANES), 1) >= cells
    diag = []
    for k in range(NBASIS):
        low = 8 * (k // 8)
        tile, at = divmod(cells * k, LANES)
        row = sums[low:, LANES * tile : LANES * (tile + 1)]
        row = pltpu.roll(row, LANES - at, 1) if at else row
        place = lax.broadcasted_iota(jnp.int32, row.shape, 0) + low
        diag.append(jnp.where(place == NBASIS + 1, float(flux[k]), row))
    weights, unit = eliminate(diag, flux)
    weights = jnp.where(padding, 0.0, weights)
    unit = jnp.where(padding, 0.0, unit)

    flux_col = jnp.concatenate([jnp.full((1, LANES), float(f), F32) for f in flux] + [jnp.zeros((7, LANES), F32)], axis=0)
    flux_cells = jnp.sum(weights * flux_col, axis=0, keepdims=True)
    curve_cells = jnp.sum(unit * flux_col, axis=0, keepdims=True)
    local = jnp.sum(flux_cells, axis=1, keepdims=True)
    sum_ref[...] = jnp.broadcast_to(local, (8, LANES))
    @pl.when(jnp.logical_not(hub))
    def _():
        pl.semaphore_wait(go, 1)

    for d in range(1, members):
        pltpu.make_async_remote_copy(
            src_ref=sum_ref,
            dst_ref=sum_landed.at[d - 1],
            send_sem=flux_sem.at[0],
            recv_sem=flux_sem.at[1],
            device_id=member(d),
            device_id_type=MESH,
        ).start()

    both = jnp.concatenate([flux_cells, curve_cells, jnp.zeros((6, LANES), F32)], axis=0)
    high, mid, low = [part.astype(F32) for part in split3(jnp.concatenate([weights, unit, both], axis=0))]
    lane = lax.broadcasted_iota(jnp.int32, high.shape, 1)
    low = jnp.where(lane < 2 * cells, pltpu.roll(mid, cells, 1), pltpu.roll(low, 2 * cells, 1))
    spread = dot(jnp.where(lane < cells, high, low).astype(BF16), cell_lane[...])
    blocks = width // LANES
    high, low = split2(shifted[0:ext_rows, :])
    windows = [
        jnp.concatenate([part[:, LANES * h : LANES * h + 2 * LANES] for h in range(blocks)], axis=0) for part in (high, low)
    ]
    columns = dot(jnp.concatenate(windows + windows[:1], axis=1), fcol[...])
    for which in range(2):
        for h in range(blocks):
            for b in range(ORDERS):
                acc = None
                for a in range(ORDERS):
                    k = 32 * which + ORDERS * a + b
                    term = spread[k : k + 1, LANES * h : LANES * (h + 1)] * columns[
                        ext_rows * h : ext_rows * (h + 1), LANES * a : LANES * (a + 1)
                    ]
                    acc = term if acc is None else acc + term
                high, low = split2(acc)
                spot = (slice(ext_rows * b, ext_rows * (b + 1)), slice(width * which + LANES * h, width * which + LANES * (h + 1)))
                combined_h[spot] = high
                combined_l[spot] = low
    matched = dot(frow[...].reshape(2 * ROWS, -1), combined_h[...])
    matched = matched[:ROWS] + (matched[ROWS:] + dot(frow[0], combined_l[...]))
    total = sum_ref[...]
    await_bytes(sum_landed, flux_sem.at[1])
    for d in range(1, members):
        total = total + sum_landed[d - 1]
    mean_flux = total[0:1, 0:1] * (1.0 / (cells * members))
    correction = (mean_flux - spread[64:65]) / spread[65:66]
    out_ref[...] = image_ref[...] - matched[:, 0:width] - correction * matched[:, width:]
    await_bytes(sum_landed, flux_sem.at[0])

    @pl.when(middle)
    def _():
        await_bytes(landed.at[pl.ds(0, 2), pl.ds(0, 5 * ROWS // 8)], rs_send)
        await_bytes(landed.at[pl.ds(0, visits - 1), pl.ds(0, 3 * ROWS // 4)], ag_send)
        await_bytes(landed.at[0, pl.ds(0, ROWS // 2)], row_send)

        @pl.when(inside(outward))
        def _():
            await_bytes(landed.at[0, pl.ds(0, 2 * 8 * visits * LANES // half)], edge_send)

    @pl.when(origin)
    def _():
        await_bytes(landed.at[pl.ds(0, 3), pl.ds(0, ROWS // 2)], rs_send)
        await_bytes(landed.at[pl.ds(0, visits - 1), pl.ds(0, ROWS // 2)], ag_send)
        await_bytes(landed.at[0], row_send)

    @pl.when(jnp.logical_not(reduces))
    def _():
        await_bytes(slot_ref, rs_send)


def fused(owner, offsets, slot, image, filters, counts):
    width = image.shape[2]
    cells = width // CELL
    visits = counts[1]
    members = counts[0] * counts[2]
    sums = filters.sum(axis=1)
    flux = (sums[:, None] * sums[None, :]).reshape(-1)
    consts = constants(filters, cells)
    deep = ORDERS * (ROWS + 2 * PAD)
    full = width + 2 * LANES
    dma = pltpu.SemaphoreType.DMA
    hbm = pl.BlockSpec(memory_space=pltpu.HBM)
    return pl.pallas_call(
        lambda *refs: fused_kernel(counts, flux, *refs),
        name="difference_patch",
        out_shape=jax.ShapeDtypeStruct((ROWS, width), F32),
        in_specs=[hbm] * (4 + len(consts)),
        out_specs=pl.BlockSpec(memory_space=pltpu.VMEM),
        scratch_shapes=[
            pltpu.SMEM(owner.shape, jnp.int32),
            pltpu.SMEM(offsets.shape, jnp.int32),
            pltpu.VMEM((ROWS, width), F32),
            pltpu.VMEM((ROWS, width), F32),
        ]
        + [pltpu.VMEM(const.shape, const.dtype) for const in consts]
        + [
            pltpu.VMEM((ROWS + 2 * PAD + 8, full), F32),
            pltpu.VMEM((visits, ROWS, width // 2), F32),
            pltpu.VMEM((8, LANES), F32),
            pltpu.VMEM((2, 2, 8, LANES), F32),
            pltpu.VMEM((ROWS + 2 * PAD + 8, full), F32),
            pltpu.VMEM((cells * STAMP, LANES), F32),
            pltpu.VMEM((cells, STAMP * STAMP), F32),
            pltpu.VMEM((cells * (APART + 1), LANES), F32),
            pltpu.VMEM((deep, 2 * width), BF16),
            pltpu.VMEM((deep, 2 * width), BF16),
            pltpu.VMEM((8, LANES), F32),
            pltpu.VMEM((members - 1, 8, LANES), F32),
            dma((9,)),
            pltpu.SemaphoreType.REGULAR,
            pltpu.SemaphoreType.REGULAR,
            dma,
            dma((2 * PIECES,)),
            dma,
            dma((3,)),
            dma,
            dma,
            dma,
            dma((2,)),
            dma((2,)),
        ],
        compiler_params=pltpu.CompilerParams(
            collective_id=0, has_side_effects=True, vmem_limit_bytes=40 << 20
        ),
    )(owner, *[pltpu.with_memory_space_constraint(v, pltpu.HBM) for v in (offsets, slot, image, *consts)])


def solution(mesh):
    counts = (mesh.shape["sky"], mesh.shape["visit"], mesh.shape["patch"])
    filters = filter_bank()

    def body(template_store, science, owner_visit, stamp_offset):
        return fused(owner_visit, stamp_offset, template_store, science, filters, counts)[None]

    spec = P("visit", "patch", "sky")
    in_specs = (spec, spec, P("sky", "patch"), P(None, "visit", "patch", "sky"))
    return jax.shard_map(body, mesh=mesh, in_specs=in_specs, out_specs=spec, check_vma=False)
```

```python
import numpy as np
import jax
import jax.numpy as jnp
from jax import lax
from jax.experimental import pallas as pl
from jax.experimental.pallas import tpu as pltpu
from jax.sharding import PartitionSpec as P

HALF = 15
TAPS = 2 * HALF + 1
ORDERS = 5
NBASIS = 25
CELL = 64
STAMP = 32
ROWS = 64
PAD = 16
LANES = 128
PIECES = 2
INNER = 2
APART = ORDERS * STAMP + 1
SIGMA = 5.0
MESH = pl.DeviceIdType.MESH
F32 = jnp.float32
BF16 = jnp.bfloat16


def filter_bank():
    x = (np.arange(TAPS) - HALF) / SIGMA
    env = np.exp(-0.5 * x * x)
    poly = [
        np.ones_like(x),
        2.0 * x,
        4.0 * x**2 - 2.0,
        8.0 * x**3 - 12.0 * x,
        16.0 * x**4 - 48.0 * x**2 + 12.0,
    ]
    shaped = np.stack(poly) * env[None]
    return shaped / np.sqrt(np.sum(shaped * shaped, axis=1, keepdims=True))


def taps_at(filters, index):
    inside = (index >= 0) & (index < TAPS)
    return np.where(inside[None], filters[:, np.clip(index, 0, TAPS - 1)], 0.0)


def two_parts(values):
    values = np.asarray(values, np.float32)
    high = values.astype(BF16)
    return high, (values - high.astype(np.float32)).astype(BF16)


def halves(values):
    return [jnp.asarray(np.stack(two_parts(values)))]


def stacked_halves(values, axis):
    high, low = two_parts(values)
    return [jnp.asarray(np.concatenate([high, high, low, low], axis=axis))]


def constants(filters, cells):
    width = cells * CELL
    stamp_rows = taps_at(filters, np.arange(CELL)[None, :] - np.arange(STAMP)[:, None])
    stamp_rows = stamp_rows.reshape(ORDERS * STAMP, CELL)
    stamp_cols = taps_at(filters, np.arange(CELL)[:, None] - np.arange(STAMP)[None, :])
    high, low = [np.asarray(part, np.float32) for part in two_parts(stamp_cols)]
    placed = np.zeros((4 * 3 * CELL, ORDERS, 4, STAMP), np.float32)
    for m in range(4):
        for part in range(2):
            at = 2 * CELL * m + CELL * part
            placed[at : at + CELL, :, m, :] = np.transpose(high, (1, 0, 2))
        at = 8 * CELL + CELL * m
        placed[at : at + CELL, :, m, :] = np.transpose(low, (1, 0, 2))
    placed = placed.reshape(-1, ORDERS * LANES)
    full_cols = taps_at(filters, np.arange(2 * LANES)[:, None] - np.arange(LANES)[None, :] - 1)
    full_cols = np.transpose(full_cols, (1, 0, 2)).reshape(2 * LANES, ORDERS * LANES)
    high, low = two_parts(full_cols)
    full_rows = taps_at(filters, np.arange(ROWS + 2 * PAD)[None, :] - np.arange(ROWS)[:, None] - 1)
    full_rows = np.transpose(full_rows, (1, 0, 2)).reshape(ROWS, ORDERS * (ROWS + 2 * PAD))
    lane = np.arange(LANES)[:, None]
    cell_lane = (lane % cells == np.arange(width)[None, :] // CELL) & (lane < 3 * cells)
    return (
        stacked_halves(stamp_rows, 1)
        + [jnp.asarray(placed, BF16)]
        + [jnp.asarray(np.concatenate([high, high, low], axis=0))]
        + halves(full_rows)
        + [jnp.asarray(cell_lane, BF16)]
    )


def dot(a, b):
    return jnp.dot(a, b, preferred_element_type=F32)


def split2(x):
    high = x.astype(BF16)
    return high, (x - high.astype(F32)).astype(BF16)


def split3(x):
    high = x.astype(BF16)
    rest = x - high.astype(F32)
    mid = rest.astype(BF16)
    return high, mid, (rest - mid.astype(F32)).astype(BF16)


def eliminate(rows, flux):
    count = len(rows)
    starts = [8 * (k // 8) for k in range(count)]
    for j in range(count):
        first = 8 * (j // 8)
        for i in range(j):
            if starts[i] < first:
                rows[i] = rows[i][first - starts[i] :]
                starts[i] = first
        pivot_row = rows[j]
        scaled = pivot_row * (1.0 / pivot_row[j - first : j - first + 1])
        for i in range(count):
            if i < j:
                rows[i] = rows[i] - rows[i][j - first : j - first + 1] * scaled
            elif i > j:
                factor = pivot_row[i - first : i - first + 1]
                rows[i] = rows[i] - factor * scaled[starts[i] - first :]
        rows[j] = scaled
    weights = jnp.concatenate([row[1:2] for row in rows] + [jnp.zeros((7, LANES), F32)], axis=0)
    unit = jnp.concatenate([row[2:3] for row in rows] + [jnp.zeros((7, LANES), F32)], axis=0)
    return weights, unit


def fused_kernel(
    counts, flux, owner_hbm, offset_hbm, slot_hbm, image_hbm,
    srow_hbm, scol_hbm, fcol_hbm, frow_hbm, put_hbm,
    out_ref,
    owner_ref, offset_ref, slot_ref, image_ref, srow, scol, fcol, frow, cell_lane,
    ext, landed, edge, edge_landed, shifted, image_rows, image_stamps, filtered, combined_h, combined_l, sum_ref, sum_landed,
    local_sem, ready, go, rs_send, rs_recv, ag_send, ag_recv, row_send, row_recv, edge_send, edge_recv, flux_sem,
):
    sky_count, visits, patches = counts
    members = sky_count * patches
    sky = lax.axis_index("sky")
    visit = lax.axis_index("visit")
    patch = lax.axis_index("patch")
    me = sky * patches + patch
    width = image_ref.shape[1]
    cells = width // CELL
    full = width + LANES
    blocks = width // LANES
    ext_rows = ROWS + 2 * PAD
    first_reducer = visits // 2 - 1
    half = width // 2
    piece = half // PIECES
    side = visit - first_reducer
    middle = (side == 0) | (side == 1)
    origin = visit == 0
    reduces = middle | origin
    reducers = (0, first_reducer, first_reducer + 1)
    outward = 2 * side - 1
    hub = (sky == sky_count - 1) & (patch == 0)

    def inside(ds):
        return (sky + ds >= 0) & (sky + ds < sky_count)

    def there(ds, other, v):
        return {
            "sky": jnp.clip(sky + ds, 0, sky_count - 1),
            "visit": v,
            "patch": 1 - patch if other else patch,
        }

    def member(d):
        other = lax.rem(me + d, members)
        return {"sky": other // patches, "patch": lax.rem(other, patches)}

    def rows_of(t):
        return pl.multiple_of(lax.rem(t + 1 - patch, 2) * (ROWS // 2), 8)

    def columns_of(i, j):
        at = i * half + (j + i * (PIECES - 1 - 2 * j)) * piece
        return at if isinstance(at, int) else pl.multiple_of(at, LANES)

    def signal(semaphore, where):
        pl.semaphore_signal(semaphore, inc=1, device_id=where, device_id_type=MESH)

    moves = [
        (owner_hbm, owner_ref),
        (offset_hbm, offset_ref),
        (image_hbm.at[0], image_ref),
        (slot_hbm.at[0], slot_ref),
        (srow_hbm, srow),
        (scol_hbm, scol),
        (fcol_hbm, fcol),
        (frow_hbm, frow),
        (put_hbm, cell_lane),
    ]
    loads = [pltpu.make_async_copy(src, dst, local_sem.at[i]) for i, (src, dst) in enumerate(moves)]

    ext[0:PAD, :] = jnp.zeros((PAD, width), F32)
    ext[PAD + ROWS :, :] = jnp.zeros((PAD + 8, width), F32)

    barrier = pltpu.get_barrier_semaphore()

    @pl.when(reduces)
    def _():
        for ds in (0, -1, 1):

            @pl.when(inside(ds))
            def _():
                for other in (0, 1):
                    for to in range(visits):
                        if ds == 0 and not other:

                            @pl.when(visit != to)
                            def _():
                                signal(barrier, there(ds, other, to))

                        else:
                            signal(barrier, there(ds, other, to))

    @pl.when(jnp.logical_not(hub))
    def _():
        signal(barrier, {"sky": sky_count - 1, "patch": 0})

    around = patches * (1 + inside(-1).astype(jnp.int32) + inside(1).astype(jnp.int32))
    alone = reduces.astype(jnp.int32)
    pl.semaphore_wait(barrier, len(reducers) * around - alone + jnp.where(hub, members - 1, 0))

    def scatter(i, n):
        start = columns_of(i, n // 2)
        rows = pl.ds(rows_of(n % 2), ROWS // 2)
        inner = n == INNER
        return pltpu.make_async_remote_copy(
            src_ref=slot_hbm.at[0, rows, pl.ds(start, piece)],
            dst_ref=landed.at[visit, rows, pl.ds(i * piece if inner else start - i * half, piece)],
            send_sem=rs_send,
            recv_sem=rs_recv.at[n],
            device_id={"visit": 0 if inner else first_reducer + i},
            device_id_type=MESH,
        )

    for n in (0, 1, 3, INNER):
        for i in range(2):

            @pl.when(jnp.logical_not(origin) if n == INNER else side != i)
            def _():
                scatter(i, n).start()

    for load in loads:
        load.start()

    for ds in (0, -1, 1):

        @pl.when(inside(ds))
        def _():
            for other in (0, 1):
                for to in reducers:
                    if ds == 0 and not other:

                        @pl.when(visit != to)
                        def _():
                            signal(ready, there(ds, other, to))

                    else:
                        signal(ready, there(ds, other, to))

    @pl.when(hub)
    def _():
        for d in range(1, members):
            signal(go, member(d))

    for load in loads[:4]:
        load.wait()
    lane = lax.broadcasted_iota(jnp.int32, (STAMP, LANES), 1)
    for g in range(cells):
        first = LANES * (g // 2)
        block = image_ref[:, first : first + LANES]
        block = pltpu.roll(block, lax.rem(ROWS - offset_ref[0, 0, 0, g], ROWS), 0)[0:STAMP]
        block = pltpu.roll(block, lax.rem(2 * LANES - CELL * (g % 2) - offset_ref[1, 0, 0, g], LANES), 1)
        block = jnp.where(lane < STAMP, block, pltpu.roll(block, STAMP, 1))
        block = jnp.where(lane < 2 * STAMP, block, pltpu.roll(block, 2 * STAMP, 1))
        image_rows[STAMP * g : STAMP * (g + 1), :] = block
    group8 = lax.broadcasted_iota(jnp.int32, (cells, LANES), 1) // STAMP
    for j in range(STAMP // 4):
        merged = image_rows[pl.ds(4 * j, cells, stride=STAMP), :]
        for m in range(1, 4):
            merged = jnp.where(group8 == m, image_rows[pl.ds(4 * j + m, cells, stride=STAMP), :], merged)
        image_stamps[:, LANES * j : LANES * (j + 1)] = merged

    owner = owner_ref[0, 0]
    lane8 = lax.broadcasted_iota(jnp.int32, (8, LANES), 1) // PAD

    def await_bytes(ref, semaphore):
        pltpu.make_async_copy(ref, ref, semaphore).wait()

    def own_copy(n, to):
        at = pl.ds(half - piece, 2 * piece) if n == INNER else pl.ds(columns_of(side, n // 2), piece)
        spot = ext.at[pl.ds(pl.multiple_of(PAD + rows_of(n % 2), 8), ROWS // 2), at]
        return pltpu.make_async_remote_copy(
            src_ref=spot,
            dst_ref=spot,
            send_sem=ag_send,
            recv_sem=ag_recv.at[2 if n == INNER else side],
            device_id={"visit": to},
            device_id_type=MESH,
        )

    def row_copy(n, to):
        at = pl.ds(half - piece, 2 * piece) if n == INNER else pl.ds(columns_of(side, 0), piece)
        return pltpu.make_async_remote_copy(
            src_ref=ext.at[pl.ds(pl.multiple_of(ROWS - (ROWS - PAD) * patch, 8), PAD), at],
            dst_ref=ext.at[pl.ds(pl.multiple_of((PAD + ROWS) * patch, 8), PAD), at],
            send_sem=row_send,
            recv_sem=row_recv,
            device_id=there(0, 1, to),
            device_id_type=MESH,
        )

    def edge_copy(to, other):
        return pltpu.make_async_remote_copy(
            src_ref=edge,
            dst_ref=edge_landed.at[side, other],
            send_sem=edge_send,
            recv_sem=edge_recv.at[side],
            device_id=there(outward, other, to),
            device_id_type=MESH,
        )

    def spread_piece(n, to):
        if n == 1:

            @pl.when(inside(outward))
            def _():
                for other in (1, 0):
                    edge_copy(to, other).start()

        if n % 2 == 0:
            row_copy(n, to).start()

        @pl.when(visit != to)
        def _():
            own_copy(n, to).start()

    def chosen(rows, at, spot):
        current = slot_ref[rows, at]
        for d in range(1, visits):
            source = lax.rem(visit + visits - d, visits)
            current = jnp.where(owner == source, landed[source, rows, spot], current)
        return current

    @pl.when(reduces)
    def _():
        pl.semaphore_wait(ready, around * visits - 1)

    @pl.when(origin)
    def _():
        rows = pl.ds(rows_of(0), ROWS // 2)
        await_bytes(landed.at[pl.ds(1, visits - 1), rows], rs_recv.at[INNER])
        at = slice(half - piece, half + piece)
        ext[pl.ds(pl.multiple_of(PAD + rows_of(0), 8), ROWS // 2), at] = chosen(rows, at, slice(0, 2 * piece))
        for to in range(visits):
            spread_piece(INNER, to)

    @pl.when(middle)
    def _():
        for n in (0, 1, 3):
            start = columns_of(side, n // 2)
            rows = pl.ds(rows_of(n % 2), ROWS // 2)
            spot = pl.ds(pl.multiple_of(start - side * half, LANES), piece)
            await_bytes(landed.at[pl.ds(0, visits - 1), rows, spot], rs_recv.at[n])
            current = chosen(rows, pl.ds(start, piece), spot)
            at = pl.ds(start, piece)
            ext[pl.ds(pl.multiple_of(PAD + rows_of(n % 2), 8), ROWS // 2), at] = current
            if n == 1:
                merged = jnp.zeros((8, LANES), F32)
                for r in range(ROWS // 8):
                    block = ext[PAD + 8 * r : PAD + 8 * r + 8, at]
                    left = pltpu.roll(block[:, 0:LANES], (PAD * r) % LANES, 1)
                    right = pltpu.roll(block[:, piece - LANES :], (PAD * (r + 1)) % LANES, 1)
                    merged = jnp.where(lane8 == r, jnp.where(side == 0, left, right), merged)
                edge[...] = merged
            spread_piece(n, 0)
        for to in range(1, visits):
            for n in (0, 1, 3):
                spread_piece(n, to)

    for load in loads[4:]:
        load.wait()
    def shift(first, last, tiles):
        lane = lax.broadcasted_iota(jnp.int32, (last - first, LANES), 1)
        for t in tiles:
            left, right = [
                pltpu.roll(ext[first:last, LANES * u : LANES * (u + 1)], PAD, 1) if 0 <= u < blocks else 0.0
                for u in (t - 1, t)
            ]
            shifted[first:last, LANES * t : LANES * (t + 1)] = jnp.where(lane < PAD, left, right)

    @pl.when(jnp.logical_not(origin))
    def _():
        await_bytes(landed.at[0, pl.ds(0, ROWS // 2), pl.ds(0, 2 * piece)], ag_recv.at[2])

    for i in range(2):

        @pl.when(side != i)
        def _():
            await_bytes(landed.at[pl.ds(0, 3), pl.ds(0, ROWS // 2), pl.ds(0, piece)], ag_recv.at[i])

        shift(PAD, PAD + ROWS, range(blocks // 2 * i, blocks // 2 + (blocks // 2 + 1) * i))

    await_bytes(ext.at[pl.ds(0, PAD), pl.ds(0, width)], row_recv)
    shift(0, PAD, range(blocks + 1))
    shift(PAD + ROWS, ext_rows + 8, range(blocks + 1))
    for i in range(2):

        @pl.when(inside(1 - 2 * i))
        def _():
            await_bytes(edge_landed.at[i], edge_recv.at[i])

    for i in range(2):
        first, base = (width, PAD) if i == 0 else (0, 0)
        here = lane8 == jnp.where(inside(1 - 2 * i), base // PAD, -1)
        packed = edge_landed[i, 0]
        for r in range(ROWS // 8):
            spot = (slice(PAD + 8 * r, PAD + 8 * r + 8), slice(first, first + LANES))
            shifted[spot] = jnp.where(here, pltpu.roll(packed, (base - PAD * r) % LANES, 1), shifted[spot])
        packed = edge_landed[i, 1]
        for r in range(2):
            spot = (pl.ds(pl.multiple_of((PAD + ROWS) * (1 - patch) + 8 * r, 8), 8), slice(first, first + LANES))
            move = lax.rem(base - PAD * r + LANES - (LANES - 2 * PAD) * patch, LANES)
            shifted[spot] = jnp.where(here, pltpu.roll(packed, move, 1), shifted[spot])

    tall = ext_rows + 8
    tall_lane = lax.broadcasted_iota(jnp.int32, (tall, LANES), 1)
    lane = lax.broadcasted_iota(jnp.int32, (CELL, LANES), 1)
    windows = []
    for g in range(cells):
        first = LANES * (g // 2)
        block = shifted[:, first : first + LANES]
        if g % 2:
            block = jnp.where(tall_lane < CELL, shifted[:, first + LANES : first + 2 * LANES], block)
        block = pltpu.roll(block, tall - 1 - offset_ref[0, 0, 0, g], 0)[0:CELL]
        move = 2 * LANES - 1 - CELL * (g % 2) - offset_ref[1, 0, 0, g]
        block = pltpu.roll(block, lax.rem(move, LANES), 1)
        windows.append(jnp.where(lane < CELL, block, pltpu.roll(block, CELL, 1)))
    high, low = split2(jnp.concatenate(windows, axis=1))
    rows_done = dot(srow[...], jnp.concatenate([high, low, high, low], axis=0))
    count = ORDERS * STAMP
    for g in range(cells):
        filtered[APART * g : APART * g + count, :] = rows_done[:, LANES * g : LANES * (g + 1)]
    lane = lax.broadcasted_iota(jnp.int32, (cells * count // 4, LANES), 1)
    parts, tops = [], []
    for m in range(4):
        by_cell = jnp.concatenate([filtered[pl.ds(r, cells, stride=APART), :] for r in range(m, count, 4)], axis=0)
        top = by_cell.astype(BF16).astype(F32)
        parts.append(jnp.where(lane < CELL, top, by_cell - top).astype(BF16))
        tops.append(top)
    for m in (0, 2):
        parts.append(jnp.where(lane < CELL, tops[m], tops[m + 1]).astype(BF16))
    basis = dot(jnp.concatenate(parts, axis=1), scol[...])
    filled = [basis[:, LANES * a : LANES * (a + 1)].reshape(count // 4, cells, LANES) for a in range(ORDERS)]
    eighth = STAMP // 4
    flat = [
        jnp.concatenate([filled[a][eighth * b + j] for j in range(eighth)], axis=1)
        for a in range(ORDERS)
        for b in range(ORDERS)
    ]
    high, low = split2(jnp.concatenate(flat + [image_stamps[...]], axis=0))
    used = cells * (NBASIS + 1)
    spare = jnp.zeros((2 * LANES - used, STAMP * STAMP), BF16)
    across = (((1,), (1,)), ((), ()))
    high_all, low_all = jnp.concatenate([high, spare], axis=0), jnp.concatenate([low, spare], axis=0)
    gram = lax.dot_general(high, high_all, across, preferred_element_type=F32)
    gram = gram + lax.dot_general(high, low_all, across, preferred_element_type=F32)
    gram = gram + lax.dot_general(low, high_all, across, preferred_element_type=F32)
    gram = gram.reshape(NBASIS + 1, cells, 2 * LANES)
    same = lax.rem(lax.broadcasted_iota(jnp.int32, gram.shape, 2), cells) == lax.broadcasted_iota(jnp.int32, gram.shape, 1)
    sums = jnp.sum(jnp.where(same, gram, 0.0), axis=1)
    sums = jnp.concatenate([sums, jnp.zeros((32 - NBASIS - 1, 2 * LANES), F32)], axis=0)
    padding = lax.broadcasted_iota(jnp.int32, (1, LANES), 1) >= cells
    diag = []
    for k in range(NBASIS):
        low = 8 * (k // 8)
        tile, at = divmod(cells * k, LANES)
        row = sums[low:, LANES * tile : LANES * (tile + 1)]
        row = pltpu.roll(row, LANES - at, 1) if at else row
        place = lax.broadcasted_iota(jnp.int32, row.shape, 0) + low
        diag.append(jnp.where(place == NBASIS + 1, float(flux[k]), row))
    weights, unit = eliminate(diag, flux)
    weights = jnp.where(padding, 0.0, weights)
    unit = jnp.where(padding, 0.0, unit)

    flux_col = jnp.concatenate([jnp.full((1, LANES), float(f), F32) for f in flux] + [jnp.zeros((7, LANES), F32)], axis=0)
    flux_cells = jnp.sum(weights * flux_col, axis=0, keepdims=True)
    curve_cells = jnp.sum(unit * flux_col, axis=0, keepdims=True)
    local = jnp.sum(flux_cells, axis=1, keepdims=True)
    sum_ref[...] = jnp.broadcast_to(local, (8, LANES))
    @pl.when(jnp.logical_not(hub))
    def _():
        pl.semaphore_wait(go, 1)

    for d in range(1, members):
        pltpu.make_async_remote_copy(
            src_ref=sum_ref.at[pl.ds(0, 1)],
            dst_ref=sum_landed.at[d - 1, pl.ds(0, 1)],
            send_sem=flux_sem.at[0],
            recv_sem=flux_sem.at[1],
            device_id=member(d),
            device_id_type=MESH,
        ).start()

    both = jnp.concatenate([flux_cells, curve_cells, jnp.zeros((6, LANES), F32)], axis=0)
    high, mid, low = [part.astype(F32) for part in split3(jnp.concatenate([weights, unit, both], axis=0))]
    lane = lax.broadcasted_iota(jnp.int32, high.shape, 1)
    low = jnp.where(lane < 2 * cells, pltpu.roll(mid, cells, 1), pltpu.roll(low, 2 * cells, 1))
    spread = dot(jnp.where(lane < cells, high, low).astype(BF16), cell_lane[...])
    high, low = split2(shifted[0:ext_rows, :])
    windows = [
        jnp.concatenate([part[:, LANES * h : LANES * h + 2 * LANES] for h in range(blocks)], axis=0) for part in (high, low)
    ]
    columns = dot(jnp.concatenate(windows + windows[:1], axis=1), fcol[...])
    for which in range(2):
        for h in range(blocks):
            for b in range(ORDERS):
                acc = None
                for a in range(ORDERS):
                    k = 32 * which + ORDERS * a + b
                    term = spread[k : k + 1, LANES * h : LANES * (h + 1)] * columns[
                        ext_rows * h : ext_rows * (h + 1), LANES * a : LANES * (a + 1)
                    ]
                    acc = term if acc is None else acc + term
                high, low = split2(acc)
                spot = (slice(ext_rows * b, ext_rows * (b + 1)), slice(width * which + LANES * h, width * which + LANES * (h + 1)))
                combined_h[spot] = high
                combined_l[spot] = low
    matched = dot(frow[...].reshape(2 * ROWS, -1), combined_h[...])
    matched = matched[:ROWS] + (matched[ROWS:] + dot(frow[0], combined_l[...]))
    total = sum_ref[0:1]
    all_sums = sum_landed.at[pl.ds(0, members - 1), pl.ds(0, 1)]
    await_bytes(all_sums, flux_sem.at[1])
    for d in range(1, members):
        total = total + sum_landed[d - 1, 0:1]
    mean_flux = total[0:1, 0:1] * (1.0 / (cells * members))
    correction = (mean_flux - spread[64:65]) / spread[65:66]
    out_ref[...] = image_ref[...] - matched[:, 0:width] - correction * matched[:, width:]
    await_bytes(all_sums, flux_sem.at[0])

    @pl.when(middle)
    def _():
        await_bytes(landed.at[pl.ds(0, 2), pl.ds(0, 5 * ROWS // 8)], rs_send)
        await_bytes(landed.at[pl.ds(0, visits - 1), pl.ds(0, 3 * ROWS // 4)], ag_send)
        await_bytes(landed.at[0, pl.ds(0, ROWS // 2)], row_send)

        @pl.when(inside(outward))
        def _():
            await_bytes(landed.at[0, pl.ds(0, 2 * 8 * visits * LANES // half)], edge_send)

    @pl.when(origin)
    def _():
        await_bytes(landed.at[pl.ds(0, 3), pl.ds(0, ROWS // 2)], rs_send)
        await_bytes(landed.at[pl.ds(0, visits - 1), pl.ds(0, ROWS // 2)], ag_send)
        await_bytes(landed.at[0], row_send)

    @pl.when(jnp.logical_not(reduces))
    def _():
        await_bytes(slot_ref, rs_send)


def fused(owner, offsets, slot, image, filters, counts):
    width = image.shape[2]
    cells = width // CELL
    visits = counts[1]
    members = counts[0] * counts[2]
    sums = filters.sum(axis=1)
    flux = (sums[:, None] * sums[None, :]).reshape(-1)
    consts = constants(filters, cells)
    deep = ORDERS * (ROWS + 2 * PAD)
    dma = pltpu.SemaphoreType.DMA
    hbm = pl.BlockSpec(memory_space=pltpu.HBM)
    return pl.pallas_call(
        lambda *refs: fused_kernel(counts, flux, *refs),
        name="difference_patch",
        out_shape=jax.ShapeDtypeStruct((ROWS, width), F32),
        in_specs=[hbm] * (4 + len(consts)),
        out_specs=pl.BlockSpec(memory_space=pltpu.VMEM),
        scratch_shapes=[
            pltpu.SMEM(owner.shape, jnp.int32),
            pltpu.SMEM(offsets.shape, jnp.int32),
            pltpu.VMEM((ROWS, width), F32),
            pltpu.VMEM((ROWS, width), F32),
        ]
        + [pltpu.VMEM(const.shape, const.dtype) for const in consts]
        + [
            pltpu.VMEM((ROWS + 2 * PAD + 8, width), F32),
            pltpu.VMEM((visits, ROWS, width // 2), F32),
            pltpu.VMEM((8, LANES), F32),
            pltpu.VMEM((2, 2, 8, LANES), F32),
            pltpu.VMEM((ROWS + 2 * PAD + 8, width + LANES), F32),
            pltpu.VMEM((cells * STAMP, LANES), F32),
            pltpu.VMEM((cells, STAMP * STAMP), F32),
            pltpu.VMEM((cells * (APART + 1), LANES), F32),
            pltpu.VMEM((deep, 2 * width), BF16),
            pltpu.VMEM((deep, 2 * width), BF16),
            pltpu.VMEM((8, LANES), F32),
            pltpu.VMEM((members - 1, 8, LANES), F32),
            dma((9,)),
            pltpu.SemaphoreType.REGULAR,
            pltpu.SemaphoreType.REGULAR,
            dma,
            dma((2 * PIECES,)),
            dma,
            dma((3,)),
            dma,
            dma,
            dma,
            dma((2,)),
            dma((2,)),
        ],
        compiler_params=pltpu.CompilerParams(
            collective_id=0, has_side_effects=True, vmem_limit_bytes=40 << 20
        ),
    )(owner, *[pltpu.with_memory_space_constraint(v, pltpu.HBM) for v in (offsets, slot, image, *consts)])


def solution(mesh):
    counts = (mesh.shape["sky"], mesh.shape["visit"], mesh.shape["patch"])
    filters = filter_bank()

    def body(template_store, science, owner_visit, stamp_offset):
        return fused(owner_visit, stamp_offset, template_store, science, filters, counts)[None]

    spec = P("visit", "patch", "sky")
    in_specs = (spec, spec, P("sky", "patch"), P(None, "visit", "patch", "sky"))
    return jax.shard_map(body, mesh=mesh, in_specs=in_specs, out_specs=spec, check_vma=False)
```

```python
import numpy as np
import jax
import jax.numpy as jnp
from jax import lax
from jax.experimental import pallas as pl
from jax.experimental.pallas import tpu as pltpu
from jax.sharding import PartitionSpec as P

HALF = 15
TAPS = 2 * HALF + 1
ORDERS = 5
NBASIS = 25
CELL = 64
STAMP = 32
ROWS = 64
PAD = 16
LANES = 128
PIECES = 2
INNER = 2
APART = ORDERS * STAMP + 1
SIGMA = 5.0
MESH = pl.DeviceIdType.MESH
F32 = jnp.float32
BF16 = jnp.bfloat16


def filter_bank():
    x = (np.arange(TAPS) - HALF) / SIGMA
    env = np.exp(-0.5 * x * x)
    poly = [
        np.ones_like(x),
        2.0 * x,
        4.0 * x**2 - 2.0,
        8.0 * x**3 - 12.0 * x,
        16.0 * x**4 - 48.0 * x**2 + 12.0,
    ]
    shaped = np.stack(poly) * env[None]
    return shaped / np.sqrt(np.sum(shaped * shaped, axis=1, keepdims=True))


def taps_at(filters, index):
    inside = (index >= 0) & (index < TAPS)
    return np.where(inside[None], filters[:, np.clip(index, 0, TAPS - 1)], 0.0)


def two_parts(values):
    values = np.asarray(values, np.float32)
    high = values.astype(BF16)
    return high, (values - high.astype(np.float32)).astype(BF16)


def halves(values):
    return [jnp.asarray(np.stack(two_parts(values)))]


def stacked_halves(values, axis):
    high, low = two_parts(values)
    return [jnp.asarray(np.concatenate([high, high, low, low], axis=axis))]


def constants(filters, cells):
    width = cells * CELL
    stamp_rows = taps_at(filters, np.arange(CELL)[None, :] - np.arange(STAMP)[:, None])
    stamp_rows = stamp_rows.reshape(ORDERS * STAMP, CELL)
    stamp_cols = taps_at(filters, np.arange(CELL)[:, None] - np.arange(STAMP)[None, :])
    high, low = [np.asarray(part, np.float32) for part in two_parts(stamp_cols)]
    placed = np.zeros((4, 4, CELL, 8, STAMP), np.float32)
    for m in range(4):
        for part, values in enumerate((high, high, low)):
            for a in range(ORDERS - 1):
                placed[m, part, :, (a + m) % 4, :] = values[a]
            placed[m, part, :, 4 + m, :] = values[ORDERS - 1]
    placed = placed.reshape(4, 4 * CELL, 2 * LANES)
    full_cols = taps_at(filters, np.arange(2 * LANES)[:, None] - np.arange(LANES)[None, :] - 1)
    full_cols = np.transpose(full_cols, (1, 0, 2)).reshape(2 * LANES, ORDERS * LANES)
    high, low = two_parts(full_cols)
    full_rows = taps_at(filters, np.arange(ROWS + 2 * PAD)[None, :] - np.arange(ROWS)[:, None] - 1)
    full_rows = np.transpose(full_rows, (1, 0, 2)).reshape(ROWS, ORDERS * (ROWS + 2 * PAD))
    lane = np.arange(LANES)[:, None]
    cell_lane = (lane % cells == np.arange(width)[None, :] // CELL) & (lane < 3 * cells)
    return (
        stacked_halves(stamp_rows, 1)
        + [jnp.asarray(placed, BF16)]
        + [jnp.asarray(np.concatenate([high, high, low], axis=0))]
        + halves(full_rows)
        + [jnp.asarray(cell_lane, BF16)]
    )


def dot(a, b):
    return jnp.dot(a, b, preferred_element_type=F32)


def split2(x):
    high = x.astype(BF16)
    return high, (x - high.astype(F32)).astype(BF16)


def split3(x):
    high = x.astype(BF16)
    rest = x - high.astype(F32)
    mid = rest.astype(BF16)
    return high, mid, (rest - mid.astype(F32)).astype(BF16)


def eliminate(rows, flux):
    count = len(rows)
    starts = [8 * (k // 8) for k in range(count)]
    for j in range(0, count - 1, 2):
        first = 8 * (j // 8)
        for i in range(j):
            if starts[i] < first:
                rows[i] = rows[i][first - starts[i] :]
                starts[i] = first
        one, two = rows[j], rows[j + 1]
        at = j - first
        a, b, d = one[at : at + 1], one[at + 1 : at + 2], two[at + 1 : at + 2]
        inverse = 1.0 / (a * d - b * b)
        a, b, d = a * inverse, b * inverse, d * inverse
        scaled_one, scaled_two = d * one - b * two, a * two - b * one
        for i in range(count):
            if i < j:
                p, q = rows[i][at : at + 1], rows[i][at + 1 : at + 2]
                rows[i] = rows[i] - (p * scaled_one + q * scaled_two)
            elif i > j + 1:
                p, q = one[i - first : i - first + 1], two[i - first : i - first + 1]
                skip = starts[i] - first
                rows[i] = rows[i] - (p * scaled_one[skip:] + q * scaled_two[skip:])
        rows[j], rows[j + 1] = scaled_one, scaled_two
    last = rows[-1]
    at = count - 1 - starts[-1]
    last = last * (1.0 / last[at : at + 1])
    for i in range(count - 1):
        row = rows[i][starts[-1] - starts[i] :]
        rows[i] = row - row[at : at + 1] * last
    rows[-1] = last
    weights = jnp.concatenate([row[1:2] for row in rows] + [jnp.zeros((7, LANES), F32)], axis=0)
    unit = jnp.concatenate([row[2:3] for row in rows] + [jnp.zeros((7, LANES), F32)], axis=0)
    return weights, unit


def fused_kernel(
    counts, flux, owner_hbm, offset_hbm, slot_hbm, image_hbm,
    srow_hbm, scol_hbm, fcol_hbm, frow_hbm, put_hbm,
    out_ref,
    owner_ref, offset_ref, slot_ref, image_ref, srow, scol, fcol, frow, cell_lane,
    ext, landed, edge, edge_landed, shifted, image_rows, image_stamps, filtered, combined_h, combined_l, sum_ref, sum_landed,
    local_sem, ready, go, rs_send, rs_recv, ag_send, ag_recv, row_send, row_recv, edge_send, edge_recv, flux_sem,
):
    sky_count, visits, patches = counts
    members = sky_count * patches
    sky = lax.axis_index("sky")
    visit = lax.axis_index("visit")
    patch = lax.axis_index("patch")
    me = sky * patches + patch
    width = image_ref.shape[1]
    cells = width // CELL
    full = width + LANES
    blocks = width // LANES
    ext_rows = ROWS + 2 * PAD
    first_reducer = visits // 2 - 1
    half = width // 2
    piece = half // PIECES
    side = visit - first_reducer
    middle = (side == 0) | (side == 1)
    origin = visit == 0
    reduces = middle | origin
    reducers = (0, first_reducer, first_reducer + 1)
    outward = 2 * side - 1
    hub = (sky == sky_count - 1) & (patch == 0)

    def inside(ds):
        return (sky + ds >= 0) & (sky + ds < sky_count)

    def there(ds, other, v):
        return {
            "sky": jnp.clip(sky + ds, 0, sky_count - 1),
            "visit": v,
            "patch": 1 - patch if other else patch,
        }

    def member(d):
        other = lax.rem(me + d, members)
        return {"sky": other // patches, "patch": lax.rem(other, patches)}

    def rows_of(t):
        return pl.multiple_of(lax.rem(t + 1 - patch, 2) * (ROWS // 2), 8)

    def columns_of(i, j):
        at = i * half + (j + i * (PIECES - 1 - 2 * j)) * piece
        return at if isinstance(at, int) else pl.multiple_of(at, LANES)

    def signal(semaphore, where):
        pl.semaphore_signal(semaphore, inc=1, device_id=where, device_id_type=MESH)

    moves = [
        (owner_hbm, owner_ref),
        (offset_hbm, offset_ref),
        (image_hbm.at[0], image_ref),
        (slot_hbm.at[0], slot_ref),
        (srow_hbm, srow),
        (scol_hbm, scol),
        (fcol_hbm, fcol),
        (frow_hbm, frow),
        (put_hbm, cell_lane),
    ]
    loads = [pltpu.make_async_copy(src, dst, local_sem.at[i]) for i, (src, dst) in enumerate(moves)]

    ext[0:PAD, :] = jnp.zeros((PAD, width), F32)
    ext[PAD + ROWS :, :] = jnp.zeros((PAD + 8, width), F32)

    barrier = pltpu.get_barrier_semaphore()

    @pl.when(reduces)
    def _():
        for ds in (0, -1, 1):

            @pl.when(inside(ds))
            def _():
                for other in (0, 1):
                    for to in range(visits):
                        if ds == 0 and not other:

                            @pl.when(visit != to)
                            def _():
                                signal(barrier, there(ds, other, to))

                        else:
                            signal(barrier, there(ds, other, to))

    @pl.when(jnp.logical_not(hub))
    def _():
        signal(barrier, {"sky": sky_count - 1, "patch": 0})

    around = patches * (1 + inside(-1).astype(jnp.int32) + inside(1).astype(jnp.int32))
    alone = reduces.astype(jnp.int32)
    pl.semaphore_wait(barrier, len(reducers) * around - alone + jnp.where(hub, members - 1, 0))

    def scatter(i, n):
        start = columns_of(i, n // 2)
        rows = pl.ds(rows_of(n % 2), ROWS // 2)
        inner = n == INNER
        return pltpu.make_async_remote_copy(
            src_ref=slot_hbm.at[0, rows, pl.ds(start, piece)],
            dst_ref=landed.at[visit, rows, pl.ds(i * piece if inner else start - i * half, piece)],
            send_sem=rs_send,
            recv_sem=rs_recv.at[n],
            device_id={"visit": 0 if inner else first_reducer + i},
            device_id_type=MESH,
        )

    for n in (0, 1, 3, INNER):
        for i in range(2):

            @pl.when(jnp.logical_not(origin) if n == INNER else side != i)
            def _():
                scatter(i, n).start()

    for load in loads:
        load.start()

    for ds in (0, -1, 1):

        @pl.when(inside(ds))
        def _():
            for other in (0, 1):
                for to in reducers:
                    if ds == 0 and not other:

                        @pl.when(visit != to)
                        def _():
                            signal(ready, there(ds, other, to))

                    else:
                        signal(ready, there(ds, other, to))

    @pl.when(hub)
    def _():
        for d in range(1, members):
            signal(go, member(d))

    for load in loads[:4]:
        load.wait()
    lane = lax.broadcasted_iota(jnp.int32, (STAMP, LANES), 1)
    for g in range(cells):
        first = LANES * (g // 2)
        block = image_ref[:, first : first + LANES]
        block = pltpu.roll(block, lax.rem(ROWS - offset_ref[0, 0, 0, g], ROWS), 0)[0:STAMP]
        block = pltpu.roll(block, lax.rem(2 * LANES - CELL * (g % 2) - offset_ref[1, 0, 0, g], LANES), 1)
        block = jnp.where(lane < STAMP, block, pltpu.roll(block, STAMP, 1))
        block = jnp.where(lane < 2 * STAMP, block, pltpu.roll(block, 2 * STAMP, 1))
        image_rows[STAMP * g : STAMP * (g + 1), :] = block
    group8 = lax.broadcasted_iota(jnp.int32, (cells, LANES), 1) // STAMP
    for j in range(STAMP // 4):
        merged = image_rows[pl.ds(4 * j, cells, stride=STAMP), :]
        for m in range(1, 4):
            merged = jnp.where(group8 == m, image_rows[pl.ds(4 * j + m, cells, stride=STAMP), :], merged)
        image_stamps[:, LANES * j : LANES * (j + 1)] = merged

    owner = owner_ref[0, 0]
    lane8 = lax.broadcasted_iota(jnp.int32, (8, LANES), 1) // PAD

    def await_bytes(ref, semaphore):
        pltpu.make_async_copy(ref, ref, semaphore).wait()

    def own_copy(n, to):
        at = pl.ds(half - piece, 2 * piece) if n == INNER else pl.ds(columns_of(side, n // 2), piece)
        spot = ext.at[pl.ds(pl.multiple_of(PAD + rows_of(n % 2), 8), ROWS // 2), at]
        return pltpu.make_async_remote_copy(
            src_ref=spot,
            dst_ref=spot,
            send_sem=ag_send,
            recv_sem=ag_recv.at[2 if n == INNER else side],
            device_id={"visit": to},
            device_id_type=MESH,
        )

    def row_copy(n, to):
        at = pl.ds(half - piece, 2 * piece) if n == INNER else pl.ds(columns_of(side, 0), piece)
        return pltpu.make_async_remote_copy(
            src_ref=ext.at[pl.ds(pl.multiple_of(ROWS - (ROWS - PAD) * patch, 8), PAD), at],
            dst_ref=ext.at[pl.ds(pl.multiple_of((PAD + ROWS) * patch, 8), PAD), at],
            send_sem=row_send,
            recv_sem=row_recv,
            device_id=there(0, 1, to),
            device_id_type=MESH,
        )

    def edge_copy(to, other):
        return pltpu.make_async_remote_copy(
            src_ref=edge,
            dst_ref=edge_landed.at[side, other],
            send_sem=edge_send,
            recv_sem=edge_recv.at[side],
            device_id=there(outward, other, to),
            device_id_type=MESH,
        )

    def spread_piece(n, to):
        if n == 1:

            @pl.when(inside(outward))
            def _():
                for other in (1, 0):
                    edge_copy(to, other).start()

        if n % 2 == 0:
            row_copy(n, to).start()

        @pl.when(visit != to)
        def _():
            own_copy(n, to).start()

    def chosen(rows, at, spot):
        current = slot_ref[rows, at]
        for d in range(1, visits):
            source = lax.rem(visit + visits - d, visits)
            current = jnp.where(owner == source, landed[source, rows, spot], current)
        return current

    @pl.when(reduces)
    def _():
        pl.semaphore_wait(ready, around * visits - 1)

    @pl.when(origin)
    def _():
        rows = pl.ds(rows_of(0), ROWS // 2)
        await_bytes(landed.at[pl.ds(1, visits - 1), rows], rs_recv.at[INNER])
        at = slice(half - piece, half + piece)
        ext[pl.ds(pl.multiple_of(PAD + rows_of(0), 8), ROWS // 2), at] = chosen(rows, at, slice(0, 2 * piece))
        for to in range(visits):
            spread_piece(INNER, to)

    @pl.when(middle)
    def _():
        for n in (0, 1, 3):
            start = columns_of(side, n // 2)
            rows = pl.ds(rows_of(n % 2), ROWS // 2)
            spot = pl.ds(pl.multiple_of(start - side * half, LANES), piece)
            await_bytes(landed.at[pl.ds(0, visits - 1), rows, spot], rs_recv.at[n])
            current = chosen(rows, pl.ds(start, piece), spot)
            at = pl.ds(start, piece)
            ext[pl.ds(pl.multiple_of(PAD + rows_of(n % 2), 8), ROWS // 2), at] = current
            if n == 1:
                merged = jnp.zeros((8, LANES), F32)
                for r in range(ROWS // 8):
                    block = ext[PAD + 8 * r : PAD + 8 * r + 8, at]
                    left = pltpu.roll(block[:, 0:LANES], (PAD * r) % LANES, 1)
                    right = pltpu.roll(block[:, piece - LANES :], (PAD * (r + 1)) % LANES, 1)
                    merged = jnp.where(lane8 == r, jnp.where(side == 0, left, right), merged)
                edge[...] = merged
            spread_piece(n, 0)
        for to in range(1, visits):
            for n in (0, 1, 3):
                spread_piece(n, to)

    for load in loads[4:]:
        load.wait()
    def shift(first, last, tiles):
        lane = lax.broadcasted_iota(jnp.int32, (last - first, LANES), 1)
        for t in tiles:
            left, right = [
                pltpu.roll(ext[first:last, LANES * u : LANES * (u + 1)], PAD, 1) if 0 <= u < blocks else 0.0
                for u in (t - 1, t)
            ]
            shifted[first:last, LANES * t : LANES * (t + 1)] = jnp.where(lane < PAD, left, right)

    @pl.when(jnp.logical_not(origin))
    def _():
        await_bytes(landed.at[0, pl.ds(0, ROWS // 2), pl.ds(0, 2 * piece)], ag_recv.at[2])

    for i in range(2):

        @pl.when(side != i)
        def _():
            await_bytes(landed.at[pl.ds(0, 3), pl.ds(0, ROWS // 2), pl.ds(0, piece)], ag_recv.at[i])

        shift(PAD, PAD + ROWS, range(blocks // 2 * i, blocks // 2 + (blocks // 2 + 1) * i))

    await_bytes(ext.at[pl.ds(0, PAD), pl.ds(0, width)], row_recv)
    shift(0, PAD, range(blocks + 1))
    shift(PAD + ROWS, ext_rows + 8, range(blocks + 1))
    for i in range(2):

        @pl.when(inside(1 - 2 * i))
        def _():
            await_bytes(edge_landed.at[i], edge_recv.at[i])

    for i in range(2):
        first, base = (width, PAD) if i == 0 else (0, 0)
        here = lane8 == jnp.where(inside(1 - 2 * i), base // PAD, -1)
        packed = edge_landed[i, 0]
        for r in range(ROWS // 8):
            spot = (slice(PAD + 8 * r, PAD + 8 * r + 8), slice(first, first + LANES))
            shifted[spot] = jnp.where(here, pltpu.roll(packed, (base - PAD * r) % LANES, 1), shifted[spot])
        packed = edge_landed[i, 1]
        for r in range(2):
            spot = (pl.ds(pl.multiple_of((PAD + ROWS) * (1 - patch) + 8 * r, 8), 8), slice(first, first + LANES))
            move = lax.rem(base - PAD * r + LANES - (LANES - 2 * PAD) * patch, LANES)
            shifted[spot] = jnp.where(here, pltpu.roll(packed, move, 1), shifted[spot])

    tall = ext_rows + 8
    tall_lane = lax.broadcasted_iota(jnp.int32, (tall, LANES), 1)
    lane = lax.broadcasted_iota(jnp.int32, (CELL, LANES), 1)
    windows = []
    for g in range(cells):
        first = LANES * (g // 2)
        block = shifted[:, first : first + LANES]
        if g % 2:
            block = jnp.where(tall_lane < CELL, shifted[:, first + LANES : first + 2 * LANES], block)
        block = pltpu.roll(block, tall - 1 - offset_ref[0, 0, 0, g], 0)[0:CELL]
        move = 2 * LANES - 1 - CELL * (g % 2) - offset_ref[1, 0, 0, g]
        block = pltpu.roll(block, lax.rem(move, LANES), 1)
        windows.append(jnp.where(lane < CELL, block, pltpu.roll(block, CELL, 1)))
    high, low = split2(jnp.concatenate(windows, axis=1))
    rows_done = dot(srow[...], jnp.concatenate([high, low, high, low], axis=0))
    count = ORDERS * STAMP
    for g in range(cells):
        filtered[APART * g : APART * g + count, :] = rows_done[:, LANES * g : LANES * (g + 1)]
    lane = lax.broadcasted_iota(jnp.int32, (cells * count // 4, LANES), 1)
    turned = []
    for m in range(4):
        by_cell = jnp.concatenate([filtered[pl.ds(r, cells, stride=APART), :] for r in range(m, count, 4)], axis=0)
        top = by_cell.astype(BF16).astype(F32)
        both = jnp.where(lane < CELL, top, by_cell - top).astype(BF16)
        turned.append(dot(jnp.concatenate([both, top.astype(BF16)], axis=1), scol[m]))
    group = lane // STAMP
    filled = []
    for a in range(ORDERS - 1):
        merged = turned[-a % 4][:, 0:LANES]
        for g in range(1, 4):
            merged = jnp.where(group == g, turned[(g - a) % 4][:, 0:LANES], merged)
        filled.append(pltpu.roll(merged, LANES - STAMP * a, 1) if a else merged)
    filled.append(sum(part[:, LANES:] for part in turned))
    filled = [part.reshape(count // 4, cells, LANES) for part in filled]
    eighth = STAMP // 4
    flat = [
        jnp.concatenate([filled[a][eighth * b + j] for j in range(eighth)], axis=1)
        for a in range(ORDERS)
        for b in range(ORDERS)
    ]
    high, low = split2(jnp.concatenate(flat + [image_stamps[...]], axis=0))
    used = cells * (NBASIS + 1)
    spare = jnp.zeros((2 * LANES - used, STAMP * STAMP), BF16)
    across = (((1,), (1,)), ((), ()))
    high_all = jnp.concatenate([high, spare], axis=0)
    gram = lax.dot_general(jnp.concatenate([high, low], axis=0), high_all, across, preferred_element_type=F32)
    mixed = jnp.concatenate([gram[used:], jnp.zeros((2 * LANES - used, 2 * LANES), F32)], axis=0)
    gram = gram[:used] + (mixed + mixed.T)[:used]
    gram = gram.reshape(NBASIS + 1, cells, 2 * LANES)
    same = lax.rem(lax.broadcasted_iota(jnp.int32, gram.shape, 2), cells) == lax.broadcasted_iota(jnp.int32, gram.shape, 1)
    sums = jnp.sum(jnp.where(same, gram, 0.0), axis=1)
    sums = jnp.concatenate([sums, jnp.zeros((32 - NBASIS - 1, 2 * LANES), F32)], axis=0)
    padding = lax.broadcasted_iota(jnp.int32, (1, LANES), 1) >= cells
    diag = []
    for k in range(NBASIS):
        low = 8 * (k // 8)
        tile, at = divmod(cells * k, LANES)
        row = sums[low:, LANES * tile : LANES * (tile + 1)]
        row = pltpu.roll(row, LANES - at, 1) if at else row
        place = lax.broadcasted_iota(jnp.int32, row.shape, 0) + low
        diag.append(jnp.where(place == NBASIS + 1, float(flux[k]), row))
    weights, unit = eliminate(diag, flux)
    weights = jnp.where(padding, 0.0, weights)
    unit = jnp.where(padding, 0.0, unit)

    flux_col = jnp.concatenate([jnp.full((1, LANES), float(f), F32) for f in flux] + [jnp.zeros((7, LANES), F32)], axis=0)
    flux_cells = jnp.sum(weights * flux_col, axis=0, keepdims=True)
    curve_cells = jnp.sum(unit * flux_col, axis=0, keepdims=True)
    local = jnp.sum(flux_cells, axis=1, keepdims=True)
    sum_ref[...] = jnp.broadcast_to(local, (8, LANES))
    @pl.when(jnp.logical_not(hub))
    def _():
        pl.semaphore_wait(go, 1)

    for d in range(1, members):
        pltpu.make_async_remote_copy(
            src_ref=sum_ref.at[pl.ds(0, 1)],
            dst_ref=sum_landed.at[d - 1, pl.ds(0, 1)],
            send_sem=flux_sem.at[0],
            recv_sem=flux_sem.at[1],
            device_id=member(d),
            device_id_type=MESH,
        ).start()

    both = jnp.concatenate([flux_cells, curve_cells, jnp.zeros((6, LANES), F32)], axis=0)
    high, mid, low = [part.astype(F32) for part in split3(jnp.concatenate([weights, unit, both], axis=0))]
    lane = lax.broadcasted_iota(jnp.int32, high.shape, 1)
    low = jnp.where(lane < 2 * cells, pltpu.roll(mid, cells, 1), pltpu.roll(low, 2 * cells, 1))
    spread = dot(jnp.where(lane < cells, high, low).astype(BF16), cell_lane[...])
    high, low = split2(shifted[0:ext_rows, :])
    windows = [
        jnp.concatenate([part[:, LANES * h : LANES * h + 2 * LANES] for h in range(blocks)], axis=0) for part in (high, low)
    ]
    columns = dot(jnp.concatenate(windows + windows[:1], axis=1), fcol[...])
    for which in range(2):
        for h in range(blocks):
            for b in range(ORDERS):
                acc = None
                for a in range(ORDERS):
                    k = 32 * which + ORDERS * a + b
                    term = spread[k : k + 1, LANES * h : LANES * (h + 1)] * columns[
                        ext_rows * h : ext_rows * (h + 1), LANES * a : LANES * (a + 1)
                    ]
                    acc = term if acc is None else acc + term
                high, low = split2(acc)
                spot = (slice(ext_rows * b, ext_rows * (b + 1)), slice(width * which + LANES * h, width * which + LANES * (h + 1)))
                combined_h[spot] = high
                combined_l[spot] = low
    matched = dot(frow[...].reshape(2 * ROWS, -1), combined_h[...])
    matched = matched[:ROWS] + (matched[ROWS:] + dot(frow[0], combined_l[...]))
    total = sum_ref[0:1]
    all_sums = sum_landed.at[pl.ds(0, members - 1), pl.ds(0, 1)]
    await_bytes(all_sums, flux_sem.at[1])
    for d in range(1, members):
        total = total + sum_landed[d - 1, 0:1]
    mean_flux = total[0:1, 0:1] * (1.0 / (cells * members))
    correction = (mean_flux - spread[64:65]) / spread[65:66]
    out_ref[...] = image_ref[...] - matched[:, 0:width] - correction * matched[:, width:]
    await_bytes(all_sums, flux_sem.at[0])

    @pl.when(middle)
    def _():
        await_bytes(landed.at[pl.ds(0, 2), pl.ds(0, 5 * ROWS // 8)], rs_send)
        await_bytes(landed.at[pl.ds(0, visits - 1), pl.ds(0, 3 * ROWS // 4)], ag_send)
        await_bytes(landed.at[0, pl.ds(0, ROWS // 2)], row_send)

        @pl.when(inside(outward))
        def _():
            await_bytes(landed.at[0, pl.ds(0, 2 * 8 * visits * LANES // half)], edge_send)

    @pl.when(origin)
    def _():
        await_bytes(landed.at[pl.ds(0, 3), pl.ds(0, ROWS // 2)], rs_send)
        await_bytes(landed.at[pl.ds(0, visits - 1), pl.ds(0, ROWS // 2)], ag_send)
        await_bytes(landed.at[0], row_send)

    @pl.when(jnp.logical_not(reduces))
    def _():
        await_bytes(slot_ref, rs_send)


def fused(owner, offsets, slot, image, filters, counts):
    width = image.shape[2]
    cells = width // CELL
    visits = counts[1]
    members = counts[0] * counts[2]
    sums = filters.sum(axis=1)
    flux = (sums[:, None] * sums[None, :]).reshape(-1)
    consts = constants(filters, cells)
    deep = ORDERS * (ROWS + 2 * PAD)
    dma = pltpu.SemaphoreType.DMA
    hbm = pl.BlockSpec(memory_space=pltpu.HBM)
    return pl.pallas_call(
        lambda *refs: fused_kernel(counts, flux, *refs),
        name="difference_patch",
        out_shape=jax.ShapeDtypeStruct((ROWS, width), F32),
        in_specs=[hbm] * (4 + len(consts)),
        out_specs=pl.BlockSpec(memory_space=pltpu.VMEM),
        scratch_shapes=[
            pltpu.SMEM(owner.shape, jnp.int32),
            pltpu.SMEM(offsets.shape, jnp.int32),
            pltpu.VMEM((ROWS, width), F32),
            pltpu.VMEM((ROWS, width), F32),
        ]
        + [pltpu.VMEM(const.shape, const.dtype) for const in consts]
        + [
            pltpu.VMEM((ROWS + 2 * PAD + 8, width), F32),
            pltpu.VMEM((visits, ROWS, width // 2), F32),
            pltpu.VMEM((8, LANES), F32),
            pltpu.VMEM((2, 2, 8, LANES), F32),
            pltpu.VMEM((ROWS + 2 * PAD + 8, width + LANES), F32),
            pltpu.VMEM((cells * STAMP, LANES), F32),
            pltpu.VMEM((cells, STAMP * STAMP), F32),
            pltpu.VMEM((cells * (APART + 1), LANES), F32),
            pltpu.VMEM((deep, 2 * width), BF16),
            pltpu.VMEM((deep, 2 * width), BF16),
            pltpu.VMEM((8, LANES), F32),
            pltpu.VMEM((members - 1, 8, LANES), F32),
            dma((9,)),
            pltpu.SemaphoreType.REGULAR,
            pltpu.SemaphoreType.REGULAR,
            dma,
            dma((2 * PIECES,)),
            dma,
            dma((3,)),
            dma,
            dma,
            dma,
            dma((2,)),
            dma((2,)),
        ],
        compiler_params=pltpu.CompilerParams(
            collective_id=0, has_side_effects=True, vmem_limit_bytes=40 << 20
        ),
    )(owner, *[pltpu.with_memory_space_constraint(v, pltpu.HBM) for v in (offsets, slot, image, *consts)])


def solution(mesh):
    counts = (mesh.shape["sky"], mesh.shape["visit"], mesh.shape["patch"])
    filters = filter_bank()

    def body(template_store, science, owner_visit, stamp_offset):
        return fused(owner_visit, stamp_offset, template_store, science, filters, counts)[None]

    spec = P("visit", "patch", "sky")
    in_specs = (spec, spec, P("sky", "patch"), P(None, "visit", "patch", "sky"))
    return jax.shard_map(body, mesh=mesh, in_specs=in_specs, out_specs=spec, check_vma=False)
```

```python
import numpy as np
import jax
import jax.numpy as jnp
from jax import lax
from jax.experimental import pallas as pl
from jax.experimental.pallas import tpu as pltpu
from jax.sharding import PartitionSpec as P

HALF = 15
TAPS = 2 * HALF + 1
ORDERS = 5
NBASIS = 25
CELL = 64
STAMP = 32
ROWS = 64
PAD = 16
LANES = 128
PIECES = 2
INNER = 2
APART = ORDERS * STAMP + 1
SIGMA = 5.0
MESH = pl.DeviceIdType.MESH
F32 = jnp.float32
BF16 = jnp.bfloat16


def filter_bank():
    x = (np.arange(TAPS) - HALF) / SIGMA
    env = np.exp(-0.5 * x * x)
    poly = [
        np.ones_like(x),
        2.0 * x,
        4.0 * x**2 - 2.0,
        8.0 * x**3 - 12.0 * x,
        16.0 * x**4 - 48.0 * x**2 + 12.0,
    ]
    shaped = np.stack(poly) * env[None]
    return shaped / np.sqrt(np.sum(shaped * shaped, axis=1, keepdims=True))


def taps_at(filters, index):
    inside = (index >= 0) & (index < TAPS)
    return np.where(inside[None], filters[:, np.clip(index, 0, TAPS - 1)], 0.0)


def two_parts(values):
    values = np.asarray(values, np.float32)
    high = values.astype(BF16)
    return high, (values - high.astype(np.float32)).astype(BF16)


def halves(values):
    return [jnp.asarray(np.stack(two_parts(values)))]


def stacked_halves(values, axis):
    high, low = two_parts(values)
    return [jnp.asarray(np.concatenate([high, high, low, low], axis=axis))]


def constants(filters, cells):
    width = cells * CELL
    stamp_rows = taps_at(filters, np.arange(CELL)[None, :] - np.arange(STAMP)[:, None])
    stamp_rows = stamp_rows.reshape(ORDERS * STAMP, CELL)
    stamp_cols = taps_at(filters, np.arange(CELL)[:, None] - np.arange(STAMP)[None, :])
    high, low = [np.asarray(part, np.float32) for part in two_parts(stamp_cols)]
    placed = np.zeros((4, 4, CELL, 8, STAMP), np.float32)
    for m in range(4):
        for part, values in enumerate((high, high, low)):
            for a in range(ORDERS - 1):
                placed[m, part, :, (a + m) % 4, :] = values[a]
            placed[m, part, :, 4 + m, :] = values[ORDERS - 1]
    placed = placed.reshape(4, 4 * CELL, 2 * LANES)
    full_cols = taps_at(filters, np.arange(2 * LANES)[:, None] - np.arange(LANES)[None, :] - 1)
    full_cols = np.transpose(full_cols, (1, 0, 2)).reshape(2 * LANES, ORDERS * LANES)
    high, low = two_parts(full_cols)
    full_rows = taps_at(filters, np.arange(ROWS + 2 * PAD)[None, :] - np.arange(ROWS)[:, None] - 1)
    full_rows = np.transpose(full_rows, (1, 0, 2)).reshape(ROWS, ORDERS * (ROWS + 2 * PAD))
    lane = np.arange(LANES)[:, None]
    cell_lane = (lane % cells == np.arange(width)[None, :] // CELL) & (lane < 3 * cells)
    return (
        stacked_halves(stamp_rows, 1)
        + [jnp.asarray(placed, BF16)]
        + [jnp.asarray(np.concatenate([high, high, low], axis=0))]
        + halves(full_rows)
        + [jnp.asarray(cell_lane, BF16)]
    )


def dot(a, b):
    return jnp.dot(a, b, preferred_element_type=F32)


def split2(x):
    high = x.astype(BF16)
    return high, (x - high.astype(F32)).astype(BF16)


def split3(x):
    high = x.astype(BF16)
    rest = x - high.astype(F32)
    mid = rest.astype(BF16)
    return high, mid, (rest - mid.astype(F32)).astype(BF16)


def eliminate(rows, flux):
    count = len(rows)
    starts = [8 * (k // 8) for k in range(count)]
    for j in range(0, count - 1, 2):
        first = 8 * (j // 8)
        for i in range(j):
            if starts[i] < first:
                rows[i] = rows[i][first - starts[i] :]
                starts[i] = first
        one, two = rows[j], rows[j + 1]
        at = j - first
        a, b, d = one[at : at + 1], one[at + 1 : at + 2], two[at + 1 : at + 2]
        inverse = 1.0 / (a * d - b * b)
        a, b, d = a * inverse, b * inverse, d * inverse
        scaled_one, scaled_two = d * one - b * two, a * two - b * one
        for i in range(count):
            if i < j:
                p, q = rows[i][at : at + 1], rows[i][at + 1 : at + 2]
                rows[i] = rows[i] - (p * scaled_one + q * scaled_two)
            elif i > j + 1:
                p, q = one[i - first : i - first + 1], two[i - first : i - first + 1]
                skip = starts[i] - first
                rows[i] = rows[i] - (p * scaled_one[skip:] + q * scaled_two[skip:])
        rows[j], rows[j + 1] = scaled_one, scaled_two
    last = rows[-1]
    at = count - 1 - starts[-1]
    last = last * (1.0 / last[at : at + 1])
    for i in range(count - 1):
        row = rows[i][starts[-1] - starts[i] :]
        rows[i] = row - row[at : at + 1] * last
    rows[-1] = last
    weights = jnp.concatenate([row[1:2] for row in rows] + [jnp.zeros((7, LANES), F32)], axis=0)
    unit = jnp.concatenate([row[2:3] for row in rows] + [jnp.zeros((7, LANES), F32)], axis=0)
    return weights, unit


def fused_kernel(
    counts, flux, owner_hbm, offset_hbm, slot_hbm, image_hbm,
    srow_hbm, scol_hbm, fcol_hbm, frow_hbm, put_hbm,
    out_ref,
    owner_ref, offset_ref, slot_ref, image_ref, srow, scol, fcol, frow, cell_lane,
    ext, landed, edge, edge_landed, shifted, image_rows, image_stamps, filtered, combined_h, combined_l, sum_ref, sum_landed,
    local_sem, ready, go, rs_send, rs_recv, ag_send, ag_recv, row_send, row_recv, edge_send, edge_recv, flux_sem,
):
    sky_count, visits, patches = counts
    members = sky_count * patches
    sky = lax.axis_index("sky")
    visit = lax.axis_index("visit")
    patch = lax.axis_index("patch")
    me = sky * patches + patch
    width = image_ref.shape[1]
    cells = width // CELL
    full = width + LANES
    blocks = width // LANES
    ext_rows = ROWS + 2 * PAD
    first_reducer = visits // 2 - 1
    half = width // 2
    piece = half // PIECES
    side = visit - first_reducer
    middle = (side == 0) | (side == 1)
    origin = visit == 0
    reduces = middle | origin
    reducers = (0, first_reducer, first_reducer + 1)
    outward = 2 * side - 1
    hub = (sky == sky_count - 1) & (patch == 0)

    def inside(ds):
        return (sky + ds >= 0) & (sky + ds < sky_count)

    def there(ds, other, v):
        return {
            "sky": jnp.clip(sky + ds, 0, sky_count - 1),
            "visit": v,
            "patch": 1 - patch if other else patch,
        }

    def member(d):
        other = lax.rem(me + d, members)
        return {"sky": other // patches, "patch": lax.rem(other, patches)}

    def rows_of(t):
        return pl.multiple_of(lax.rem(t + 1 - patch, 2) * (ROWS // 2), 8)

    def columns_of(i, j):
        at = i * half + (j + i * (PIECES - 1 - 2 * j)) * piece
        return at if isinstance(at, int) else pl.multiple_of(at, LANES)

    def signal(semaphore, where):
        pl.semaphore_signal(semaphore, inc=1, device_id=where, device_id_type=MESH)

    moves = [
        (owner_hbm, owner_ref),
        (offset_hbm, offset_ref),
        (image_hbm.at[0], image_ref),
        (slot_hbm.at[0], slot_ref),
        (srow_hbm, srow),
        (scol_hbm, scol),
        (fcol_hbm, fcol),
        (frow_hbm, frow),
        (put_hbm, cell_lane),
    ]
    loads = [pltpu.make_async_copy(src, dst, local_sem.at[i]) for i, (src, dst) in enumerate(moves)]

    loads[3].start()
    ext[0:PAD, :] = jnp.zeros((PAD, width), F32)
    ext[PAD + ROWS :, :] = jnp.zeros((PAD + 8, width), F32)

    barrier = pltpu.get_barrier_semaphore()

    @pl.when(reduces)
    def _():
        for ds in (0, -1, 1):

            @pl.when(inside(ds))
            def _():
                for other in (0, 1):
                    for to in range(visits):
                        if ds == 0 and not other:

                            @pl.when(visit != to)
                            def _():
                                signal(barrier, there(ds, other, to))

                        else:
                            signal(barrier, there(ds, other, to))

    @pl.when(jnp.logical_not(hub))
    def _():
        signal(barrier, {"sky": sky_count - 1, "patch": 0})

    around = patches * (1 + inside(-1).astype(jnp.int32) + inside(1).astype(jnp.int32))
    alone = reduces.astype(jnp.int32)
    pl.semaphore_wait(barrier, len(reducers) * around - alone + jnp.where(hub, members - 1, 0))

    def scatter(i, n):
        start = columns_of(i, n // 2)
        rows = pl.ds(rows_of(n % 2), ROWS // 2)
        inner = n == INNER
        return pltpu.make_async_remote_copy(
            src_ref=slot_ref.at[rows, pl.ds(start, piece)],
            dst_ref=landed.at[visit, rows, pl.ds(i * piece if inner else start - i * half, piece)],
            send_sem=rs_send,
            recv_sem=rs_recv.at[n],
            device_id={"visit": 0 if inner else first_reducer + i},
            device_id_type=MESH,
        )

    loads[3].wait()
    for n in (0, 1, 3, INNER):
        for i in range(2):

            @pl.when(jnp.logical_not(origin) if n == INNER else side != i)
            def _():
                scatter(i, n).start()

    for load in loads[:3] + loads[4:]:
        load.start()

    for ds in (0, -1, 1):

        @pl.when(inside(ds))
        def _():
            for other in (0, 1):
                for to in reducers:
                    if ds == 0 and not other:

                        @pl.when(visit != to)
                        def _():
                            signal(ready, there(ds, other, to))

                    else:
                        signal(ready, there(ds, other, to))

    @pl.when(hub)
    def _():
        for d in range(1, members):
            signal(go, member(d))

    for load in loads[:3]:
        load.wait()
    lane = lax.broadcasted_iota(jnp.int32, (STAMP, LANES), 1)
    for g in range(cells):
        first = LANES * (g // 2)
        block = image_ref[:, first : first + LANES]
        block = pltpu.roll(block, lax.rem(ROWS - offset_ref[0, 0, 0, g], ROWS), 0)[0:STAMP]
        block = pltpu.roll(block, lax.rem(2 * LANES - CELL * (g % 2) - offset_ref[1, 0, 0, g], LANES), 1)
        block = jnp.where(lane < STAMP, block, pltpu.roll(block, STAMP, 1))
        block = jnp.where(lane < 2 * STAMP, block, pltpu.roll(block, 2 * STAMP, 1))
        image_rows[STAMP * g : STAMP * (g + 1), :] = block
    group8 = lax.broadcasted_iota(jnp.int32, (cells, LANES), 1) // STAMP
    for j in range(STAMP // 4):
        merged = image_rows[pl.ds(4 * j, cells, stride=STAMP), :]
        for m in range(1, 4):
            merged = jnp.where(group8 == m, image_rows[pl.ds(4 * j + m, cells, stride=STAMP), :], merged)
        image_stamps[:, LANES * j : LANES * (j + 1)] = merged

    owner = owner_ref[0, 0]
    lane8 = lax.broadcasted_iota(jnp.int32, (8, LANES), 1) // PAD

    def await_bytes(ref, semaphore):
        pltpu.make_async_copy(ref, ref, semaphore).wait()

    def own_copy(n, to):
        at = pl.ds(half - piece, 2 * piece) if n == INNER else pl.ds(columns_of(side, n // 2), piece)
        spot = ext.at[pl.ds(pl.multiple_of(PAD + rows_of(n % 2), 8), ROWS // 2), at]
        return pltpu.make_async_remote_copy(
            src_ref=spot,
            dst_ref=spot,
            send_sem=ag_send,
            recv_sem=ag_recv.at[2 if n == INNER else side],
            device_id={"visit": to},
            device_id_type=MESH,
        )

    def row_copy(n, to):
        at = pl.ds(half - piece, 2 * piece) if n == INNER else pl.ds(columns_of(side, 0), piece)
        return pltpu.make_async_remote_copy(
            src_ref=ext.at[pl.ds(pl.multiple_of(ROWS - (ROWS - PAD) * patch, 8), PAD), at],
            dst_ref=ext.at[pl.ds(pl.multiple_of((PAD + ROWS) * patch, 8), PAD), at],
            send_sem=row_send,
            recv_sem=row_recv,
            device_id=there(0, 1, to),
            device_id_type=MESH,
        )

    def edge_copy(to, other):
        return pltpu.make_async_remote_copy(
            src_ref=edge,
            dst_ref=edge_landed.at[side, other],
            send_sem=edge_send,
            recv_sem=edge_recv.at[side],
            device_id=there(outward, other, to),
            device_id_type=MESH,
        )

    def spread_piece(n, to):
        if n == 1:

            @pl.when(inside(outward))
            def _():
                for other in (1, 0):
                    edge_copy(to, other).start()

        if n % 2 == 0:
            row_copy(n, to).start()

        @pl.when(visit != to)
        def _():
            own_copy(n, to).start()

    def chosen(rows, at, spot):
        current = slot_ref[rows, at]
        for d in range(1, visits):
            source = lax.rem(visit + visits - d, visits)
            current = jnp.where(owner == source, landed[source, rows, spot], current)
        return current

    @pl.when(reduces)
    def _():
        pl.semaphore_wait(ready, around * visits - 1)

    @pl.when(origin)
    def _():
        rows = pl.ds(rows_of(0), ROWS // 2)
        await_bytes(landed.at[pl.ds(1, visits - 1), rows], rs_recv.at[INNER])
        at = slice(half - piece, half + piece)
        ext[pl.ds(pl.multiple_of(PAD + rows_of(0), 8), ROWS // 2), at] = chosen(rows, at, slice(0, 2 * piece))
        for to in range(visits):
            spread_piece(INNER, to)

    @pl.when(middle)
    def _():
        for n in (0, 1, 3):
            start = columns_of(side, n // 2)
            rows = pl.ds(rows_of(n % 2), ROWS // 2)
            spot = pl.ds(pl.multiple_of(start - side * half, LANES), piece)
            await_bytes(landed.at[pl.ds(0, visits - 1), rows, spot], rs_recv.at[n])
            current = chosen(rows, pl.ds(start, piece), spot)
            at = pl.ds(start, piece)
            ext[pl.ds(pl.multiple_of(PAD + rows_of(n % 2), 8), ROWS // 2), at] = current
            if n == 1:
                merged = jnp.zeros((8, LANES), F32)
                for r in range(ROWS // 8):
                    block = ext[PAD + 8 * r : PAD + 8 * r + 8, at]
                    left = pltpu.roll(block[:, 0:LANES], (PAD * r) % LANES, 1)
                    right = pltpu.roll(block[:, piece - LANES :], (PAD * (r + 1)) % LANES, 1)
                    merged = jnp.where(lane8 == r, jnp.where(side == 0, left, right), merged)
                edge[...] = merged
            spread_piece(n, 0)
        for to in range(1, visits):
            for n in (0, 1, 3):
                spread_piece(n, to)

    for load in loads[4:]:
        load.wait()
    def shift(first, last, tiles):
        lane = lax.broadcasted_iota(jnp.int32, (last - first, LANES), 1)
        for t in tiles:
            left, right = [
                pltpu.roll(ext[first:last, LANES * u : LANES * (u + 1)], PAD, 1) if 0 <= u < blocks else 0.0
                for u in (t - 1, t)
            ]
            shifted[first:last, LANES * t : LANES * (t + 1)] = jnp.where(lane < PAD, left, right)

    @pl.when(jnp.logical_not(origin))
    def _():
        await_bytes(landed.at[0, pl.ds(0, ROWS // 2), pl.ds(0, 2 * piece)], ag_recv.at[2])

    for i in range(2):

        @pl.when(side != i)
        def _():
            await_bytes(landed.at[pl.ds(0, 3), pl.ds(0, ROWS // 2), pl.ds(0, piece)], ag_recv.at[i])

        shift(PAD, PAD + ROWS, range(blocks // 2 * i, blocks // 2 + (blocks // 2 + 1) * i))

    await_bytes(ext.at[pl.ds(0, PAD), pl.ds(0, width)], row_recv)
    shift(0, PAD, range(blocks + 1))
    shift(PAD + ROWS, ext_rows + 8, range(blocks + 1))
    for i in range(2):

        @pl.when(inside(1 - 2 * i))
        def _():
            await_bytes(edge_landed.at[i], edge_recv.at[i])

    for i in range(2):
        first, base = (width, PAD) if i == 0 else (0, 0)
        here = lane8 == jnp.where(inside(1 - 2 * i), base // PAD, -1)
        packed = edge_landed[i, 0]
        for r in range(ROWS // 8):
            spot = (slice(PAD + 8 * r, PAD + 8 * r + 8), slice(first, first + LANES))
            shifted[spot] = jnp.where(here, pltpu.roll(packed, (base - PAD * r) % LANES, 1), shifted[spot])
        packed = edge_landed[i, 1]
        for r in range(2):
            spot = (pl.ds(pl.multiple_of((PAD + ROWS) * (1 - patch) + 8 * r, 8), 8), slice(first, first + LANES))
            move = lax.rem(base - PAD * r + LANES - (LANES - 2 * PAD) * patch, LANES)
            shifted[spot] = jnp.where(here, pltpu.roll(packed, move, 1), shifted[spot])

    tall = ext_rows + 8
    tall_lane = lax.broadcasted_iota(jnp.int32, (tall, LANES), 1)
    lane = lax.broadcasted_iota(jnp.int32, (CELL, LANES), 1)
    windows = []
    for g in range(cells):
        first = LANES * (g // 2)
        block = shifted[:, first : first + LANES]
        if g % 2:
            block = jnp.where(tall_lane < CELL, shifted[:, first + LANES : first + 2 * LANES], block)
        block = pltpu.roll(block, tall - 1 - offset_ref[0, 0, 0, g], 0)[0:CELL]
        move = 2 * LANES - 1 - CELL * (g % 2) - offset_ref[1, 0, 0, g]
        block = pltpu.roll(block, lax.rem(move, LANES), 1)
        windows.append(jnp.where(lane < CELL, block, pltpu.roll(block, CELL, 1)))
    high, low = split2(jnp.concatenate(windows, axis=1))
    rows_done = dot(srow[...], jnp.concatenate([high, low, high, low], axis=0))
    count = ORDERS * STAMP
    for g in range(cells):
        filtered[APART * g : APART * g + count, :] = rows_done[:, LANES * g : LANES * (g + 1)]
    lane = lax.broadcasted_iota(jnp.int32, (cells * count // 4, LANES), 1)
    turned = []
    for m in range(4):
        by_cell = jnp.concatenate([filtered[pl.ds(r, cells, stride=APART), :] for r in range(m, count, 4)], axis=0)
        top = by_cell.astype(BF16).astype(F32)
        both = jnp.where(lane < CELL, top, by_cell - top).astype(BF16)
        turned.append(dot(jnp.concatenate([both, top.astype(BF16)], axis=1), scol[m]))
    group = lane // STAMP
    filled = []
    for a in range(ORDERS - 1):
        merged = turned[-a % 4][:, 0:LANES]
        for g in range(1, 4):
            merged = jnp.where(group == g, turned[(g - a) % 4][:, 0:LANES], merged)
        filled.append(pltpu.roll(merged, LANES - STAMP * a, 1) if a else merged)
    filled.append(sum(part[:, LANES:] for part in turned))
    filled = [part.reshape(count // 4, cells, LANES) for part in filled]
    eighth = STAMP // 4
    flat = [
        jnp.concatenate([filled[a][eighth * b + j] for j in range(eighth)], axis=1)
        for a in range(ORDERS)
        for b in range(ORDERS)
    ]
    high, low = split2(jnp.concatenate(flat + [image_stamps[...]], axis=0))
    used = cells * (NBASIS + 1)
    spare = jnp.zeros((2 * LANES - used, STAMP * STAMP), BF16)
    across = (((1,), (1,)), ((), ()))
    high_all = jnp.concatenate([high, spare], axis=0)
    gram = lax.dot_general(jnp.concatenate([high, low], axis=0), high_all, across, preferred_element_type=F32)
    mixed = jnp.concatenate([gram[used:], jnp.zeros((2 * LANES - used, 2 * LANES), F32)], axis=0)
    gram = gram[:used] + (mixed + mixed.T)[:used]
    gram = gram.reshape(NBASIS + 1, cells, 2 * LANES)
    same = lax.rem(lax.broadcasted_iota(jnp.int32, gram.shape, 2), cells) == lax.broadcasted_iota(jnp.int32, gram.shape, 1)
    sums = jnp.sum(jnp.where(same, gram, 0.0), axis=1)
    sums = jnp.concatenate([sums, jnp.zeros((32 - NBASIS - 1, 2 * LANES), F32)], axis=0)
    padding = lax.broadcasted_iota(jnp.int32, (1, LANES), 1) >= cells
    diag = []
    for k in range(NBASIS):
        low = 8 * (k // 8)
        tile, at = divmod(cells * k, LANES)
        row = sums[low:, LANES * tile : LANES * (tile + 1)]
        row = pltpu.roll(row, LANES - at, 1) if at else row
        place = lax.broadcasted_iota(jnp.int32, row.shape, 0) + low
        diag.append(jnp.where(place == NBASIS + 1, float(flux[k]), row))
    weights, unit = eliminate(diag, flux)
    weights = jnp.where(padding, 0.0, weights)
    unit = jnp.where(padding, 0.0, unit)

    flux_col = jnp.concatenate([jnp.full((1, LANES), float(f), F32) for f in flux] + [jnp.zeros((7, LANES), F32)], axis=0)
    flux_cells = jnp.sum(weights * flux_col, axis=0, keepdims=True)
    curve_cells = jnp.sum(unit * flux_col, axis=0, keepdims=True)
    local = jnp.sum(flux_cells, axis=1, keepdims=True)
    sum_ref[...] = jnp.broadcast_to(local, (8, LANES))
    @pl.when(jnp.logical_not(hub))
    def _():
        pl.semaphore_wait(go, 1)

    for d in range(1, members):
        pltpu.make_async_remote_copy(
            src_ref=sum_ref.at[pl.ds(0, 1)],
            dst_ref=sum_landed.at[d - 1, pl.ds(0, 1)],
            send_sem=flux_sem.at[0],
            recv_sem=flux_sem.at[1],
            device_id=member(d),
            device_id_type=MESH,
        ).start()

    both = jnp.concatenate([flux_cells, curve_cells, jnp.zeros((6, LANES), F32)], axis=0)
    high, mid, low = [part.astype(F32) for part in split3(jnp.concatenate([weights, unit, both], axis=0))]
    lane = lax.broadcasted_iota(jnp.int32, high.shape, 1)
    low = jnp.where(lane < 2 * cells, pltpu.roll(mid, cells, 1), pltpu.roll(low, 2 * cells, 1))
    spread = dot(jnp.where(lane < cells, high, low).astype(BF16), cell_lane[...])
    high, low = split2(shifted[0:ext_rows, :])
    windows = [
        jnp.concatenate([part[:, LANES * h : LANES * h + 2 * LANES] for h in range(blocks)], axis=0) for part in (high, low)
    ]
    columns = dot(jnp.concatenate(windows + windows[:1], axis=1), fcol[...])
    for which in range(2):
        for h in range(blocks):
            for b in range(ORDERS):
                acc = None
                for a in range(ORDERS):
                    k = 32 * which + ORDERS * a + b
                    term = spread[k : k + 1, LANES * h : LANES * (h + 1)] * columns[
                        ext_rows * h : ext_rows * (h + 1), LANES * a : LANES * (a + 1)
                    ]
                    acc = term if acc is None else acc + term
                high, low = split2(acc)
                spot = (slice(ext_rows * b, ext_rows * (b + 1)), slice(width * which + LANES * h, width * which + LANES * (h + 1)))
                combined_h[spot] = high
                combined_l[spot] = low
    matched = dot(frow[...].reshape(2 * ROWS, -1), combined_h[...])
    matched = matched[:ROWS] + (matched[ROWS:] + dot(frow[0], combined_l[...]))
    total = sum_ref[0:1]
    all_sums = sum_landed.at[pl.ds(0, members - 1), pl.ds(0, 1)]
    await_bytes(all_sums, flux_sem.at[1])
    for d in range(1, members):
        total = total + sum_landed[d - 1, 0:1]
    mean_flux = total[0:1, 0:1] * (1.0 / (cells * members))
    correction = (mean_flux - spread[64:65]) / spread[65:66]
    out_ref[...] = image_ref[...] - matched[:, 0:width] - correction * matched[:, width:]
    await_bytes(all_sums, flux_sem.at[0])

    @pl.when(middle)
    def _():
        await_bytes(landed.at[pl.ds(0, 2), pl.ds(0, 5 * ROWS // 8)], rs_send)
        await_bytes(landed.at[pl.ds(0, visits - 1), pl.ds(0, 3 * ROWS // 4)], ag_send)
        await_bytes(landed.at[0, pl.ds(0, ROWS // 2)], row_send)

        @pl.when(inside(outward))
        def _():
            await_bytes(landed.at[0, pl.ds(0, 2 * 8 * visits * LANES // half)], edge_send)

    @pl.when(origin)
    def _():
        await_bytes(landed.at[pl.ds(0, 3), pl.ds(0, ROWS // 2)], rs_send)
        await_bytes(landed.at[pl.ds(0, visits - 1), pl.ds(0, ROWS // 2)], ag_send)
        await_bytes(landed.at[0], row_send)

    @pl.when(jnp.logical_not(reduces))
    def _():
        await_bytes(slot_ref, rs_send)


def fused(owner, offsets, slot, image, filters, counts):
    width = image.shape[2]
    cells = width // CELL
    visits = counts[1]
    members = counts[0] * counts[2]
    sums = filters.sum(axis=1)
    flux = (sums[:, None] * sums[None, :]).reshape(-1)
    consts = constants(filters, cells)
    deep = ORDERS * (ROWS + 2 * PAD)
    dma = pltpu.SemaphoreType.DMA
    hbm = pl.BlockSpec(memory_space=pltpu.HBM)
    return pl.pallas_call(
        lambda *refs: fused_kernel(counts, flux, *refs),
        name="difference_patch",
        out_shape=jax.ShapeDtypeStruct((ROWS, width), F32),
        in_specs=[hbm] * (4 + len(consts)),
        out_specs=pl.BlockSpec(memory_space=pltpu.VMEM),
        scratch_shapes=[
            pltpu.SMEM(owner.shape, jnp.int32),
            pltpu.SMEM(offsets.shape, jnp.int32),
            pltpu.VMEM((ROWS, width), F32),
            pltpu.VMEM((ROWS, width), F32),
        ]
        + [pltpu.VMEM(const.shape, const.dtype) for const in consts]
        + [
            pltpu.VMEM((ROWS + 2 * PAD + 8, width), F32),
            pltpu.VMEM((visits, ROWS, width // 2), F32),
            pltpu.VMEM((8, LANES), F32),
            pltpu.VMEM((2, 2, 8, LANES), F32),
            pltpu.VMEM((ROWS + 2 * PAD + 8, width + LANES), F32),
            pltpu.VMEM((cells * STAMP, LANES), F32),
            pltpu.VMEM((cells, STAMP * STAMP), F32),
            pltpu.VMEM((cells * (APART + 1), LANES), F32),
            pltpu.VMEM((deep, 2 * width), BF16),
            pltpu.VMEM((deep, 2 * width), BF16),
            pltpu.VMEM((8, LANES), F32),
            pltpu.VMEM((members - 1, 8, LANES), F32),
            dma((9,)),
            pltpu.SemaphoreType.REGULAR,
            pltpu.SemaphoreType.REGULAR,
            dma,
            dma((2 * PIECES,)),
            dma,
            dma((3,)),
            dma,
            dma,
            dma,
            dma((2,)),
            dma((2,)),
        ],
        compiler_params=pltpu.CompilerParams(
            collective_id=0, has_side_effects=True, vmem_limit_bytes=40 << 20
        ),
    )(owner, *[pltpu.with_memory_space_constraint(v, pltpu.HBM) for v in (offsets, slot, image, *consts)])


def solution(mesh):
    counts = (mesh.shape["sky"], mesh.shape["visit"], mesh.shape["patch"])
    filters = filter_bank()

    def body(template_store, science, owner_visit, stamp_offset):
        return fused(owner_visit, stamp_offset, template_store, science, filters, counts)[None]

    spec = P("visit", "patch", "sky")
    in_specs = (spec, spec, P("sky", "patch"), P(None, "visit", "patch", "sky"))
    return jax.shard_map(body, mesh=mesh, in_specs=in_specs, out_specs=spec, check_vma=False)
```
